32 devices in a mesh: img: 2 (over x), tok: 4 (over z), seq: 4 (over y, core).
Axes of the slice: x: 2, y: 2, z: 4, core: 2. Of those that a mesh axis runs over, the one named last changes fastest.
Arguments:
- images: bfloat16 [2, 64, 64, 768], P('img', ('tok', 'seq')), may hold values from -6 to 6
- teacher: bfloat16 [2, 64, 64, 768], P('img', ('tok', 'seq')), may hold values from -6 to 6
- valid_mask: int32 [2, 64, 64], P('img', ('tok', 'seq')), may hold values from 0 to 1, as said below
- out_grad: bfloat16 [2, 64, 64, 768], P('img', ('tok', 'seq')), may hold values from -6 to 6
- attn_gain: float32 [768], replicated, may hold values from 0.5 to 1.5
- attn_shift: float32 [768], replicated, may hold values from -1 to 1
- qkv_weight: bfloat16 [768, 2304], P('img'), may hold values from -0.21875 to 0.21875
- query_bias: float32 [768], replicated, may hold values from -1 to 1
- value_bias: float32 [768], replicated, may hold values from -1 to 1
- rel_rows: float32 [27, 64], replicated, may hold values from -0.6 to 0.6
- rel_cols: float32 [27, 64], replicated, may hold values from -0.6 to 0.6
- proj_weight: bfloat16 [768, 768], P('img'), may hold values from -0.875 to 0.875
- proj_bias: float32 [768], replicated, may hold values from -1 to 1
- mlp_gain: float32 [768], replicated, may hold values from 0.5 to 1.5
- mlp_shift: float32 [768], replicated, may hold values from -1 to 1
- up_weight: bfloat16 [768, 3072], P('img'), may hold values from -0.21875 to 0.21875
- up_bias: float32 [3072], replicated, may hold values from -1 to 1
- down_weight: bfloat16 [3072, 768], P('img'), may hold values from -0.109375 to 0.109375
- down_bias: float32 [768], replicated, may hold values from -1 to 1
Outputs:
- block_out: bfloat16 [2, 64, 64, 768], P('img', ('tok', 'seq'))
- distill_loss: float32 [], replicated
- images_grad: float32 [2, 64, 64, 768], P('img', ('tok', 'seq'))
- attn_gain_grad: float32 [768], replicated
- attn_shift_grad: float32 [768], replicated
- qkv_weight_grad: float32 [768, 2304], P('img')
- query_bias_grad: float32 [768], replicated
- value_bias_grad: float32 [768], replicated
- rel_rows_grad: float32 [27, 64], replicated
- rel_cols_grad: float32 [27, 64], replicated
- proj_weight_grad: float32 [768, 768], P('img')
- proj_bias_grad: float32 [768], replicated
- mlp_gain_grad: float32 [768], replicated
- mlp_shift_grad: float32 [768], replicated
- up_weight_grad: float32 [768, 3072], P('img')
- up_bias_grad: float32 [3072], replicated
- down_weight_grad: float32 [3072, 768], P('img')
- down_bias_grad: float32 [768], replicated
The draws below stay inside these ranges and needn't reach their ends.
Inputs may be any that keep to these rules, and one draw needn't show every extreme that they name: `valid_mask`: the first token of every image is valid.
All inputs are finite; a program needn't handle non-finite values.
Results may differ from the reference program's by a relative error of at most 0.012.
Values may be sent and summed in bfloat16 or wider, within the bound.
No kernel may reach another device: no remote copies, remote signals or barrier semaphores. Data moves between devices by JAX's collectives and lax.ppermute only.
A program may use at most 320 MiB of HBM per device.

```python
import jax
import jax.numpy as jnp
from jax import lax

C = 768
HEADS = 12
HD = 64
MLP = 3072
WIN = 14
H = 64
W = 64
IMAGES = 2
TOKENS = 8192
GRID_H = 70
GRID_W = 70


def draw_valid_mask(key, part):
    grid_shape = (IMAGES, H, W)
    picture = lax.broadcasted_iota(jnp.int32, grid_shape, 0)
    percent = 25 + 50 * picture // max(IMAGES - 1, 1)
    rolled = jax.random.randint(key, grid_shape, 0, 100)
    chosen = (rolled < percent).astype(jnp.int32)
    corner = lax.broadcasted_iota(jnp.int32, grid_shape, 1) + lax.broadcasted_iota(jnp.int32, grid_shape, 2) == 0
    return jnp.where(corner, 1, chosen)


def steps_of(key, shape, cuts, least, largest):
    def one(axis_at, shards_of):
        draws = jax.random.uniform(jax.random.fold_in(jax.random.fold_in(key, 6), axis_at), (shards_of,), jnp.float32, least / len(cuts), largest / len(cuts))
        return jnp.repeat(jnp.exp(draws), shape[axis_at] // shards_of).reshape((-1,) + (1,) * (len(shape) - axis_at - 1))

    loudness = one(*cuts[0])
    for cut in cuts[1:]:
        loudness = loudness * one(*cut)
    return loudness


def bell_draw(key, dims, deviation, reach, cuts=(), held_as=jnp.bfloat16):
    entries = jax.random.normal(key, dims, jnp.float32) * deviation
    if len(cuts) > 0:
        entries = steps_of(key, dims, cuts, -0.22, 0.18) * entries
    return jnp.clip(entries, min=-reach, max=reach).astype(held_as)


def setup_inputs(seed: int = 0) -> dict:
    seeds = jax.random.split(jax.random.key(seed), 20)
    images = bell_draw(seeds[0], (IMAGES, H, W, C), 1.0, 6.0, ((0, 2), (1, 16)))
    teacher = bell_draw(seeds[1], (IMAGES, H, W, C), 1.0, 6.0, ((0, 2), (1, 16)))
    valid_mask = draw_valid_mask(jax.random.fold_in(seeds[19], 71), 0)
    out_grad = bell_draw(seeds[3], (IMAGES, H, W, C), 1.0, 6.0, ((0, 2), (1, 16)))
    attn_gain = jnp.clip(1.0 + 0.1 * jax.random.normal(seeds[4], (C,), jnp.float32), 0.5, 1.5)
    attn_shift = bell_draw(seeds[5], (C,), 0.2, 1.0, (), jnp.float32)
    qkv_weight = bell_draw(seeds[6], (C, 3 * C), C ** -0.5, 0.21875, ((0, 2),))
    query_bias = bell_draw(seeds[7], (C,), 0.2, 1.0, (), jnp.float32)
    value_bias = bell_draw(seeds[8], (C,), 0.2, 1.0, (), jnp.float32)
    rel_rows = bell_draw(seeds[9], (2 * WIN - 1, HD), 0.1, 0.6, (), jnp.float32)
    rel_cols = bell_draw(seeds[10], (2 * WIN - 1, HD), 0.1, 0.6, (), jnp.float32)
    proj_weight = bell_draw(seeds[11], (C, C), (C // 16) ** -0.5, 0.875, ((0, 2),))
    proj_bias = bell_draw(seeds[12], (C,), 0.2, 1.0, (), jnp.float32)
    mlp_gain = jnp.clip(1.0 + 0.1 * jax.random.normal(seeds[13], (C,), jnp.float32), 0.5, 1.5)
    mlp_shift = bell_draw(seeds[14], (C,), 0.2, 1.0, (), jnp.float32)
    up_weight = bell_draw(seeds[15], (C, MLP), C ** -0.5, 0.21875, ((0, 2),))
    up_bias = bell_draw(seeds[16], (MLP,), 0.2, 1.0, (), jnp.float32)
    down_weight = bell_draw(seeds[17], (MLP, C), MLP ** -0.5, 0.109375, ((0, 2),))
    down_bias = bell_draw(seeds[18], (C,), 0.2, 1.0, (), jnp.float32)
    return dict(images=images, teacher=teacher, valid_mask=valid_mask, out_grad=out_grad, attn_gain=attn_gain, attn_shift=attn_shift, qkv_weight=qkv_weight, query_bias=query_bias, value_bias=value_bias, rel_rows=rel_rows, rel_cols=rel_cols, proj_weight=proj_weight, proj_bias=proj_bias, mlp_gain=mlp_gain, mlp_shift=mlp_shift, up_weight=up_weight, up_bias=up_bias, down_weight=down_weight, down_bias=down_bias)


EPS = 1e-06
HIGHEST = lax.Precision.HIGHEST

@jax.custom_vjp
def low(v):
    return lax.optimization_barrier(v.astype(jnp.bfloat16)).astype(jnp.float32)

@jax.custom_vjp
def low_back(v):
    return v

def low_keep(v):
    return (low(v), None)

def low_pass(kept, grad):
    return (grad,)

def back_keep(v):
    return (v, None)

def back_low(kept, grad):
    return (low(grad),)
low.defvjp(low_keep, low_pass)
low_back.defvjp(back_keep, back_low)

def norm_rows(values, gain, shift):
    centre = lax.optimization_barrier(jnp.mean(values, axis=-1, keepdims=True))
    centred = values - centre
    spread = lax.optimization_barrier(jnp.mean(centred * centred, axis=-1, keepdims=True))
    return centred * lax.rsqrt(spread + EPS) * gain + shift

def gelu_exact(values):
    return jax.nn.gelu(values, approximate=False)

def rel_lookup(rel_table):
    places = jnp.arange(WIN)
    return rel_table[places[:, None] - places[None, :] + WIN - 1]

def block_forward(params, inputs, target, valid_rows, count_total):
    attn_gain, attn_shift, qkv_weight, query_bias, value_bias, rel_rows, rel_cols, proj_weight, proj_bias, mlp_gain, mlp_shift, up_weight, up_bias, down_weight, down_bias = params
    normed = norm_rows(inputs, attn_gain, attn_shift)
    padded = low(jnp.pad(normed, ((0, GRID_H - H), (0, GRID_W - W), (0, 0))))
    qkv_bias = jnp.concatenate([query_bias, jnp.zeros_like(query_bias), value_bias])
    mixed_qkv = jnp.einsum('rwc,cf->rwf', padded, qkv_weight, precision=HIGHEST) + qkv_bias
    mixed_qkv = low(low_back(mixed_qkv)).reshape(GRID_H // WIN, WIN, GRID_W // WIN, WIN, 3, HEADS, HD)
    queries = mixed_qkv[:, :, :, :, 0]
    keys_win = mixed_qkv[:, :, :, :, 1]
    values = mixed_qkv[:, :, :, :, 2]
    row_table = rel_lookup(rel_rows)
    col_table = rel_lookup(rel_cols)
    direct = jnp.einsum('aibjhc,akblhc->abhijkl', queries, keys_win, precision=HIGHEST) * HD ** (-0.5)
    along_rows = jnp.einsum('aibjhc,ikc->abhijk', queries, row_table, precision=HIGHEST)
    along_cols = jnp.einsum('aibjhc,jlc->abhijl', queries, col_table, precision=HIGHEST)
    scores = low_back(direct + along_rows[..., None] + along_cols[..., None, :])
    lead_shape = scores.shape[:5]
    weights_soft = jax.nn.softmax(scores.reshape(lead_shape + (WIN * WIN,)), axis=-1).reshape(scores.shape)
    attended = jnp.einsum('abhijkl,akblhc->aibjhc', low(weights_soft), values, precision=HIGHEST)
    attended = low(low_back(attended.reshape(GRID_H, GRID_W, HEADS * HD)))[:H, :W]
    projected = low_back(jnp.einsum('rwf,fc->rwc', attended, proj_weight, precision=HIGHEST) + proj_bias)
    residual = inputs + projected
    normed_two = low(norm_rows(residual, mlp_gain, mlp_shift))
    hidden_pre = low_back(jnp.einsum('rwc,cm->rwm', normed_two, up_weight, precision=HIGHEST) + up_bias)
    hidden = low(gelu_exact(hidden_pre))
    result = residual + low_back(jnp.einsum('rwm,mc->rwc', hidden, down_weight, precision=HIGHEST) + down_bias)
    differ = result - target
    part_loss = jnp.sum(valid_rows[..., None] * differ * differ) / (count_total * C)
    return (result, part_loss)

def reference(images, teacher, valid_mask, out_grad, attn_gain, attn_shift, qkv_weight, query_bias, value_bias, rel_rows, rel_cols, proj_weight, proj_bias, mlp_gain, mlp_shift, up_weight, up_bias, down_weight, down_bias):
    params = tuple((argument.astype(jnp.float32) for argument in (attn_gain, attn_shift, qkv_weight, query_bias, value_bias, rel_rows, rel_cols, proj_weight, proj_bias, mlp_gain, mlp_shift, up_weight, up_bias, down_weight, down_bias)))
    count_total = jnp.sum(valid_mask.astype(jnp.float32))
    loss_weight = jnp.float32(TOKENS * C / 8)

    def one_image(running, sliced):
        grad_totals, loss_total = running
        one_input, target, valid_rows, cotangent = sliced

        def forward(params_in, inputs):
            return block_forward(params_in, inputs, target, valid_rows, count_total)
        (result, part_loss), pullback = jax.vjp(forward, params, one_input.astype(jnp.float32))
        param_grads, input_grad = pullback((cotangent.astype(jnp.float32), loss_weight))
        grad_totals = jax.tree.map(jnp.add, grad_totals, param_grads)
        return ((grad_totals, loss_total + part_loss), (result.astype(jnp.bfloat16), input_grad))
    empty_grads = jax.tree.map(jnp.zeros_like, params)
    (grads, loss_total), (results, input_grads) = lax.scan(one_image, (empty_grads, jnp.float32(0.0)), (images, teacher.astype(jnp.float32), valid_mask.astype(jnp.float32), out_grad))
    return (results, loss_total, input_grads, grads[0], grads[1], grads[2], grads[3], grads[4], grads[5], grads[6], grads[7], grads[8], grads[9], grads[10], grads[11], grads[12], grads[13], grads[14])
```

```python
import functools

import jax
import jax.numpy as jnp
import numpy as np
from jax import lax
from jax.experimental import pallas as pl
from jax.experimental.pallas import tpu as pltpu
from jax.sharding import Mesh
from jax.sharding import PartitionSpec as P

HD = 64
WIN = 14
SLOT = 16
EDGE = 8
EPS = 1e-06
KEYS = 256
LANES = 128
FAR = 128.0
BF = jnp.bfloat16
F32 = jnp.float32
SEQ = ("yy", "core")
EVERY = ("img", "tok", "yy", "core")


def swapped(block, axis):
    size = lax.axis_size(axis)
    return lax.ppermute(block, axis, [(i, size - 1 - i) for i in range(size)])


def moved(block, axis, pairs):
    return lax.ppermute(block, axis, pairs)


def pick(pair_low, pair_high, flag):
    return jnp.where(flag == 0, pair_low, pair_high)


def tie(*values):
    return lax.optimization_barrier(values)


def layout_marks(band, place):
    first, last = band == 0, band == lax.axis_size("tok") - 1
    turned = (first & (place == 0)) | (last & (place > 0))
    corner = first & (place == 2)
    edge = turned | jnp.where(first, place == 1, place == 0)
    start = 8 - 2 * band
    real = jnp.where(edge, WIN * EDGE, jnp.where(corner, EDGE * EDGE, 0))
    return (
        start, jnp.where(corner, 0, start), turned.astype(jnp.int32), real, first.astype(jnp.int32),
        band, lax.axis_index("yy"), lax.axis_index("core"),
    )


def whole_spec(shape):
    return pl.BlockSpec(shape, lambda *_: (0,) * len(shape))


def column_picks(ways, cols):
    out = np.zeros((ways, SLOT + EDGE, cols), np.float32)
    for s in range(ways):
        for j in range(SLOT):
            out[s, j, WIN * s + j] = 1.0
        for j in range(EDGE):
            out[s, SLOT + j, WIN * ways + j] = 1.0
    return out


def turn_picks():
    out = np.zeros((WIN * EDGE, EDGE * (SLOT + EDGE)), np.float32)
    for i in range(WIN):
        for j in range(EDGE):
            out[i * EDGE + j, j * (SLOT + EDGE) + i] = 1.0
    return out


def pack_kernel(picks, block, out):
    ways, full = out.shape[0], SLOT + EDGE
    for r in range(block.shape[1]):
        both = jnp.dot(picks[...], block[0, r], preferred_element_type=F32)
        for s in range(ways):
            out[s, 0, r] = both[s * full : (s + 1) * full].astype(BF)


def packed(block):
    count, rows, cols, width = block.shape
    ways = lax.axis_size("yy") * lax.axis_size("core")
    full = SLOT + EDGE
    picks = jnp.asarray(column_picks(ways, cols).reshape(ways * full, cols), BF)
    return pl.pallas_call(
        pack_kernel,
        grid=(count,),
        in_specs=[
            whole_spec(picks.shape),
            pl.BlockSpec((1, rows, cols, width), lambda n: (n, 0, 0, 0)),
        ],
        out_specs=pl.BlockSpec((ways, 1, rows, full, width), lambda n: (0, n, 0, 0, 0)),
        out_shape=jax.ShapeDtypeStruct((ways, count, rows, full, width), BF),
        cost_estimate=pl.CostEstimate(flops=0, bytes_accessed=0, transcendentals=0),
        name="pack",
    )(picks, block)


def window_kernel(at, got, ring, turn, out):
    count, rows = got.shape[1], got.shape[2]
    start_a, start_e, turned, first = at[0], at[1], at[2], at[4]
    for n in range(count):

        def row_of(row, cols):
            own = jnp.maximum(row - 8, 0)
            before = ring[n, jnp.minimum(row, 7), cols].astype(F32)
            return jnp.where(row < 8, before, got[own // rows, n, own % rows, cols].astype(F32))

        for i in range(WIN):
            full = row_of(start_a + i, slice(0, SLOT))
            out[n, i * SLOT : (i + 1) * SLOT] = full.astype(BF)
        edge = jnp.concatenate(
            [row_of(start_e + i, slice(SLOT, SLOT + EDGE)) for i in range(WIN)], axis=0
        )
        tail = jnp.concatenate(
            [
                jnp.where(first == 1, ring[n, k], got[2 + k // rows, n, k % rows]).astype(F32)
                for k in range(EDGE)
            ],
            axis=0,
        ).astype(BF)
        bottom = jnp.dot(turn[...], tail, preferred_element_type=F32)
        out[n, WIN * SLOT :] = jnp.where(turned == 1, bottom, edge).astype(BF)


def window_norm_kernel(at, got, ring, turn, gain, shift, out, low):
    window_kernel(at, got, ring, turn, out)
    for start, size in ((0, WIN * SLOT), (WIN * SLOT, WIN * EDGE)):
        unit, _ = norm_parts(out[0, start : start + size].astype(F32))
        row = lax.broadcasted_iota(jnp.int32, (size, 1), 0)
        real = (row & (SLOT - 1)) < WIN if start == 0 else row < at[3]
        low[start : start + size] = jnp.where(real, unit * gain[...] + shift[...], 0.0).astype(BF)


def ring_rows(got, step):
    bands = lax.axis_size("tok")
    send = jnp.moveaxis(got[2:], 1, 0)
    send = send.reshape(send.shape[0], 8, SLOT + EDGE, send.shape[-1])
    return moved(send, "tok", [(i, (i + step) % bands) for i in range(bands)])


def windowed(got, ring, marks, norm=None):
    count, width = got.shape[1], got.shape[-1]
    tokens = WIN * (SLOT + EDGE)
    specs = [
        whole_spec(got.shape),
        whole_spec(ring.shape),
        whole_spec((WIN * EDGE, EDGE * (SLOT + EDGE))),
    ]
    out_specs = [whole_spec((count, tokens, width))]
    out_shape = [jax.ShapeDtypeStruct((count, tokens, width), BF)]
    if norm is not None:
        specs += [whole_spec((width,))] * 2
        out_specs.append(whole_spec((tokens, width)))
        out_shape.append(jax.ShapeDtypeStruct((tokens, width), BF))
    return pl.pallas_call(
        window_kernel if norm is None else window_norm_kernel,
        grid_spec=pltpu.PrefetchScalarGridSpec(
            num_scalar_prefetch=1, grid=(1,), in_specs=specs, out_specs=out_specs
        ),
        out_shape=out_shape,
        cost_estimate=pl.CostEstimate(flops=0, bytes_accessed=0, transcendentals=0),
        name="window",
    )(marks, got, ring, jnp.asarray(turn_picks(), BF), *(norm or ()))


def unwindow_kernel(at, *refs):
    flats, (turn, up, mid) = refs[:-3], refs[-3:]
    start_a, start_e, turned, first = at[0], at[1], at[2], at[4]
    full = SLOT + EDGE
    for n, flat in enumerate(flats):
        bottom = lax.dot_general(
            turn[...],
            flat[WIN * SLOT :].astype(BF),
            (((0,), (0,)), ((), ())),
            preferred_element_type=F32,
        )
        for row in range(24):
            i = row - start_e
            held = (i >= 0) & (i < WIN) & (turned == 0)
            at_row = pl.multiple_of(WIN * SLOT + EDGE * jnp.clip(i, 0, WIN - 1), EDGE)
            right = jnp.where(held, flat[pl.ds(at_row, EDGE)], 0.0)
            i = row - start_a
            at_row = pl.multiple_of(SLOT * jnp.clip(i, 0, WIN - 1), SLOT)
            left = jnp.where((i >= 0) & (i < WIN), flat[pl.ds(at_row, SLOT)], 0.0)
            if row < 8 or row >= 16:
                base = row % 8 * full
                here = (turned == 1) & (first == (1 if row < 8 else 0))
                left = jnp.where(here, bottom[base : base + SLOT], left)
            both = jnp.concatenate([left, right], axis=0).astype(BF)
            if row < 8:
                up[n, row] = both
            else:
                mid[n, row - 8] = both


def unwindowed(flats, marks):
    width = flats[0].shape[1]
    count, full = len(flats), SLOT + EDGE
    shapes = [(count, 8, full, width), (count, 16, full, width)]
    return pl.pallas_call(
        unwindow_kernel,
        grid_spec=pltpu.PrefetchScalarGridSpec(
            num_scalar_prefetch=1,
            grid=(1,),
            in_specs=[whole_spec(f.shape) for f in flats] + [whole_spec((WIN * EDGE, EDGE * full))],
            out_specs=[whole_spec(shape) for shape in shapes],
        ),
        out_shape=[jax.ShapeDtypeStruct(shape, BF) for shape in shapes],
        cost_estimate=pl.CostEstimate(flops=0, bytes_accessed=0, transcendentals=0),
        name="unwindow",
    )(marks, *flats, jnp.asarray(turn_picks(), BF))


def unpack_kernel(picks, got, *outs):
    for n, out in enumerate(outs):
        for r in range(got.shape[2]):
            total = None
            for s in range(got.shape[0]):
                part = lax.dot_general(
                    picks[s], got[s, n, r], (((0,), (0,)), ((), ())), preferred_element_type=F32
                )
                total = part if total is None else total + part
            out[r] = total.astype(out.dtype)


def unpacked(got, cols, dtypes):
    ways, count, rows, full, width = got.shape
    picks = column_picks(ways, cols)
    picks[:, WIN:SLOT] = 0.0
    return pl.pallas_call(
        unpack_kernel,
        in_specs=[whole_spec(picks.shape), whole_spec(got.shape)],
        out_specs=[whole_spec((rows, cols, width))] * count,
        grid=(1,),
        out_shape=[jax.ShapeDtypeStruct((rows, cols, width), dtype) for dtype in dtypes],
        cost_estimate=pl.CostEstimate(flops=0, bytes_accessed=0, transcendentals=0),
        name="unpack",
    )(jnp.asarray(picks, BF), got)


def exchanged(send):
    return lax.all_to_all(send, SEQ, split_axis=0, concat_axis=0, tiled=True)


def sent_back(up):
    bands = lax.axis_size("tok")
    return moved(up, "tok", [((i + 1) % bands, i) for i in range(bands)])


def band_rows_of(mid, ring):
    own = mid + jnp.pad(ring, ((0, 0), (8, 0), (0, 0), (0, 0)))
    ways = lax.axis_size("yy") * lax.axis_size("core")
    own = own.reshape(own.shape[0], ways, 16 // ways, SLOT + EDGE, own.shape[-1])
    return jnp.swapaxes(own, 0, 1)


def two_images():
    return lax.axis_size("img") == 2


def quarter(shard):
    if not two_images():
        return shard
    rows = shard.shape[0] // 4
    at = lax.axis_index("yy") * 2 + lax.axis_index("core")
    return lax.dynamic_slice_in_dim(shard, at * rows, rows, 0)


def half_of(shard, chunks=1):
    if not two_images():
        return [shard]
    rows = shard.shape[0] // (2 * chunks)
    first = lax.axis_index("core") * rows * chunks
    return [lax.dynamic_slice_in_dim(shard, first + i * rows, rows, 0) for i in range(chunks)]


def over_images(block):
    if two_images():
        return swapped(block, "img")
    return lax.all_gather(block, "img", axis=0, tiled=True)


def half_over_cores(block):
    return (block, swapped(block, "core")) if two_images() else block


def assembled_halves(shard, *parts):
    if not two_images():
        return parts[0]
    core, image = lax.axis_index("core"), lax.axis_index("img")
    other = jnp.concatenate(
        [pick(here, there, core) for here, there in parts]
        + [pick(there, here, core) for here, there in parts],
        axis=0,
    )
    return jnp.concatenate([pick(shard, other, image), pick(other, shard, image)], axis=0)


def gather_over_rows(block):
    return swapped(block, "yy") if two_images() else block


def gather_over_cores(first, second):
    if not two_images():
        return first
    high = lax.axis_index("yy")
    here = jnp.stack([pick(first, second, high), pick(second, first, high)])
    return here, swapped(here, "core")


def assembled(shard, parts):
    if not two_images():
        return parts
    here, there = parts
    core, image = lax.axis_index("core"), lax.axis_index("img")
    even, odd = pick(here, there, core), pick(there, here, core)
    other = jnp.stack([even, odd], axis=1).reshape(shard.shape)
    return jnp.concatenate([pick(shard, other, image), pick(other, shard, image)], axis=0)


def part_of(terms, dim, axis, other):
    index = lax.axis_index(axis)
    index = 1 - index if other else index
    return [lax.dynamic_index_in_dim(t, index, dim, keepdims=False) for t in terms]


def added(terms):
    total = terms[0].astype(F32)
    for t in terms[1:]:
        total = total + t.astype(F32)
    return total.astype(BF)


def to_send(terms, dim, axis):
    if lax.axis_size(axis) != 2:
        return jnp.moveaxis(added(terms), dim, 0)
    return added(part_of(terms, dim, axis, True))


def sent(block, axis):
    if lax.axis_size(axis) != 2:
        return lax.all_to_all(block, axis, split_axis=0, concat_axis=0, tiled=True)
    return swapped(block, axis)


def kept(terms, dim, axis, got):
    if lax.axis_size(axis) != 2:
        return [got[i] for i in range(got.shape[0])]
    return part_of(terms, dim, axis, False) + [got]


def split_grad(left, right):
    images, bands = lax.axis_size("img"), lax.axis_size("tok")
    core = lax.axis_index("core")
    rows, cols = left.shape[1], right.shape[1] // 2
    shape = (images, 2, bands, rows // images // 2 // bands, cols)

    def one(index):
        half = lax.dynamic_slice_in_dim(right, index * cols, cols, 1)
        return mm_tn(left, half).astype(BF).reshape(shape)

    return one(1 - core), one(core)


def crossed(block, distance):
    size = lax.axis_size("tok")
    return lax.ppermute(block, "tok", [(i, i ^ distance) for i in range(size)])


def band_parts(piece):
    band = lax.axis_index("tok")
    return [
        lax.dynamic_index_in_dim(piece, band ^ d, 0, keepdims=False)
        for d in range(lax.axis_size("tok"))
    ]


def over_bands(parts):
    return [crossed(part, d) for d, part in enumerate(parts) if d > 0]


def to_bands(total):
    return [crossed(total, d) for d in range(1, lax.axis_size("tok"))]


def final_kernel(splits, unit, at, near_own, near_other, far_own, far_other, *outs):
    band, core = at[5], at[7]

    def write(own, other):
        for t in range(own.shape[0]):
            to = t ^ band
            for (rows, first, blocks), out in zip(splits, outs):
                size = blocks * unit
                a = own[t, :, first * unit : first * unit + size].astype(F32)
                b = other[t, :, first * unit : first * unit + size].astype(F32)
                out[0, to, :, :size] = jnp.where(core == 0, a, b)
                out[0, to, :, size:] = jnp.where(core == 0, b, a)

    @pl.when(pl.program_id(0) == 0)
    def near():
        write(near_own, near_other)

    @pl.when(pl.program_id(0) == 1)
    def far():
        write(far_own, far_other)


def final(marks, own, other_core, beside, beside_other_core, splits):
    bands, rows, cols = own.shape
    unit = cols // sum(blocks for _, _, blocks in splits)
    outs = pl.pallas_call(
        functools.partial(final_kernel, splits, unit),
        grid_spec=pltpu.PrefetchScalarGridSpec(
            num_scalar_prefetch=1,
            grid=(2,),
            in_specs=[whole_spec(own.shape)] * 4,
            out_specs=[
                pl.BlockSpec((1, bands, n, 2 * blocks * unit), lambda y, at: (y ^ at[6], 0, 0, 0))
                for n, _, blocks in splits
            ],
        ),
        out_shape=[
            jax.ShapeDtypeStruct((2, bands, n, 2 * blocks * unit), F32) for n, _, blocks in splits
        ],
        cost_estimate=pl.CostEstimate(flops=0, bytes_accessed=0, transcendentals=0),
        name="final",
    )(marks, own, other_core, beside, beside_other_core)
    return [o.reshape(-1, o.shape[-1]) for o in outs]


def device_count():
    devices = 1
    for axis in EVERY:
        devices = devices * lax.axis_size(axis)
    return devices


def spread_sum(values):
    devices = device_count()
    part = -(-values.shape[0] // devices)
    cut = jnp.pad(values, (0, part * devices - values.shape[0])).reshape(devices, part)
    return jnp.sum(lax.all_to_all(cut, EVERY, split_axis=0, concat_axis=0, tiled=True), axis=0)


def all_counts(value):
    wide = jnp.broadcast_to(value, (device_count(), 8, LANES))
    got = lax.all_to_all(wide, EVERY, split_axis=0, concat_axis=0, tiled=True)
    return got


def to_all(part):
    wide = jnp.broadcast_to(part[None], (device_count(),) + part.shape)
    return lax.all_to_all(wide, EVERY, split_axis=0, concat_axis=0, tiled=True)


def rolled(block, amount):
    return pltpu.roll(block, amount, 1, stride=1, stride_axis=0)


def rel_places():
    size = 2 * WIN - 1
    out = np.zeros((4, LANES, size), np.float32)
    for m in range(size):
        out[0, size - 1 - m, m] = 1.0
        out[1, 32 + size - 1 - m, m] = 1.0
        out[2, m, m] = 1.0
        out[3, 64 + m, m] = 1.0
    return out


def head_places():
    out = np.zeros((2, HD, LANES), np.float32)
    for c in range(HD):
        out[0, c, c] = 1.0
        out[1, c, HD + c] = 1.0
    return out


def build_rel(tables, places, heads, out):
    for half in (0, 1):
        total = None
        for table, place in zip(tables, places):
            high = table.astype(BF)
            value = (table - high.astype(F32)).astype(BF) if half else high
            part = jnp.dot(place, value, preferred_element_type=F32)
            total = part if total is None else total + part
        for head in (0, 1):
            lanes = jnp.dot(total.astype(BF), heads[head], preferred_element_type=F32)
            out[head, :, half * LANES : (half + 1) * LANES] = lanes.astype(BF)


def build_both(at, rows, cols, places, heads, rel_a, rel_b):
    @pl.when(pl.program_id(0) == 0)
    def build():
        turned = at[2] == 1
        build_rel((rows[...], cols[...]), places, heads, rel_a)
        first = jnp.where(turned, cols[...], rows[...])
        second = jnp.where(turned, rows[...], cols[...])
        build_rel((first, second), places, heads, rel_b)


def wide_queries(q, rel, group):
    m = q.shape[0]
    terms = lax.dot_general(
        jnp.concatenate([q, q], axis=1), rel, (((1,), (1,)), ((), ())), preferred_element_type=F32
    )
    lane = lax.broadcasted_iota(jnp.int32, (group, LANES), 1)
    blocks = []
    for i in range(WIN):
        t = terms[i * group : (i + 1) * group]
        by_row = pltpu.roll(t, (LANES - (WIN - 1) + i) % LANES, 1)
        by_col = rolled(t, 19)
        blocks.append(jnp.where(lane < 64, by_row, by_col))
    both = jnp.concatenate(blocks, axis=0)
    high = both.astype(BF).astype(F32)
    low = pltpu.roll(both - high, 32, 1)
    lane = lax.broadcasted_iota(jnp.int32, (m, LANES), 1)
    mixed = jnp.where((lane & 63) < 32, high, low)
    mixed = jnp.where(lane == LANES - 1, 1.0, mixed)
    return jnp.concatenate([q * BF(HD**-0.5), mixed.astype(BF)], axis=1)


def full_keys(k, v, v_pad):
    n = k.shape[0]
    zeros = jnp.zeros((KEYS - n, LANES), BF)
    if v_pad is None:
        return jnp.concatenate([k, zeros], axis=0), jnp.concatenate([v, zeros], axis=0)
    fill = jnp.broadcast_to(v_pad, (KEYS - n, LANES)).astype(BF)
    return jnp.concatenate([k, zeros], axis=0), jnp.concatenate([v, fill], axis=0)


def only(block, head):
    lane = lax.broadcasted_iota(jnp.int32, block.shape, 1)
    return jnp.where((lane < HD) == (head == 0), block, jnp.zeros_like(block))


def attend(q, k, v, v_pad, rel_ref, hot, group, probs_ref):
    keys, vals = full_keys(k, v, v_pad)
    out = None
    for head in (0, 1):
        wide = wide_queries(q, rel_ref[head], group)
        scores = lax.dot_general(
            wide,
            jnp.concatenate([only(keys, head), hot], axis=1),
            (((1,), (1,)), ((), ())),
            preferred_element_type=F32,
        )
        top = jnp.max(scores, axis=1, keepdims=True)
        e = jnp.exp(scores - top)
        total = jnp.sum(e, axis=1, keepdims=True)
        p = (e * (1.0 / total)).astype(BF)
        probs_ref[head] = p
        part = jnp.dot(p, only(vals, head), preferred_element_type=F32)
        out = part if out is None else out + part
    return out.astype(BF)


def attend_kernel(
    at, q, k, v, v_pad, rows, cols, places, heads, hot_a, hot_b, out, probs_a, probs_b, rel_a, rel_b
):
    build_both(at, rows, cols, (places[0], places[1]), heads, rel_a, rel_b)
    n = WIN * SLOT
    pad = v_pad[...].astype(BF)
    out[:n] = attend(q[:n], k[:n], v[:n], None, rel_a, hot_a[...], SLOT, probs_a)
    out[n:] = attend(q[n:], k[n:], v[n:], pad, rel_b, hot_b[...], EDGE, probs_b)


def attend_back(q, k, v, v_pad, out_grad, rel_ref, hot, group, probs_ref, rel_grad):
    keys, vals = full_keys(k, v, v_pad)
    scale = HD**-0.5
    lane = lax.broadcasted_iota(jnp.int32, (group, LANES), 1)
    pair = lax.broadcasted_iota(jnp.int32, (KEYS, LANES), 1)
    dq, dks, dvs = None, [], []
    for head in (0, 1):
        probs = probs_ref[head]
        wide = probs.astype(F32)
        dp = lax.dot_general(
            out_grad, only(vals, head), (((1,), (1,)), ((), ())), preferred_element_type=F32
        )
        inner = jnp.sum(wide * dp, axis=1, keepdims=True)
        ds = (wide * (dp - inner)).astype(BF)
        both = jnp.dot(
            ds, jnp.concatenate([only(keys, head), hot], axis=1), preferred_element_type=F32
        )
        part = both[:, :LANES] * scale
        blocks = []
        for i in range(WIN):
            t = both[i * group : (i + 1) * group, LANES:]
            by_row = pltpu.roll(jnp.where(lane < WIN, t, 0.0), i, 1) if i else jnp.where(
                lane < WIN, t, 0.0
            )
            by_col = rolled(jnp.where((lane >= 64) & (lane < 64 + WIN), t, 0.0), 0)
            blocks.append(by_row + by_col)
        terms = jnp.concatenate(blocks, axis=0)
        high = terms.astype(BF)
        low = (terms - high.astype(F32)).astype(BF)
        split = jnp.concatenate([high, low], axis=1)
        rel = rel_ref[head]
        part = part + jnp.dot(
            split,
            jnp.concatenate([rel[:, :LANES], rel[:, :LANES]], axis=0),
            preferred_element_type=F32,
        )
        part = part + jnp.dot(high, rel[:, LANES:], preferred_element_type=F32)
        dq = part if dq is None else dq + part
        rel_grad[head] += lax.dot_general(
            split, q, (((0,), (0,)), ((), ())), preferred_element_type=F32
        )
        dks.append(
            lax.dot_general(ds, q, (((0,), (0,)), ((), ())), preferred_element_type=F32) * scale
        )
        dvs.append(
            lax.dot_general(probs, out_grad, (((0,), (0,)), ((), ())), preferred_element_type=F32)
        )
    dk = jnp.where(pair < HD, dks[0], dks[1]).astype(BF)
    dv = jnp.where(pair < HD, dvs[0], dvs[1]).astype(BF)
    return dq.astype(BF), dk, dv


def attend_back_kernel(
    at, q, k, v, v_pad, rows, cols, places, heads, hot_a, hot_b, grad, probs_a, probs_b,
    dqkv, pad_sum, rows_grad, cols_grad, rel_a, rel_b, acc_a, acc_b,
):
    step = pl.program_id(0)
    steps = dqkv.shape[1] // (3 * LANES)
    build_both(at, rows, cols, (places[2], places[3]), heads, rel_a, rel_b)

    @pl.when(step == 0)
    def clear():
        acc_a[...] = jnp.zeros_like(acc_a)
        acc_b[...] = jnp.zeros_like(acc_b)

    n = WIN * SLOT
    pad = v_pad[...].astype(BF)
    part_a = attend_back(
        q[:n], k[:n], v[:n], None, grad[:n], rel_a, hot_a[...], SLOT, probs_a, acc_a
    )
    part_b = attend_back(
        q[n:], k[n:], v[n:], pad, grad[n:], rel_b, hot_b[...], EDGE, probs_b, acc_b
    )
    for i in range(3):
        to = pl.ds(pl.multiple_of((i * steps + step) * LANES, LANES), LANES)
        dqkv[:n, to] = part_a[i][:n]
        dqkv[n:, to] = part_b[i][: WIN * EDGE]
    pad_sum[...] = jnp.sum(part_b[2][WIN * EDGE :].astype(F32), axis=0, keepdims=True)

    @pl.when(step == steps - 1)
    def tables():
        def table(acc):
            even = acc[0, :LANES] + acc[0, LANES:]
            odd = acc[1, :LANES] + acc[1, LANES:]
            return even + pltpu.roll(odd, HD, 1)

        size = 2 * WIN - 1
        a, b = table(acc_a), table(acc_b)
        turned = at[2] == 1
        low, high = slice(0, size), slice(64, 64 + size)
        rows_grad[...] = a[low, :HD] + jnp.where(turned, b[high, :HD], b[low, :HD])
        cols_grad[...] = a[high, :HD] + jnp.where(turned, b[low, :HD], b[high, :HD])


def hot_tables():
    def table(place):
        out = np.zeros((2, KEYS, LANES), np.float32)
        for key in range(KEYS):
            at = place(key)
            if at is None:
                out[0, key, LANES - 1] = -1e30
            else:
                for base, index in ((0, at[0]), (32, at[0]), (64, at[1]), (96, at[1])):
                    out[0, key, base + index] = 1.0
                out[1, key, WIN - 1 - at[0]] = 1.0
                out[1, key, 64 + WIN - 1 - at[1]] = 1.0
        return out

    def whole(key):
        i, j = divmod(key, SLOT)
        return (i, j) if i < WIN and j < WIN else None

    def partial(key):
        if key < WIN * EDGE:
            return divmod(key, EDGE)
        i, j = divmod(key - WIN * EDGE, EDGE)
        return (i, EDGE + j) if i < WIN and EDGE + j < WIN else None

    return table(whole), table(partial)


def attention(qkv, v_pad, rel_rows, rel_cols, marks):
    tokens_a, tokens_b = WIN * SLOT, WIN * EDGE
    tokens, width = qkv.shape[0], qkv.shape[1] // 3
    pairs = width // LANES
    table = (2 * WIN - 1, HD)
    hots = [jnp.asarray(t, BF) for t in hot_tables()]
    places, heads = jnp.asarray(rel_places(), BF), jnp.asarray(head_places(), BF)

    def cols(n, base):
        return pl.BlockSpec((n, LANES), lambda p, at: (0, base * pairs + p))

    specs = [cols(tokens, i) for i in range(3)] + [
        pl.BlockSpec((LANES,), lambda p, at: (p,)),
        whole_spec(table),
        whole_spec(table),
        whole_spec(places.shape),
        whole_spec(heads.shape),
        whole_spec((KEYS, LANES)),
        whole_spec((KEYS, LANES)),
    ]
    probs_specs = [
        pl.BlockSpec((2, tokens_a, KEYS), lambda p, at: (p, 0, 0)),
        pl.BlockSpec((2, tokens_b, KEYS), lambda p, at: (p, 0, 0)),
    ]
    rel_scratch = [pltpu.VMEM((2, LANES, 2 * LANES), BF)] * 2
    shared = (marks, qkv, qkv, qkv, v_pad, rel_rows, rel_cols, places, heads)
    out, probs_a, probs_b = pl.pallas_call(
        attend_kernel,
        grid_spec=pltpu.PrefetchScalarGridSpec(
            num_scalar_prefetch=1,
            grid=(pairs,),
            in_specs=specs,
            out_specs=[cols(tokens, 0)] + probs_specs,
            scratch_shapes=rel_scratch,
        ),
        out_shape=[
            jax.ShapeDtypeStruct((tokens, width), BF),
            jax.ShapeDtypeStruct((2 * pairs, tokens_a, KEYS), BF),
            jax.ShapeDtypeStruct((2 * pairs, tokens_b, KEYS), BF),
        ],
        cost_estimate=pl.CostEstimate(flops=0, bytes_accessed=0, transcendentals=0),
        name="attend",
    )(*shared, hots[0][0], hots[1][0])

    def back(grad):
        return pl.pallas_call(
            attend_back_kernel,
            grid_spec=pltpu.PrefetchScalarGridSpec(
                num_scalar_prefetch=1,
                grid=(pairs,),
                in_specs=specs + [cols(tokens, 0)] + probs_specs,
                out_specs=[
                    whole_spec((tokens, 3 * width)),
                    cols(1, 0),
                    whole_spec(table),
                    whole_spec(table),
                ],
                scratch_shapes=rel_scratch + [pltpu.VMEM((2, 2 * LANES, LANES), F32)] * 2,
            ),
            out_shape=[
                jax.ShapeDtypeStruct((tokens, 3 * width), BF),
                jax.ShapeDtypeStruct((1, width), F32),
                jax.ShapeDtypeStruct(table, F32),
                jax.ShapeDtypeStruct(table, F32),
            ],
            cost_estimate=pl.CostEstimate(flops=0, bytes_accessed=0, transcendentals=0),
            name="attend_back",
        )(*shared, hots[0][1], hots[1][1], grad, probs_a, probs_b)

    return out, back


def norm_parts(values):
    centre = jnp.mean(values, axis=-1, keepdims=True)
    centred = values - centre
    spread = jnp.mean(centred * centred, axis=-1, keepdims=True)
    scale = lax.rsqrt(spread + EPS)
    return centred * scale, scale


def norm_back(grad, unit, scale, gain):
    g = grad * gain
    mean = jnp.mean(g, axis=-1, keepdims=True)
    along = jnp.mean(g * unit, axis=-1, keepdims=True)
    return scale * (g - mean - unit * along)


def mm(a, b):
    return jnp.dot(a, b, preferred_element_type=F32)


def mm_nt(a, b):
    return lax.dot_general(a, b, (((1,), (1,)), ((), ())), preferred_element_type=F32)


def mm_tn(a, b):
    return lax.dot_general(a, b, (((0,), (0,)), ((), ())), preferred_element_type=F32)


def local(
    images, teacher, valid_mask, out_grad, attn_gain, attn_shift, qkv_weight, query_bias,
    value_bias, rel_rows, rel_cols, proj_weight, proj_bias, mlp_gain, mlp_shift, up_weight,
    up_bias, down_weight, down_bias,
):
    band = lax.axis_index("tok")
    bands = lax.axis_size("tok")
    place = lax.axis_index("yy") * lax.axis_size("core") + lax.axis_index("core")
    width = images.shape[-1]
    image_rows = images.shape[1] * bands * lax.axis_size("yy") * lax.axis_size("core")
    tokens_all = images.shape[0] * lax.axis_size("img") * image_rows * images.shape[2]

    marks = layout_marks(band, place)
    real_edge = marks[3]
    marks = jnp.stack(marks).astype(jnp.int32)
    x_got = exchanged(packed(images))
    qkv_1 = over_images(quarter(qkv_weight))
    proj_1 = [over_images(c) for c in half_of(proj_weight)]
    up_1 = [over_images(c) for c in half_of(up_weight, 2)]
    down_1 = [over_images(c) for c in half_of(down_weight, 2)]
    x_got, qkv_1, marks = tie(x_got, qkv_1, marks)
    qkv_2 = gather_over_rows(qkv_1)
    x_ring = ring_rows(x_got, 1)
    marked = jnp.where(valid_mask[..., None] > 0, teacher, jnp.full_like(teacher, FAR))
    late_pack = packed(tie(jnp.concatenate([marked, out_grad], axis=0), qkv_1)[0])
    qkv_2, x_ring, x_got, late_pack, up_1[0] = tie(qkv_2, x_ring, x_got, late_pack, up_1[0])
    qkv_3 = gather_over_cores(qkv_1, qkv_2)
    x_low, tokens_low = windowed(x_got, x_ring, marks, (attn_gain, attn_shift))
    x_low = x_low[0]
    qkv_3, x_low, tokens_low, proj_1[0] = tie(qkv_3, x_low, tokens_low, proj_1[0])
    proj_2 = half_over_cores(proj_1[0])

    row_a = lax.broadcasted_iota(jnp.int32, (WIN * SLOT, 1), 0)
    row_b = lax.broadcasted_iota(jnp.int32, (WIN * EDGE, 1), 0)
    real = jnp.concatenate(
        [(row_a & (SLOT - 1)) < WIN, row_b < real_edge], axis=0
    )
    inputs = x_low.astype(F32)
    qkv_bias = jnp.concatenate([query_bias, jnp.zeros_like(query_bias), value_bias])
    qkv_full = assembled(qkv_weight, qkv_3)
    qkv = (mm(tokens_low, qkv_full) + qkv_bias).astype(BF)
    qkv, late_pack, proj_2, up_1 = tie(qkv, late_pack, proj_2, up_1)
    up_2 = [half_over_cores(c) for c in up_1]
    late_got = exchanged(late_pack)
    attended, attention_back = attention(qkv, value_bias, rel_rows, rel_cols, marks)
    proj_full = assembled_halves(proj_weight, proj_2)
    attended, up_2, proj_full, down_1[0] = tie(attended, up_2, proj_full, down_1[0])
    resid = inputs + mm(attended, proj_full) + proj_bias
    unit2, scale2 = norm_parts(resid)
    normed2 = (unit2 * mlp_gain + mlp_shift).astype(BF)
    up_full = assembled_halves(up_weight, *up_2)
    normed2, up_full, late_got = tie(normed2, up_full, late_got)
    late_ring = ring_rows(late_got, 1)
    counts = all_counts(jnp.sum(tie(valid_mask, late_got)[0].astype(F32)))
    hidden_pre = mm(normed2, up_full) + up_bias
    cdf = 0.5 * (1.0 + lax.erf(hidden_pre * (0.5**0.5)))
    hidden = (hidden_pre * cdf).astype(BF)
    slope = cdf + hidden_pre * jnp.exp(-0.5 * hidden_pre * hidden_pre) * ((2 * np.pi) ** -0.5)
    hidden, slope, late_ring, down_1, counts = tie(hidden, slope, late_ring, down_1, counts)
    count_total = jnp.sum(counts[:, 0, 0])
    down_2 = [half_over_cores(c) for c in down_1]
    (late,) = windowed(late_got, late_ring, marks)
    late, down_2 = tie(late, down_2)
    down_full = assembled_halves(down_weight, *down_2)
    result = resid + mm(hidden, down_full) + down_bias

    teach = late[0].astype(F32)
    valid = (real & (teach[:, :1] < 0.5 * FAR)).astype(F32)
    differ = valid * (result - teach)
    squares = jnp.sum(differ * differ)
    grads = jnp.where(real, late[1], jnp.zeros_like(late[1])).astype(F32)
    result_grad = grads + differ * (tokens_all / (4.0 * count_total))
    down_in = result_grad.astype(BF)

    d_send, d_keep = split_grad(hidden, down_in)
    d_send, down_in = tie(d_send, down_in)
    d_got = sent(d_send, "core")
    pre_grad = (slope * mm_nt(down_in, down_full)).astype(BF)
    d_got, d_keep, pre_grad = tie(d_got, d_keep, pre_grad)
    d_terms = [d_keep, d_got]
    d_out, pre_grad = tie(to_send(d_terms, 0, "img"), pre_grad)
    d_got = sent(d_out, "img")
    u_send, u_keep = split_grad(normed2, pre_grad)
    u_send, pre_grad = tie(u_send, pre_grad)
    u_got = sent(u_send, "core")
    normed2_grad = mm_nt(pre_grad, up_full)
    u_got, u_keep, normed2_grad = tie(u_got, u_keep, normed2_grad)
    u_terms = [u_keep, u_got]
    u_out, normed2_grad = tie(to_send(u_terms, 1, "yy"), normed2_grad)
    u_got = sent(u_out, "yy")
    resid_grad = result_grad + norm_back(normed2_grad, unit2, scale2, mlp_gain)
    proj_in = resid_grad.astype(BF)
    p_send, p_keep = split_grad(attended, proj_in)
    p_send, proj_in = tie(p_send, proj_in)
    p_got = sent(p_send, "core")
    attended_grad = mm_nt(proj_in, proj_full).astype(BF)
    attended_grad, p_got, p_keep = tie(attended_grad, p_got, p_keep)
    p_terms = [p_keep, p_got]
    p_out, attended_grad = tie(to_send(p_terms, 0, "img"), attended_grad)
    p_got = sent(p_out, "img")

    dqkv, pad_sum, rel_rows_grad, rel_cols_grad = attention_back(attended_grad)
    dqkv, pad_sum, d_got, u_got = tie(dqkv, pad_sum, d_got, u_got)
    d_terms = kept(d_terms, 0, "img", d_got)
    u_terms = kept(u_terms, 1, "yy", u_got)
    d_out, u_out, dqkv = tie(to_send(d_terms, 0, "yy"), to_send(u_terms, 0, "img"), dqkv)
    d_got = sent(d_out, "yy")
    u_got = sent(u_out, "img")
    q_send, q_keep = split_grad(tokens_low, dqkv)
    q_send, dqkv = tie(q_send, dqkv)
    q_got = sent(q_send, "core")
    normed_grad = jnp.where(real, mm_nt(dqkv, qkv_full), 0.0)
    normed_grad, q_got, q_keep, p_got = tie(normed_grad, q_got, q_keep, p_got)
    p_terms = kept(p_terms, 0, "img", p_got)
    half = bands // 2
    qa_terms = [q_keep[:, :, :half], q_got[:, :, :half]]
    qb_terms = [q_keep[:, :, half:], q_got[:, :, half:]]
    qa_out, qb_out, p_out, normed_grad = tie(
        to_send(qa_terms, 0, "img"), to_send(qb_terms, 1, "yy"), to_send(p_terms, 0, "yy"), normed_grad
    )
    qa_got = sent(qa_out, "img")
    qb_got = sent(qb_out, "yy")
    p_got = sent(p_out, "yy")
    unit, scale = norm_parts(inputs)
    images_grad = resid_grad + norm_back(normed_grad, unit, scale, attn_gain)
    down_bias_grad = jnp.sum(down_in.astype(F32), axis=0)
    up_bias_grad = jnp.sum(pre_grad.astype(F32), axis=0)
    mlp_gain_grad = jnp.sum(normed2_grad * unit2, axis=0)
    mlp_shift_grad = jnp.sum(normed2_grad, axis=0)
    proj_bias_grad = jnp.sum(proj_in.astype(F32), axis=0)
    qkv_sums = jnp.sum(dqkv.astype(F32), axis=0)
    query_bias_grad = qkv_sums[:width]
    value_bias_grad = qkv_sums[2 * width :] + pad_sum[0]
    attn_gain_grad = jnp.sum(normed_grad * unit, axis=0)
    attn_shift_grad = jnp.sum(normed_grad, axis=0)
    small = (
        squares.reshape(1), attn_gain_grad, attn_shift_grad, query_bias_grad, value_bias_grad,
        rel_rows_grad, rel_cols_grad, proj_bias_grad, mlp_gain_grad, mlp_shift_grad,
        up_bias_grad, down_bias_grad,
    )
    flat, images_grad = tie(jnp.concatenate([s.reshape(-1) for s in small]), images_grad)
    total = spread_sum(flat)
    backs = unwindowed([jnp.where(real, result, 0.0), images_grad], marks)
    backs, d_got, total = tie(backs, d_got, total)
    back_ring = sent_back(backs[0])
    d_parts = tie(*band_parts(added(kept(d_terms, 0, "yy", d_got))))
    d_got = over_bands(d_parts)
    u_got, p_got, d_parts = tie(u_got, p_got, d_parts)
    u_sum = added(kept(u_terms, 0, "img", u_got))
    p_sum = added(kept(p_terms, 0, "yy", p_got))
    part, cols = p_sum.shape[1], p_sum.shape[2]
    blocks = u_sum.shape[-1] // cols
    u_parts = tie(*band_parts(jnp.concatenate([u_sum, p_sum], axis=-1)))
    u_got = over_bands(u_parts)
    qa_got, qb_got, u_parts = tie(qa_got, qb_got, u_parts)
    qa_terms = kept(qa_terms, 0, "img", qa_got)
    qb_terms = kept(qb_terms, 1, "yy", qb_got)
    qa_out, qb_out = tie(to_send(qa_terms, 0, "yy"), to_send(qb_terms, 0, "img"))
    qa_got = sent(qa_out, "yy")
    qb_got = sent(qb_out, "img")
    back_ring, qa_out = tie(back_ring, qa_out)
    own_rows = band_rows_of(backs[1], back_ring)
    back_got = exchanged(own_rows)
    d_got, own_rows = tie(d_got, own_rows)
    d_sum = added([d_parts[0]] + d_got)
    d_all = to_bands(d_sum)
    qa_got, qb_got, d_sum = tie(qa_got, qb_got, d_sum)
    q_parts = tie(
        *band_parts(
            jnp.concatenate(
                [added(kept(qa_terms, 0, "yy", qa_got)), added(kept(qb_terms, 0, "img", qb_got))],
                axis=0,
            )
        )
    )
    q_got = over_bands(q_parts)
    u_got, q_parts, back_got = tie(u_got, q_parts, back_got)
    u_sum = added([u_parts[0]] + u_got)
    u_all = to_bands(u_sum)
    block_out, images_grad = unpacked(back_got, images.shape[2], (BF, F32))
    d_all, u_sum, block_out, total = tie(d_all, u_sum, block_out, total)
    d_own = jnp.stack([d_sum] + d_all)
    d_beside, d_other = swapped(d_own, "yy"), swapped(d_own, "core")
    q_got, d_own = tie(q_got, d_own)
    q_sum = added([q_parts[0]] + q_got)
    q_all = to_bands(q_sum)
    total = to_all(tie(total, q_sum)[0])
    d_beside, d_other, u_all, q_sum = tie(d_beside, d_other, u_all, q_sum)
    u_own = jnp.stack([u_sum] + u_all)
    u_beside, u_other = swapped(u_own, "yy"), swapped(u_own, "core")
    d_last = swapped(d_beside, "core")
    u_own, d_last, total = tie(u_own, d_last, total)
    (down_grad,) = final(marks, d_own, d_other, d_beside, d_last, ((d_own.shape[1], 0, 1),))
    q_all, down_grad = tie(q_all, down_grad)
    q_own = jnp.stack([q_sum] + q_all)
    q_beside, q_other = swapped(q_own, "yy"), swapped(q_own, "core")
    u_beside, q_own = tie(u_beside, q_own)
    u_last = swapped(u_beside, "core")
    up_grad, proj_grad = final(
        marks, u_own, u_other, u_beside, u_last, ((part, 0, blocks), (part, blocks, 1))
    )
    q_beside, up_grad = tie(q_beside, up_grad)
    q_last = swapped(q_beside, "core")
    (qkv_grad,) = final(marks, q_own, q_other, q_beside, q_last, ((q_own.shape[1], 0, 1),))
    total = total.reshape(-1)
    cut, at = [], 0
    for s in small:
        cut.append(total[at : at + s.size].reshape(s.shape))
        at += s.size
    distill_loss = cut[0][0] / (count_total * width)
    return (
        block_out[None], distill_loss, images_grad[None], cut[1], cut[2], qkv_grad, cut[3], cut[4],
        cut[5], cut[6], proj_grad, cut[7], cut[8], cut[9], up_grad, cut[10], down_grad, cut[11],
    )


def solution(mesh):
    shape = dict(mesh.shape)
    fine = Mesh(
        mesh.devices.reshape(shape["img"], shape["tok"], shape["seq"] // 2, 2), EVERY
    )
    tokens = P("img", ("tok",) + SEQ, None, None)
    mask = P("img", ("tok",) + SEQ, None)
    split, whole = P("img", None), P()
    return jax.shard_map(
        local,
        mesh=fine,
        in_specs=(
            tokens, tokens, mask, tokens, whole, whole, split, whole, whole, whole, whole, split,
            whole, whole, whole, split, whole, split, whole,
        ),
        out_specs=(
            tokens, whole, tokens, whole, whole, split, whole, whole, whole, whole, split, whole,
            whole, whole, split, whole, split, whole,
        ),
        check_vma=False,
    )
```

```python
import functools

import jax
import jax.numpy as jnp
import numpy as np
from jax import lax
from jax.experimental import pallas as pl
from jax.experimental.pallas import tpu as pltpu
from jax.sharding import Mesh
from jax.sharding import PartitionSpec as P

HD = 64
WIN = 14
SLOT = 16
EDGE = 8
EPS = 1e-06
KEYS = 256
LANES = 128
FAR = 128.0
BF = jnp.bfloat16
F32 = jnp.float32
SEQ = ("yy", "core")
EVERY = ("img", "tok", "yy", "core")


def swapped(block, axis):
    size = lax.axis_size(axis)
    return lax.ppermute(block, axis, [(i, size - 1 - i) for i in range(size)])


def moved(block, axis, pairs):
    return lax.ppermute(block, axis, pairs)


def pick(pair_low, pair_high, flag):
    return jnp.where(flag == 0, pair_low, pair_high)


def tie(*values):
    return lax.optimization_barrier(values)


def layout_marks(band, place):
    first, last = band == 0, band == lax.axis_size("tok") - 1
    turned = (first & (place == 0)) | (last & (place > 0))
    corner = first & (place == 2)
    edge = turned | jnp.where(first, place == 1, place == 0)
    start = 8 - 2 * band
    real = jnp.where(edge, WIN * EDGE, jnp.where(corner, EDGE * EDGE, 0))
    return (
        start, jnp.where(corner, 0, start), turned.astype(jnp.int32), real, first.astype(jnp.int32),
        band, lax.axis_index("yy"), lax.axis_index("core"),
    )


def whole_spec(shape):
    return pl.BlockSpec(shape, lambda *_: (0,) * len(shape))


def column_picks(ways, cols):
    out = np.zeros((ways, SLOT + EDGE, cols), np.float32)
    for s in range(ways):
        for j in range(SLOT):
            out[s, j, WIN * s + j] = 1.0
        for j in range(EDGE):
            out[s, SLOT + j, WIN * ways + j] = 1.0
    return out


def turn_picks():
    out = np.zeros((WIN * EDGE, EDGE * (SLOT + EDGE)), np.float32)
    for i in range(WIN):
        for j in range(EDGE):
            out[i * EDGE + j, j * (SLOT + EDGE) + i] = 1.0
    return out


def pack_kernel(picks, block, out):
    ways, full = out.shape[0], SLOT + EDGE
    for r in range(block.shape[1]):
        both = jnp.dot(picks[...], block[0, r], preferred_element_type=F32)
        for s in range(ways):
            out[s, 0, r] = both[s * full : (s + 1) * full].astype(BF)


def packed(block):
    count, rows, cols, width = block.shape
    ways = lax.axis_size("yy") * lax.axis_size("core")
    full = SLOT + EDGE
    picks = jnp.asarray(column_picks(ways, cols).reshape(ways * full, cols), BF)
    return pl.pallas_call(
        pack_kernel,
        grid=(count,),
        in_specs=[
            whole_spec(picks.shape),
            pl.BlockSpec((1, rows, cols, width), lambda n: (n, 0, 0, 0)),
        ],
        out_specs=pl.BlockSpec((ways, 1, rows, full, width), lambda n: (0, n, 0, 0, 0)),
        out_shape=jax.ShapeDtypeStruct((ways, count, rows, full, width), BF),
        cost_estimate=pl.CostEstimate(flops=0, bytes_accessed=0, transcendentals=0),
        name="pack",
    )(picks, block)


def window_kernel(at, got, ring, turn, out):
    count, rows = got.shape[1], got.shape[2]
    start_a, start_e, turned, first = at[0], at[1], at[2], at[4]
    for n in range(count):

        def row_of(row, cols):
            own = jnp.maximum(row - 8, 0)
            before = ring[n, jnp.minimum(row, 7), cols].astype(F32)
            return jnp.where(row < 8, before, got[own // rows, n, own % rows, cols].astype(F32))

        for i in range(WIN):
            full = row_of(start_a + i, slice(0, SLOT))
            out[n, i * SLOT : (i + 1) * SLOT] = full.astype(BF)
        edge = jnp.concatenate(
            [row_of(start_e + i, slice(SLOT, SLOT + EDGE)) for i in range(WIN)], axis=0
        )
        tail = jnp.concatenate(
            [
                jnp.where(first == 1, ring[n, k], got[2 + k // rows, n, k % rows]).astype(F32)
                for k in range(EDGE)
            ],
            axis=0,
        ).astype(BF)
        bottom = jnp.dot(turn[...], tail, preferred_element_type=F32)
        out[n, WIN * SLOT :] = jnp.where(turned == 1, bottom, edge).astype(BF)


def window_norm_kernel(at, got, ring, turn, gain, shift, out, low):
    window_kernel(at, got, ring, turn, out)
    for start, size in ((0, WIN * SLOT), (WIN * SLOT, WIN * EDGE)):
        unit, _ = norm_parts(out[0, start : start + size].astype(F32))
        row = lax.broadcasted_iota(jnp.int32, (size, 1), 0)
        real = (row & (SLOT - 1)) < WIN if start == 0 else row < at[3]
        low[start : start + size] = jnp.where(real, unit * gain[...] + shift[...], 0.0).astype(BF)


def ring_rows(got, step):
    bands = lax.axis_size("tok")
    send = jnp.moveaxis(got[2:], 1, 0)
    send = send.reshape(send.shape[0], 8, SLOT + EDGE, send.shape[-1])
    return moved(send, "tok", [(i, (i + step) % bands) for i in range(bands)])


def windowed(got, ring, marks, norm=None):
    count, width = got.shape[1], got.shape[-1]
    tokens = WIN * (SLOT + EDGE)
    specs = [
        whole_spec(got.shape),
        whole_spec(ring.shape),
        whole_spec((WIN * EDGE, EDGE * (SLOT + EDGE))),
    ]
    out_specs = [whole_spec((count, tokens, width))]
    out_shape = [jax.ShapeDtypeStruct((count, tokens, width), BF)]
    if norm is not None:
        specs += [whole_spec((width,))] * 2
        out_specs.append(whole_spec((tokens, width)))
        out_shape.append(jax.ShapeDtypeStruct((tokens, width), BF))
    return pl.pallas_call(
        window_kernel if norm is None else window_norm_kernel,
        grid_spec=pltpu.PrefetchScalarGridSpec(
            num_scalar_prefetch=1, grid=(1,), in_specs=specs, out_specs=out_specs
        ),
        out_shape=out_shape,
        cost_estimate=pl.CostEstimate(flops=0, bytes_accessed=0, transcendentals=0),
        name="window",
    )(marks, got, ring, jnp.asarray(turn_picks(), BF), *(norm or ()))


def unwindow(at, flats, turn, up, mid):
    start_a, start_e, turned, first = at[0], at[1], at[2], at[4]
    full = SLOT + EDGE
    for n, flat in enumerate(flats):
        bottom = lax.dot_general(
            turn[...],
            flat[WIN * SLOT :].astype(BF),
            (((0,), (0,)), ((), ())),
            preferred_element_type=F32,
        )
        for row in range(24):
            i = row - start_e
            held = (i >= 0) & (i < WIN) & (turned == 0)
            at_row = pl.multiple_of(WIN * SLOT + EDGE * jnp.clip(i, 0, WIN - 1), EDGE)
            right = jnp.where(held, flat[pl.ds(at_row, EDGE)], 0.0)
            i = row - start_a
            at_row = pl.multiple_of(SLOT * jnp.clip(i, 0, WIN - 1), SLOT)
            left = jnp.where((i >= 0) & (i < WIN), flat[pl.ds(at_row, SLOT)], 0.0)
            if row < 8 or row >= 16:
                base = row % 8 * full
                here = (turned == 1) & (first == (1 if row < 8 else 0))
                left = jnp.where(here, bottom[base : base + SLOT], left)
            both = jnp.concatenate([left, right], axis=0).astype(BF)
            if row < 8:
                up[n, row] = both
            else:
                mid[n, row - 8] = both


def unpack_kernel(picks, got, *outs):
    for n, out in enumerate(outs):
        for r in range(got.shape[2]):
            total = None
            for s in range(got.shape[0]):
                part = lax.dot_general(
                    picks[s], got[s, n, r], (((0,), (0,)), ((), ())), preferred_element_type=F32
                )
                total = part if total is None else total + part
            out[r] = total.astype(out.dtype)


def unpacked(got, cols, dtypes):
    ways, count, rows, full, width = got.shape
    picks = column_picks(ways, cols)
    picks[:, WIN:SLOT] = 0.0
    return pl.pallas_call(
        unpack_kernel,
        in_specs=[whole_spec(picks.shape), whole_spec(got.shape)],
        out_specs=[whole_spec((rows, cols, width))] * count,
        grid=(1,),
        out_shape=[jax.ShapeDtypeStruct((rows, cols, width), dtype) for dtype in dtypes],
        cost_estimate=pl.CostEstimate(flops=0, bytes_accessed=0, transcendentals=0),
        name="unpack",
    )(jnp.asarray(picks, BF), got)


def exchanged(send):
    return lax.all_to_all(send, SEQ, split_axis=0, concat_axis=0, tiled=True)


def sent_back(up):
    bands = lax.axis_size("tok")
    return moved(up, "tok", [((i + 1) % bands, i) for i in range(bands)])


def band_rows_of(mid, ring):
    own = mid + jnp.pad(ring, ((0, 0), (8, 0), (0, 0), (0, 0)))
    ways = lax.axis_size("yy") * lax.axis_size("core")
    own = own.reshape(own.shape[0], ways, 16 // ways, SLOT + EDGE, own.shape[-1])
    return jnp.swapaxes(own, 0, 1)


def two_images():
    return lax.axis_size("img") == 2


def quarter(shard):
    if not two_images():
        return shard
    rows = shard.shape[0] // 4
    at = lax.axis_index("yy") * 2 + lax.axis_index("core")
    return lax.dynamic_slice_in_dim(shard, at * rows, rows, 0)


def half_of(shard, chunks=1):
    if not two_images():
        return [shard]
    rows = shard.shape[0] // (2 * chunks)
    first = lax.axis_index("core") * rows * chunks
    return [lax.dynamic_slice_in_dim(shard, first + i * rows, rows, 0) for i in range(chunks)]


def over_images(block):
    if two_images():
        return swapped(block, "img")
    return lax.all_gather(block, "img", axis=0, tiled=True)


def half_over_cores(block):
    return (block, swapped(block, "core")) if two_images() else block


def assembled_halves(shard, *parts):
    if not two_images():
        return parts[0]
    core, image = lax.axis_index("core"), lax.axis_index("img")
    other = jnp.concatenate(
        [pick(here, there, core) for here, there in parts]
        + [pick(there, here, core) for here, there in parts],
        axis=0,
    )
    return jnp.concatenate([pick(shard, other, image), pick(other, shard, image)], axis=0)


def over_cores(block):
    return swapped(block, "core") if two_images() else block


def gather_over_rows(block):
    return swapped(block, "yy") if two_images() else block


def assembled(shard, first, second, first_across, second_across):
    if not two_images():
        return first
    core, high, image = (lax.axis_index(a) for a in ("core", "yy", "img"))
    rows = []
    for a, b, c, d in ((first, second, first_across, second_across), (second, first, second_across, first_across)):
        here, there = pick(a, b, high), pick(c, d, high)
        rows += [pick(here, there, core), pick(there, here, core)]
    other = jnp.concatenate(rows, axis=0)
    return jnp.concatenate([pick(shard, other, image), pick(other, shard, image)], axis=0)


def part_of(terms, dim, axis, other):
    index = lax.axis_index(axis)
    index = 1 - index if other else index
    return [lax.dynamic_index_in_dim(t, index, dim, keepdims=False) for t in terms]


def added(terms):
    total = terms[0].astype(F32)
    for t in terms[1:]:
        total = total + t.astype(F32)
    return total.astype(BF)


def to_send(terms, dim, axis):
    if lax.axis_size(axis) != 2:
        return jnp.moveaxis(added(terms), dim, 0)
    return added(part_of(terms, dim, axis, True))


def sent(block, axis):
    if lax.axis_size(axis) != 2:
        return lax.all_to_all(block, axis, split_axis=0, concat_axis=0, tiled=True)
    return swapped(block, axis)


def kept(terms, dim, axis, got):
    if lax.axis_size(axis) != 2:
        return [got[i] for i in range(got.shape[0])]
    return part_of(terms, dim, axis, False) + [got]


def split_grad(left, right):
    images, bands = lax.axis_size("img"), lax.axis_size("tok")
    core = lax.axis_index("core")
    rows, cols = left.shape[1], right.shape[1] // 2
    shape = (images, 2, bands, rows // images // 2 // bands, cols)

    def one(index):
        half = lax.dynamic_slice_in_dim(right, index * cols, cols, 1)
        return mm_tn(left, half).astype(BF).reshape(shape)

    return one(1 - core), one(core)


def crossed(block, distance):
    size = lax.axis_size("tok")
    return lax.ppermute(block, "tok", [(i, i ^ distance) for i in range(size)])


def band_parts(piece):
    band = lax.axis_index("tok")
    return [
        lax.dynamic_index_in_dim(piece, band ^ d, 0, keepdims=False)
        for d in range(lax.axis_size("tok"))
    ]


def over_bands(parts):
    return [crossed(part, d) for d, part in enumerate(parts) if d > 0]


def to_bands(total):
    return [crossed(total, d) for d in range(1, lax.axis_size("tok"))]


def final_kernel(splits, unit, at, near_own, near_other, far_own, far_other, *outs):
    band, core = at[5], at[7]

    def write(own, other):
        for t in range(own.shape[0]):
            to = t ^ band
            for (rows, first, blocks), out in zip(splits, outs):
                size = blocks * unit
                a = own[t, :, first * unit : first * unit + size].astype(F32)
                b = other[t, :, first * unit : first * unit + size].astype(F32)
                out[0, to, :, :size] = jnp.where(core == 0, a, b)
                out[0, to, :, size:] = jnp.where(core == 0, b, a)

    @pl.when(pl.program_id(0) == 0)
    def near():
        write(near_own, near_other)

    @pl.when(pl.program_id(0) == 1)
    def far():
        write(far_own, far_other)


def final(marks, own, other_core, beside, beside_other_core, splits):
    bands, rows, cols = own.shape
    unit = cols // sum(blocks for _, _, blocks in splits)
    outs = pl.pallas_call(
        functools.partial(final_kernel, splits, unit),
        grid_spec=pltpu.PrefetchScalarGridSpec(
            num_scalar_prefetch=1,
            grid=(2,),
            in_specs=[whole_spec(own.shape)] * 4,
            out_specs=[
                pl.BlockSpec((1, bands, n, 2 * blocks * unit), lambda y, at: (y ^ at[6], 0, 0, 0))
                for n, _, blocks in splits
            ],
        ),
        out_shape=[
            jax.ShapeDtypeStruct((2, bands, n, 2 * blocks * unit), F32) for n, _, blocks in splits
        ],
        cost_estimate=pl.CostEstimate(flops=0, bytes_accessed=0, transcendentals=0),
        name="final",
    )(marks, own, other_core, beside, beside_other_core)
    return [o.reshape(-1, o.shape[-1]) for o in outs]


def paired(value, axis):
    if axis == "img" and not two_images():
        return lax.psum(value, "img")
    across = crossed(value, axis) if isinstance(axis, int) else swapped(value, axis)
    return value + across


def small_pack_kernel(*refs):
    vectors, up_bias, tables, squares, out = refs[:8], refs[8], refs[9], refs[10], refs[11]
    width = out.shape[1]
    for i, vector in enumerate(vectors):
        out[i, :] = vector[...]
    row = len(vectors)
    for i in range(up_bias.shape[0] // width):
        out[row, :] = up_bias[i * width : (i + 1) * width]
        row += 1
    fit = width // LANES
    for m in range(2 * WIN - 1):
        at = (m % fit) * LANES
        out[row + m // fit, at : at + LANES] = tables[m, :]
    row += -(-(2 * WIN - 1) // fit)
    out[row, :LANES] = squares[...]


def small_packed(vectors, up_bias, tables, squares):
    width = vectors[0].shape[0]
    rows = len(vectors) + up_bias.shape[0] // width - (-(2 * WIN - 1) // (width // LANES)) + 1
    args = (*vectors, up_bias, tables, squares)
    return pl.pallas_call(
        small_pack_kernel,
        grid=(1,),
        in_specs=[whole_spec(a.shape) for a in args],
        out_specs=whole_spec((rows, width)),
        out_shape=jax.ShapeDtypeStruct((rows, width), F32),
        cost_estimate=pl.CostEstimate(flops=0, bytes_accessed=0, transcendentals=0),
        name="small_pack",
    )(*args)


def small_unpack_kernel(packed, *outs):
    vectors, up_bias, rows_out, cols_out, squares = outs[:8], outs[8], outs[9], outs[10], outs[11]
    width = packed.shape[1]
    for i, vector in enumerate(vectors):
        vector[...] = packed[i, :]
    row = len(vectors)
    for i in range(up_bias.shape[0] // width):
        up_bias[i * width : (i + 1) * width] = packed[row, :]
        row += 1
    fit = width // LANES
    for m in range(2 * WIN - 1):
        at = (m % fit) * LANES
        both = packed[row + m // fit : row + m // fit + 1, at : at + LANES]
        rows_out[m : m + 1, :] = both[:, :HD]
        cols_out[m : m + 1, :] = pltpu.roll(both, HD, 1)[:, :HD]
    row += -(-(2 * WIN - 1) // fit)
    squares[...] = packed[row, :LANES]


def small_unpacked(packed, vectors, up_width):
    width = packed.shape[1]
    table = (2 * WIN - 1, HD)
    shapes = [(width,)] * vectors + [(up_width,), table, table, (LANES,)]
    return pl.pallas_call(
        small_unpack_kernel,
        grid=(1,),
        in_specs=[whole_spec(packed.shape)],
        out_specs=[whole_spec(shape) for shape in shapes],
        out_shape=[jax.ShapeDtypeStruct(shape, F32) for shape in shapes],
        cost_estimate=pl.CostEstimate(flops=0, bytes_accessed=0, transcendentals=0),
        name="small_unpack",
    )(packed)


def rolled(block, amount):
    return pltpu.roll(block, amount, 1, stride=1, stride_axis=0)


def rel_places():
    size = 2 * WIN - 1
    out = np.zeros((4, LANES, size), np.float32)
    for m in range(size):
        out[0, size - 1 - m, m] = 1.0
        out[1, 32 + size - 1 - m, m] = 1.0
        out[2, m, m] = 1.0
        out[3, 64 + m, m] = 1.0
    return out


def head_places():
    out = np.zeros((2, HD, LANES), np.float32)
    for c in range(HD):
        out[0, c, c] = 1.0
        out[1, c, HD + c] = 1.0
    return out


def build_rel(tables, places, heads, out):
    for half in (0, 1):
        total = None
        for table, place in zip(tables, places):
            high = table.astype(BF)
            value = (table - high.astype(F32)).astype(BF) if half else high
            part = jnp.dot(place, value, preferred_element_type=F32)
            total = part if total is None else total + part
        for head in (0, 1):
            lanes = jnp.dot(total.astype(BF), heads[head], preferred_element_type=F32)
            out[head, :, half * LANES : (half + 1) * LANES] = lanes.astype(BF)


def build_both(at, rows, cols, places, heads, rel_a, rel_b):
    @pl.when(pl.program_id(0) == 0)
    def build():
        turned = at[2] == 1
        build_rel((rows[...], cols[...]), places, heads, rel_a)
        first = jnp.where(turned, cols[...], rows[...])
        second = jnp.where(turned, rows[...], cols[...])
        build_rel((first, second), places, heads, rel_b)


def rel_terms(q, rel):
    return lax.dot_general(
        jnp.concatenate([q, q], axis=1), rel, (((1,), (1,)), ((), ())), preferred_element_type=F32
    )


def wide_queries(q, terms, group):
    m = q.shape[0]
    lane = lax.broadcasted_iota(jnp.int32, (group, LANES), 1)
    blocks = []
    for i in range(WIN):
        t = terms[i * group : (i + 1) * group]
        by_row = pltpu.roll(t, (LANES - (WIN - 1) + i) % LANES, 1)
        by_col = rolled(t, 19)
        blocks.append(jnp.where(lane < 64, by_row, by_col))
    both = jnp.concatenate(blocks, axis=0)
    high = both.astype(BF).astype(F32)
    low = pltpu.roll(both - high, 32, 1)
    lane = lax.broadcasted_iota(jnp.int32, (m, LANES), 1)
    mixed = jnp.where((lane & 63) < 32, high, low)
    mixed = jnp.where(lane == LANES - 1, 1.0, mixed)
    return jnp.concatenate([q * BF(HD**-0.5), mixed.astype(BF)], axis=1)


def full_keys(k, v, v_pad):
    n = k.shape[0]
    zeros = jnp.zeros((KEYS - n, LANES), BF)
    if v_pad is None:
        return jnp.concatenate([k, zeros], axis=0), jnp.concatenate([v, zeros], axis=0)
    fill = jnp.broadcast_to(v_pad, (KEYS - n, LANES)).astype(BF)
    return jnp.concatenate([k, zeros], axis=0), jnp.concatenate([v, fill], axis=0)


def only(block, head):
    lane = lax.broadcasted_iota(jnp.int32, block.shape, 1)
    return jnp.where((lane < HD) == (head == 0), block, jnp.zeros_like(block))


def scored(wide, keys, hot, head):
    return lax.dot_general(
        wide,
        jnp.concatenate([only(keys, head), hot], axis=1),
        (((1,), (1,)), ((), ())),
        preferred_element_type=F32,
    )


def softmax_low(scores):
    e = jnp.exp(scores - jnp.max(scores, axis=1, keepdims=True))
    return (e * (1.0 / jnp.sum(e, axis=1, keepdims=True))).astype(BF)


def attend_kernel(
    at, q, k, v, v_pad, rows, cols, places, heads, hot_a, hot_b, out, probs_a, probs_b, rel_a, rel_b
):
    build_both(at, rows, cols, (places[0], places[1]), heads, rel_a, rel_b)
    n = WIN * SLOT
    pad = v_pad[...].astype(BF)
    slots = (
        (slice(0, n), None, rel_a, hot_a, SLOT, probs_a),
        (slice(n, n + WIN * EDGE), pad, rel_b, hot_b, EDGE, probs_b),
    )
    both = [(s, h) for s in (0, 1) for h in (0, 1)]
    queries = [q[slot[0]] for slot in slots]
    terms = [
        rel_terms(queries[i], slots[i][2][...].reshape(2 * LANES, 2 * LANES)) for i in (0, 1)
    ]
    filled = [full_keys(k[slot[0]], v[slot[0]], slot[1]) for slot in slots]
    wide = [
        wide_queries(queries[i], terms[i][:, h * LANES : (h + 1) * LANES], slots[i][4])
        for i, h in both
    ]
    scores = [scored(w, filled[i][0], slots[i][3][...], h) for w, (i, h) in zip(wide, both)]
    probs = [softmax_low(x) for x in scores]
    for p, (i, h) in zip(probs, both):
        slots[i][5][h] = p
    parts = [
        jnp.dot(p, only(filled[i][1], h), preferred_element_type=F32)
        for p, (i, h) in zip(probs, both)
    ]
    for i in (0, 1):
        out[slots[i][0]] = (parts[2 * i] + parts[2 * i + 1]).astype(BF)


def back_terms(both, group):
    lane = lax.broadcasted_iota(jnp.int32, (group, LANES), 1)
    blocks = []
    for i in range(WIN):
        t = both[i * group : (i + 1) * group, LANES:]
        by_row = jnp.where(lane < WIN, t, 0.0)
        by_row = pltpu.roll(by_row, i, 1) if i else by_row
        by_col = rolled(jnp.where((lane >= 64) & (lane < 64 + WIN), t, 0.0), 0)
        blocks.append(by_row + by_col)
    terms = jnp.concatenate(blocks, axis=0)
    high = terms.astype(BF)
    return jnp.concatenate([high, (terms - high.astype(F32)).astype(BF)], axis=1)


def over_rows(left, right):
    return lax.dot_general(left, right, (((0,), (0,)), ((), ())), preferred_element_type=F32)


def attend_back_kernel(
    at, q, k, v, v_pad, rows, cols, places, heads, hot_a, hot_b, grad, probs_a, probs_b,
    dqkv, pad_sum, rel_grad, rel_a, rel_b, acc_a, acc_b,
):
    step = pl.program_id(0)
    steps = dqkv.shape[1] // (3 * LANES)
    build_both(at, rows, cols, (places[2], places[3]), heads, rel_a, rel_b)

    @pl.when(step == 0)
    def clear():
        acc_a[...] = jnp.zeros_like(acc_a)
        acc_b[...] = jnp.zeros_like(acc_b)

    n = WIN * SLOT
    scale = HD**-0.5
    pad = v_pad[...].astype(BF)
    slots = (
        (slice(0, n), None, rel_a, hot_a, SLOT, probs_a, acc_a),
        (slice(n, n + WIN * EDGE), pad, rel_b, hot_b, EDGE, probs_b, acc_b),
    )
    both = [(s, h) for s in (0, 1) for h in (0, 1)]
    queries = [q[slot[0]] for slot in slots]
    grads = [grad[slot[0]] for slot in slots]
    filled = [full_keys(k[slot[0]], v[slot[0]], slot[1]) for slot in slots]
    probs_grad = [
        lax.dot_general(
            grads[i], only(filled[i][1], h), (((1,), (1,)), ((), ())), preferred_element_type=F32
        )
        for i, h in both
    ]
    dvs = [over_rows(slots[i][5][h], grads[i]) for i, h in both]
    scores_grad = []
    for dp, (i, h) in zip(probs_grad, both):
        wide = slots[i][5][h].astype(F32)
        inner = jnp.sum(wide * dp, axis=1, keepdims=True)
        scores_grad.append((wide * (dp - inner)).astype(BF))
    sums = [
        jnp.dot(
            ds,
            jnp.concatenate([only(filled[i][0], h), slots[i][3][...]], axis=1),
            preferred_element_type=F32,
        )
        for ds, (i, h) in zip(scores_grad, both)
    ]
    dks = [over_rows(ds, queries[i]) * scale for ds, (i, h) in zip(scores_grad, both)]
    split = [back_terms(x, slots[i][4]) for x, (i, h) in zip(sums, both)]
    parts = []
    for x, t, (i, h) in zip(sums, split, both):
        rel = slots[i][2][h]
        part = x[:, :LANES] * scale + jnp.dot(
            t,
            jnp.concatenate([rel[:, :LANES], rel[:, :LANES]], axis=0),
            preferred_element_type=F32,
        )
        parts.append(part + jnp.dot(t[:, :LANES], rel[:, LANES:], preferred_element_type=F32))
    for t, (i, h) in zip(split, both):
        slots[i][6][h] += over_rows(t, queries[i])
    lane = lax.broadcasted_iota(jnp.int32, (KEYS, LANES), 1)
    for i in (0, 1):
        here, size = slots[i][0], queries[i].shape[0]
        dk = jnp.where(lane < HD, dks[2 * i], dks[2 * i + 1]).astype(BF)
        dv = jnp.where(lane < HD, dvs[2 * i], dvs[2 * i + 1]).astype(BF)
        found = ((parts[2 * i] + parts[2 * i + 1]).astype(BF), dk[:size], dv[:size])
        for j, value in enumerate(found):
            to = pl.ds(pl.multiple_of((j * steps + step) * LANES, LANES), LANES)
            dqkv[here, to] = value
    pad_sum[...] = jnp.sum(dv[WIN * EDGE :].astype(F32), axis=0, keepdims=True)

    @pl.when(step == steps - 1)
    def tables():
        def table(acc):
            even = acc[0, :LANES] + acc[0, LANES:]
            odd = acc[1, :LANES] + acc[1, LANES:]
            return even + pltpu.roll(odd, HD, 1)

        a, b = table(acc_a), table(acc_b)
        turned = at[2] == 1
        low, high = slice(0, 32), slice(64, 96)
        rows_grad = a[low] + jnp.where(turned, b[high], b[low])
        cols_grad = a[high] + jnp.where(turned, b[low], b[high])
        lane = lax.broadcasted_iota(jnp.int32, (32, LANES), 1)
        rel_grad[...] = jnp.where(lane < HD, rows_grad, pltpu.roll(cols_grad, HD, 1))


def hot_tables():
    def table(place):
        out = np.zeros((2, KEYS, LANES), np.float32)
        for key in range(KEYS):
            at = place(key)
            if at is None:
                out[0, key, LANES - 1] = -1e30
            else:
                for base, index in ((0, at[0]), (32, at[0]), (64, at[1]), (96, at[1])):
                    out[0, key, base + index] = 1.0
                out[1, key, WIN - 1 - at[0]] = 1.0
                out[1, key, 64 + WIN - 1 - at[1]] = 1.0
        return out

    def whole(key):
        i, j = divmod(key, SLOT)
        return (i, j) if i < WIN and j < WIN else None

    def partial(key):
        if key < WIN * EDGE:
            return divmod(key, EDGE)
        i, j = divmod(key - WIN * EDGE, EDGE)
        return (i, EDGE + j) if i < WIN and EDGE + j < WIN else None

    return table(whole), table(partial)


def attention(qkv, v_pad, rel_rows, rel_cols, marks):
    tokens_a, tokens_b = WIN * SLOT, WIN * EDGE
    tokens, width = qkv.shape[0], qkv.shape[1] // 3
    pairs = width // LANES
    table = (2 * WIN - 1, HD)
    hots = [jnp.asarray(t, BF) for t in hot_tables()]
    places, heads = jnp.asarray(rel_places(), BF), jnp.asarray(head_places(), BF)

    def cols(n, base):
        return pl.BlockSpec((n, LANES), lambda p, at: (0, base * pairs + p))

    specs = [cols(tokens, i) for i in range(3)] + [
        pl.BlockSpec((LANES,), lambda p, at: (p,)),
        whole_spec(table),
        whole_spec(table),
        whole_spec(places.shape),
        whole_spec(heads.shape),
        whole_spec((KEYS, LANES)),
        whole_spec((KEYS, LANES)),
    ]
    probs_specs = [
        pl.BlockSpec((2, tokens_a, KEYS), lambda p, at: (p, 0, 0)),
        pl.BlockSpec((2, tokens_b, KEYS), lambda p, at: (p, 0, 0)),
    ]
    rel_scratch = [pltpu.VMEM((2, LANES, 2 * LANES), BF)] * 2
    shared = (marks, qkv, qkv, qkv, v_pad, rel_rows, rel_cols, places, heads)
    out, probs_a, probs_b = pl.pallas_call(
        attend_kernel,
        grid_spec=pltpu.PrefetchScalarGridSpec(
            num_scalar_prefetch=1,
            grid=(pairs,),
            in_specs=specs,
            out_specs=[cols(tokens, 0)] + probs_specs,
            scratch_shapes=rel_scratch,
        ),
        out_shape=[
            jax.ShapeDtypeStruct((tokens, width), BF),
            jax.ShapeDtypeStruct((2 * pairs, tokens_a, KEYS), BF),
            jax.ShapeDtypeStruct((2 * pairs, tokens_b, KEYS), BF),
        ],
        cost_estimate=pl.CostEstimate(flops=0, bytes_accessed=0, transcendentals=0),
        name="attend",
    )(*shared, hots[0][0], hots[1][0])

    def back(grad):
        return pl.pallas_call(
            attend_back_kernel,
            grid_spec=pltpu.PrefetchScalarGridSpec(
                num_scalar_prefetch=1,
                grid=(pairs,),
                in_specs=specs + [cols(tokens, 0)] + probs_specs,
                out_specs=[
                    whole_spec((tokens, 3 * width)),
                    cols(1, 0),
                    whole_spec((32, LANES)),
                ],
                scratch_shapes=rel_scratch + [pltpu.VMEM((2, 2 * LANES, LANES), F32)] * 2,
            ),
            out_shape=[
                jax.ShapeDtypeStruct((tokens, 3 * width), BF),
                jax.ShapeDtypeStruct((1, width), F32),
                jax.ShapeDtypeStruct((32, LANES), F32),
            ],
            cost_estimate=pl.CostEstimate(flops=0, bytes_accessed=0, transcendentals=0),
            name="attend_back",
        )(*shared, hots[0][1], hots[1][1], grad, probs_a, probs_b)

    return out, back


def norm_parts(values):
    centre = jnp.mean(values, axis=-1, keepdims=True)
    centred = values - centre
    spread = jnp.mean(centred * centred, axis=-1, keepdims=True)
    scale = lax.rsqrt(spread + EPS)
    return centred * scale, scale


def norm_back(grad, unit, scale, gain):
    g = grad * gain
    mean = jnp.mean(g, axis=-1, keepdims=True)
    along = jnp.mean(g * unit, axis=-1, keepdims=True)
    return scale * (g - mean - unit * along)


def mlp_back_kernel(
    pre, up, resid, result_grad, gain, proj, resid_grad, proj_in, attended_grad, gain_grad, shift_grad,
    proj_bias_grad, up_bias_grad, total,
):
    step = pl.program_id(0)
    part = mm_nt(pre[...], up[...])
    up_bias_grad[...] = jnp.sum(pre[...].astype(F32), axis=0)

    @pl.when(step == 0)
    def first():
        total[...] = part

    @pl.when(step > 0)
    def more():
        total[...] += part

    @pl.when(step == pl.num_programs(0) - 1)
    def last():
        grad = total[...]
        unit, scale = norm_parts(resid[...])
        gain_grad[...] = jnp.sum(grad * unit, axis=0)
        shift_grad[...] = jnp.sum(grad, axis=0)
        found = result_grad[...] + norm_back(grad, unit, scale, gain[...])
        resid_grad[...] = found
        low = found.astype(BF)
        proj_in[...] = low
        proj_bias_grad[...] = jnp.sum(low.astype(F32), axis=0)
        attended_grad[...] = mm_nt(low, proj[...]).astype(BF)


def mlp_back(pre_grad, up_full, resid, result_grad, gain, proj_full):
    tokens, hidden = pre_grad.shape
    width = resid.shape[1]
    size = 1024
    steps = hidden // size
    flat = jax.ShapeDtypeStruct((width,), F32)
    return pl.pallas_call(
        mlp_back_kernel,
        grid=(steps,),
        in_specs=[
            pl.BlockSpec((tokens, size), lambda k: (0, k)),
            pl.BlockSpec((width, size), lambda k: (0, k)),
            whole_spec(resid.shape),
            whole_spec(resid.shape),
            whole_spec((width,)),
            whole_spec(proj_full.shape),
        ],
        out_specs=[whole_spec(resid.shape)] * 3
        + [whole_spec((width,))] * 3
        + [pl.BlockSpec((size,), lambda k: (k,))],
        out_shape=[
            jax.ShapeDtypeStruct(resid.shape, F32),
            jax.ShapeDtypeStruct(resid.shape, BF),
            jax.ShapeDtypeStruct(resid.shape, BF),
            flat,
            flat,
            flat,
            jax.ShapeDtypeStruct((hidden,), F32),
        ],
        scratch_shapes=[pltpu.VMEM(resid.shape, F32)],
        cost_estimate=pl.CostEstimate(flops=0, bytes_accessed=0, transcendentals=0),
        name="mlp_back",
    )(pre_grad, up_full, resid, result_grad, gain, proj_full)


def input_back_kernel(
    at, dqkv, weight, low, resid_grad, result, gain, pad_sum, turn, up, mid, gain_grad, shift_grad,
    query_sum, value_sum, total, block,
):
    step = pl.program_id(0)
    part = mm_nt(dqkv[...], weight[...])
    sums = jnp.sum(dqkv[...].astype(F32), axis=0)

    @pl.when(step == 0)
    def first():
        total[...] = part
        query_sum[...] = sums

    @pl.when(step > 0)
    def more():
        total[...] += part

    @pl.when(step == pl.num_programs(0) - 1)
    def last():
        value_sum[...] = sums + pad_sum[0]
        row = lax.broadcasted_iota(jnp.int32, (total.shape[0], 1), 0)
        full = WIN * SLOT
        limit = jnp.where(row < full, row - (row & (SLOT - 1)) + WIN, full + at[3])
        real = row < limit
        grad = jnp.where(real, total[...], 0.0)
        unit, scale = norm_parts(low[...].astype(F32))
        gain_grad[...] = jnp.sum(grad * unit, axis=0)
        shift_grad[...] = jnp.sum(grad, axis=0)
        total[...] = resid_grad[...] + norm_back(grad, unit, scale, gain[...])
        block[...] = jnp.where(real, result[...], 0.0)
        unwindow(at, (block, total), turn, up, mid)


def input_back(marks, dqkv, qkv_full, low, resid_grad, result, gain, pad_sum):
    tokens, width = low.shape
    full = SLOT + EDGE
    flat = jax.ShapeDtypeStruct((width,), F32)
    shapes = [(2, 8, full, width), (2, 16, full, width)]
    return pl.pallas_call(
        input_back_kernel,
        grid_spec=pltpu.PrefetchScalarGridSpec(
            num_scalar_prefetch=1,
            grid=(3,),
            in_specs=[
                pl.BlockSpec((tokens, width), lambda k, at: (0, k)),
                pl.BlockSpec((width, width), lambda k, at: (0, k)),
                whole_spec(low.shape),
                whole_spec(low.shape),
                whole_spec(low.shape),
                whole_spec((width,)),
                whole_spec((1, width)),
                whole_spec((WIN * EDGE, EDGE * full)),
            ],
            out_specs=[whole_spec(shape) for shape in shapes] + [whole_spec((width,))] * 4,
            scratch_shapes=[pltpu.VMEM(low.shape, F32)] * 2,
        ),
        out_shape=[jax.ShapeDtypeStruct(shape, BF) for shape in shapes] + [flat] * 4,
        cost_estimate=pl.CostEstimate(flops=0, bytes_accessed=0, transcendentals=0),
        name="input_back",
    )(marks, dqkv, qkv_full, low, resid_grad, result, gain, pad_sum, jnp.asarray(turn_picks(), BF))


def mm(a, b):
    return jnp.dot(a, b, preferred_element_type=F32)


def mm_nt(a, b):
    return lax.dot_general(a, b, (((1,), (1,)), ((), ())), preferred_element_type=F32)


def mm_tn(a, b):
    return lax.dot_general(a, b, (((0,), (0,)), ((), ())), preferred_element_type=F32)


def local(
    images, teacher, valid_mask, out_grad, attn_gain, attn_shift, qkv_weight, query_bias,
    value_bias, rel_rows, rel_cols, proj_weight, proj_bias, mlp_gain, mlp_shift, up_weight,
    up_bias, down_weight, down_bias,
):
    band = lax.axis_index("tok")
    bands = lax.axis_size("tok")
    place = lax.axis_index("yy") * lax.axis_size("core") + lax.axis_index("core")
    width = images.shape[-1]
    image_rows = images.shape[1] * bands * lax.axis_size("yy") * lax.axis_size("core")
    tokens_all = images.shape[0] * lax.axis_size("img") * image_rows * images.shape[2]

    marks = layout_marks(band, place)
    real_edge = marks[3]
    marks = jnp.stack(marks).astype(jnp.int32)
    x_got = exchanged(packed(images))
    qkv_1 = over_images(quarter(qkv_weight))
    proj_1 = [over_images(c) for c in half_of(proj_weight)]
    up_1 = [over_images(c) for c in half_of(up_weight, 2)]
    down_1 = [over_images(c) for c in half_of(down_weight, 2)]
    count = jnp.broadcast_to(jnp.sum(valid_mask.astype(F32)), (8, LANES))
    count = paired(count, "img")
    x_got, qkv_1, marks, count = tie(x_got, qkv_1, marks, count)
    qkv_2 = gather_over_rows(qkv_1)
    x_ring = ring_rows(x_got, 1)
    qkv_3 = over_cores(qkv_1)
    count = paired(count, "core")
    marked = jnp.where(valid_mask[..., None] > 0, teacher, jnp.full_like(teacher, FAR))
    late_pack = packed(tie(jnp.concatenate([marked, out_grad], axis=0), qkv_1)[0])
    x_ring, x_got, late_pack, up_1[0], count = tie(x_ring, x_got, late_pack, up_1[0], count)
    x_low, tokens_low = windowed(x_got, x_ring, marks, (attn_gain, attn_shift))
    x_low = x_low[0]
    count = paired(count, "yy")
    qkv_2, x_low, tokens_low, qkv_3 = tie(qkv_2, x_low, tokens_low, qkv_3)
    qkv_4 = over_cores(qkv_2)
    up_2 = [half_over_cores(up_1[0])]
    qkv_4, proj_1[0], count = tie(qkv_4, proj_1[0], count)
    proj_2 = half_over_cores(proj_1[0])
    count = paired(count, 1)

    row_a = lax.broadcasted_iota(jnp.int32, (WIN * SLOT, 1), 0)
    row_b = lax.broadcasted_iota(jnp.int32, (WIN * EDGE, 1), 0)
    real = jnp.concatenate(
        [(row_a & (SLOT - 1)) < WIN, row_b < real_edge], axis=0
    )
    inputs = x_low.astype(F32)
    qkv_bias = jnp.concatenate([query_bias, jnp.zeros_like(query_bias), value_bias])
    qkv_full = assembled(qkv_weight, qkv_1, qkv_2, qkv_3, qkv_4)
    qkv = (mm(tokens_low, qkv_full) + qkv_bias).astype(BF)
    qkv, late_pack, proj_2, count, up_2 = tie(qkv, late_pack, proj_2, count, up_2)
    late_got = exchanged(late_pack)
    count = paired(count, 2)
    attended, attention_back = attention(qkv, value_bias, rel_rows, rel_cols, marks)
    proj_full = assembled_halves(proj_weight, proj_2)
    attended, up_1, proj_full, count = tie(attended, up_1, proj_full, count)
    up_2 = up_2 + [half_over_cores(c) for c in up_1[1:]]
    resid = inputs + mm(attended, proj_full) + proj_bias
    unit2, scale2 = norm_parts(resid)
    normed2 = (unit2 * mlp_gain + mlp_shift).astype(BF)
    up_full = assembled_halves(up_weight, *up_2)
    normed2, up_full, late_got, down_1[0] = tie(normed2, up_full, late_got, down_1[0])
    late_ring = ring_rows(late_got, 1)
    hidden_pre = mm(normed2, up_full) + up_bias
    cdf = 0.5 * (1.0 + lax.erf(hidden_pre * (0.5**0.5)))
    hidden = (hidden_pre * cdf).astype(BF)
    slope = cdf + hidden_pre * jnp.exp(-0.5 * hidden_pre * hidden_pre) * ((2 * np.pi) ** -0.5)
    hidden, slope, late_ring, down_1 = tie(hidden, slope, late_ring, down_1)
    count_total = count[0, 0]
    down_2 = [half_over_cores(c) for c in down_1]
    (late,) = windowed(late_got, late_ring, marks)
    late, down_2 = tie(late, down_2)
    down_full = assembled_halves(down_weight, *down_2)
    result = resid + mm(hidden, down_full) + down_bias

    teach = late[0].astype(F32)
    valid = (real & (teach[:, :1] < 0.5 * FAR)).astype(F32)
    differ = valid * (result - teach)
    squares = jnp.sum(differ * differ)
    grads = jnp.where(real, late[1], jnp.zeros_like(late[1])).astype(F32)
    result_grad = grads + differ * (tokens_all / (4.0 * count_total))
    down_in = result_grad.astype(BF)

    d_send, d_keep = split_grad(hidden, down_in)
    d_send, down_in = tie(d_send, down_in)
    d_got = sent(d_send, "core")
    pre_grad = (slope * mm_nt(down_in, down_full)).astype(BF)
    d_got, d_keep, pre_grad = tie(d_got, d_keep, pre_grad)
    d_terms = [d_keep, d_got]
    d_out, pre_grad = tie(to_send(d_terms, 0, "img"), pre_grad)
    d_got = sent(d_out, "img")
    u_send, u_keep = split_grad(normed2, pre_grad)
    u_send, pre_grad = tie(u_send, pre_grad)
    u_got = sent(u_send, "core")
    u_got, u_keep, pre_grad = tie(u_got, u_keep, pre_grad)
    u_terms = [u_keep, u_got]
    u_out, pre_grad = tie(to_send(u_terms, 1, "yy"), pre_grad)
    u_got = sent(u_out, "yy")
    (
        resid_grad, proj_in, attended_grad, mlp_gain_grad, mlp_shift_grad, proj_bias_grad, up_bias_grad
    ) = mlp_back(pre_grad, up_full, resid, result_grad, mlp_gain, proj_full)
    p_send, p_keep = split_grad(attended, proj_in)
    p_send, proj_in = tie(p_send, proj_in)
    p_got = sent(p_send, "core")
    attended_grad, p_got, p_keep = tie(attended_grad, p_got, p_keep)
    p_terms = [p_keep, p_got]
    p_out, attended_grad = tie(to_send(p_terms, 0, "img"), attended_grad)
    p_got = sent(p_out, "img")

    dqkv, pad_sum, rel_grad = attention_back(attended_grad)
    dqkv, pad_sum, d_got, u_got = tie(dqkv, pad_sum, d_got, u_got)
    d_terms = kept(d_terms, 0, "img", d_got)
    u_terms = kept(u_terms, 1, "yy", u_got)
    d_out, u_out, dqkv = tie(to_send(d_terms, 0, "yy"), to_send(u_terms, 0, "img"), dqkv)
    d_got = sent(d_out, "yy")
    u_got = sent(u_out, "img")
    q_send, q_keep = split_grad(tokens_low, dqkv)
    q_send, dqkv = tie(q_send, dqkv)
    q_got = sent(q_send, "core")
    q_got, q_keep, dqkv, p_got = tie(q_got, q_keep, dqkv, p_got)
    p_terms = kept(p_terms, 0, "img", p_got)
    half = bands // 2
    qa_terms = [q_keep[:, :, :half], q_got[:, :, :half]]
    qb_terms = [q_keep[:, :, half:], q_got[:, :, half:]]
    qa_out, qb_out, p_out, dqkv = tie(
        to_send(qa_terms, 0, "img"), to_send(qb_terms, 1, "yy"), to_send(p_terms, 0, "yy"), dqkv
    )
    qa_got = sent(qa_out, "img")
    qb_got = sent(qb_out, "yy")
    p_got = sent(p_out, "yy")
    down_bias_grad = jnp.sum(down_in.astype(F32), axis=0)
    *backs, attn_gain_grad, attn_shift_grad, query_bias_grad, value_bias_grad = input_back(
        marks, dqkv, qkv_full, x_low, resid_grad, result, attn_gain, pad_sum
    )
    small = small_packed(
        (
            attn_gain_grad, attn_shift_grad, query_bias_grad, value_bias_grad, proj_bias_grad,
            mlp_gain_grad, mlp_shift_grad, down_bias_grad,
        ),
        up_bias_grad,
        rel_grad,
        jnp.broadcast_to(squares, (LANES,)),
    )
    small = paired(small, "core")
    backs, d_got, small = tie(backs, d_got, small)
    small = paired(small, "img")
    back_ring = sent_back(backs[0])
    d_parts = tie(*band_parts(added(kept(d_terms, 0, "yy", d_got))))
    d_got = over_bands(d_parts)
    u_got, p_got, d_parts = tie(u_got, p_got, d_parts)
    u_sum = added(kept(u_terms, 0, "img", u_got))
    p_sum = added(kept(p_terms, 0, "yy", p_got))
    part, cols = p_sum.shape[1], p_sum.shape[2]
    blocks = u_sum.shape[-1] // cols
    u_parts = tie(*band_parts(jnp.concatenate([u_sum, p_sum], axis=-1)))
    u_got = over_bands(u_parts)
    qa_got, qb_got, u_parts, small = tie(qa_got, qb_got, u_parts, small)
    small = paired(small, "yy")
    qa_terms = kept(qa_terms, 0, "img", qa_got)
    qb_terms = kept(qb_terms, 1, "yy", qb_got)
    qa_out, qb_out = tie(to_send(qa_terms, 0, "yy"), to_send(qb_terms, 0, "img"))
    qa_got = sent(qa_out, "yy")
    qb_got = sent(qb_out, "img")
    back_ring, qa_out = tie(back_ring, qa_out)
    own_rows = band_rows_of(backs[1], back_ring)
    back_got = exchanged(own_rows)
    qa_got, qb_got, own_rows = tie(qa_got, qb_got, own_rows)
    q_parts = tie(
        *band_parts(
            jnp.concatenate(
                [added(kept(qa_terms, 0, "yy", qa_got)), added(kept(qb_terms, 0, "img", qb_got))],
                axis=0,
            )
        )
    )
    q_got = over_bands(q_parts)
    d_got, q_parts, small = tie(d_got, q_parts, small)
    d_sum = added([d_parts[0]] + d_got)
    d_all = to_bands(d_sum)
    small = paired(small, 1)
    u_got, d_sum = tie(u_got, d_sum)
    u_sum = added([u_parts[0]] + u_got)
    u_all = to_bands(u_sum)
    back_got, u_sum = tie(back_got, u_sum)
    block_out, images_grad = unpacked(back_got, images.shape[2], (BF, F32))
    d_all, block_out, small = tie(d_all, block_out, small)
    small = paired(small, 2)
    d_own = jnp.stack([d_sum] + d_all)
    d_beside, d_other = swapped(d_own, "yy"), swapped(d_own, "core")
    q_got, d_own = tie(q_got, d_own)
    q_sum = added([q_parts[0]] + q_got)
    q_all = to_bands(q_sum)
    d_beside, d_other, u_all, q_sum = tie(d_beside, d_other, u_all, q_sum)
    u_own = jnp.stack([u_sum] + u_all)
    u_beside, u_other = swapped(u_own, "yy"), swapped(u_own, "core")
    d_last = swapped(d_beside, "core")
    u_own, d_last, small = tie(u_own, d_last, small)
    *sums, squares = small_unpacked(small, 8, up_bias.shape[0])
    squares, d_last = tie(squares, d_last)
    (down_grad,) = final(marks, d_own, d_other, d_beside, d_last, ((d_own.shape[1], 0, 1),))
    q_all, down_grad = tie(q_all, down_grad)
    q_own = jnp.stack([q_sum] + q_all)
    q_beside, q_other = swapped(q_own, "yy"), swapped(q_own, "core")
    u_beside, q_own = tie(u_beside, q_own)
    u_last = swapped(u_beside, "core")
    up_grad, proj_grad = final(
        marks, u_own, u_other, u_beside, u_last, ((part, 0, blocks), (part, blocks, 1))
    )
    q_beside, up_grad = tie(q_beside, up_grad)
    q_last = swapped(q_beside, "core")
    (qkv_grad,) = final(marks, q_own, q_other, q_beside, q_last, ((q_own.shape[1], 0, 1),))
    distill_loss = squares[0] / (count_total * width)
    return (
        block_out[None], distill_loss, images_grad[None], sums[0], sums[1], qkv_grad, sums[2], sums[3],
        sums[9], sums[10], proj_grad, sums[4], sums[5], sums[6], up_grad, sums[8], down_grad, sums[7],
    )


def solution(mesh):
    shape = dict(mesh.shape)
    fine = Mesh(
        mesh.devices.reshape(shape["img"], shape["tok"], shape["seq"] // 2, 2), EVERY
    )
    tokens = P("img", ("tok",) + SEQ, None, None)
    mask = P("img", ("tok",) + SEQ, None)
    split, whole = P("img", None), P()
    return jax.shard_map(
        local,
        mesh=fine,
        in_specs=(
            tokens, tokens, mask, tokens, whole, whole, split, whole, whole, whole, whole, split,
            whole, whole, whole, split, whole, split, whole,
        ),
        out_specs=(
            tokens, whole, tokens, whole, whole, split, whole, whole, whole, whole, split, whole,
            whole, whole, split, whole, split, whole,
        ),
        check_vma=False,
    )
```

```python
import functools

import jax
import jax.numpy as jnp
import numpy as np
from jax import lax
from jax.experimental import pallas as pl
from jax.experimental.pallas import tpu as pltpu
from jax.sharding import Mesh
from jax.sharding import PartitionSpec as P

HD = 64
WIN = 14
SLOT = 16
EDGE = 8
EPS = 1e-06
KEYS = 256
LANES = 128
FAR = 128.0
BF = jnp.bfloat16
F32 = jnp.float32
SEQ = ("yy", "core")
EVERY = ("img", "tok", "yy", "core")


def swapped(block, axis):
    size = lax.axis_size(axis)
    return lax.ppermute(block, axis, [(i, size - 1 - i) for i in range(size)])


def moved(block, axis, pairs):
    return lax.ppermute(block, axis, pairs)


def pick(pair_low, pair_high, flag):
    return jnp.where(flag == 0, pair_low, pair_high)


def tie(*values):
    return lax.optimization_barrier(values)


def layout_marks(band, place):
    first, last = band == 0, band == lax.axis_size("tok") - 1
    turned = (first & (place == 0)) | (last & (place > 0))
    corner = first & (place == 2)
    edge = turned | jnp.where(first, place == 1, place == 0)
    start = 8 - 2 * band
    real = jnp.where(edge, WIN * EDGE, jnp.where(corner, EDGE * EDGE, 0))
    return (
        start, jnp.where(corner, 0, start), turned.astype(jnp.int32), real, first.astype(jnp.int32),
        band, lax.axis_index("yy"), lax.axis_index("core"),
    )


def whole_spec(shape):
    return pl.BlockSpec(shape, lambda *_: (0,) * len(shape))


def column_picks(ways, cols):
    out = np.zeros((ways, SLOT + EDGE, cols), np.float32)
    for s in range(ways):
        for j in range(SLOT):
            out[s, j, WIN * s + j] = 1.0
        for j in range(EDGE):
            out[s, SLOT + j, WIN * ways + j] = 1.0
    return out


def turn_picks():
    out = np.zeros((WIN * EDGE, EDGE * (SLOT + EDGE)), np.float32)
    for i in range(WIN):
        for j in range(EDGE):
            out[i * EDGE + j, j * (SLOT + EDGE) + i] = 1.0
    return out


def pack_kernel(picks, block, out):
    ways, full = out.shape[0], SLOT + EDGE
    for r in range(block.shape[1]):
        both = jnp.dot(picks[...], block[0, r], preferred_element_type=F32)
        for s in range(ways):
            out[s, 0, r] = both[s * full : (s + 1) * full].astype(BF)


def packed(block):
    count, rows, cols, width = block.shape
    ways = lax.axis_size("yy") * lax.axis_size("core")
    full = SLOT + EDGE
    picks = jnp.asarray(column_picks(ways, cols).reshape(ways * full, cols), BF)
    return pl.pallas_call(
        pack_kernel,
        grid=(count,),
        in_specs=[
            whole_spec(picks.shape),
            pl.BlockSpec((1, rows, cols, width), lambda n: (n, 0, 0, 0)),
        ],
        out_specs=pl.BlockSpec((ways, 1, rows, full, width), lambda n: (0, n, 0, 0, 0)),
        out_shape=jax.ShapeDtypeStruct((ways, count, rows, full, width), BF),
        cost_estimate=pl.CostEstimate(flops=0, bytes_accessed=0, transcendentals=0),
        name="pack",
    )(picks, block)


def window_kernel(at, got, ring, turn, out):
    count, rows = got.shape[1], got.shape[2]
    start_a, start_e, turned, first = at[0], at[1], at[2], at[4]
    for n in range(count):

        def row_of(row, cols):
            own = jnp.maximum(row - 8, 0)
            before = ring[n, jnp.minimum(row, 7), cols].astype(F32)
            return jnp.where(row < 8, before, got[own // rows, n, own % rows, cols].astype(F32))

        for i in range(WIN):
            full = row_of(start_a + i, slice(0, SLOT))
            out[n, i * SLOT : (i + 1) * SLOT] = full.astype(BF)
        edge = jnp.concatenate(
            [row_of(start_e + i, slice(SLOT, SLOT + EDGE)) for i in range(WIN)], axis=0
        )
        tail = jnp.concatenate(
            [
                jnp.where(first == 1, ring[n, k], got[2 + k // rows, n, k % rows]).astype(F32)
                for k in range(EDGE)
            ],
            axis=0,
        ).astype(BF)
        bottom = jnp.dot(turn[...], tail, preferred_element_type=F32)
        out[n, WIN * SLOT :] = jnp.where(turned == 1, bottom, edge).astype(BF)


def window_norm_kernel(at, got, ring, turn, gain, shift, out, low):
    window_kernel(at, got, ring, turn, out)
    for start, size in ((0, WIN * SLOT), (WIN * SLOT, WIN * EDGE)):
        unit, _ = norm_parts(out[0, start : start + size].astype(F32))
        row = lax.broadcasted_iota(jnp.int32, (size, 1), 0)
        real = (row & (SLOT - 1)) < WIN if start == 0 else row < at[3]
        low[start : start + size] = jnp.where(real, unit * gain[...] + shift[...], 0.0).astype(BF)


def ring_rows(got, step):
    bands = lax.axis_size("tok")
    send = jnp.moveaxis(got[2:], 1, 0)
    send = send.reshape(send.shape[0], 8, SLOT + EDGE, send.shape[-1])
    return moved(send, "tok", [(i, (i + step) % bands) for i in range(bands)])


def windowed(got, ring, marks, norm=None):
    count, width = got.shape[1], got.shape[-1]
    tokens = WIN * (SLOT + EDGE)
    specs = [
        whole_spec(got.shape),
        whole_spec(ring.shape),
        whole_spec((WIN * EDGE, EDGE * (SLOT + EDGE))),
    ]
    out_specs = [whole_spec((count, tokens, width))]
    out_shape = [jax.ShapeDtypeStruct((count, tokens, width), BF)]
    if norm is not None:
        specs += [whole_spec((width,))] * 2
        out_specs.append(whole_spec((tokens, width)))
        out_shape.append(jax.ShapeDtypeStruct((tokens, width), BF))
    return pl.pallas_call(
        window_kernel if norm is None else window_norm_kernel,
        grid_spec=pltpu.PrefetchScalarGridSpec(
            num_scalar_prefetch=1, grid=(1,), in_specs=specs, out_specs=out_specs
        ),
        out_shape=out_shape,
        cost_estimate=pl.CostEstimate(flops=0, bytes_accessed=0, transcendentals=0),
        name="window",
    )(marks, got, ring, jnp.asarray(turn_picks(), BF), *(norm or ()))


def unwindow(at, flats, turn, up, mid):
    start_a, start_e, turned, first = at[0], at[1], at[2], at[4]
    full = SLOT + EDGE
    for n, flat in enumerate(flats):
        bottom = lax.dot_general(
            turn[...],
            flat[WIN * SLOT :].astype(BF),
            (((0,), (0,)), ((), ())),
            preferred_element_type=F32,
        )
        for row in range(24):
            i = row - start_e
            held = (i >= 0) & (i < WIN) & (turned == 0)
            at_row = pl.multiple_of(WIN * SLOT + EDGE * jnp.clip(i, 0, WIN - 1), EDGE)
            right = jnp.where(held, flat[pl.ds(at_row, EDGE)], 0.0)
            i = row - start_a
            at_row = pl.multiple_of(SLOT * jnp.clip(i, 0, WIN - 1), SLOT)
            left = jnp.where((i >= 0) & (i < WIN), flat[pl.ds(at_row, SLOT)], 0.0)
            if row < 8 or row >= 16:
                base = row % 8 * full
                here = (turned == 1) & (first == (1 if row < 8 else 0))
                left = jnp.where(here, bottom[base : base + SLOT], left)
            both = jnp.concatenate([left, right], axis=0).astype(BF)
            if row < 8:
                up[n, row] = both
            else:
                mid[n, row - 8] = both


def unpack_kernel(picks, got, *outs):
    for n, out in enumerate(outs):
        for r in range(got.shape[2]):
            total = None
            for s in range(got.shape[0]):
                part = lax.dot_general(
                    picks[s], got[s, n, r], (((0,), (0,)), ((), ())), preferred_element_type=F32
                )
                total = part if total is None else total + part
            out[r] = total.astype(out.dtype)


def unpacked(got, cols, dtypes):
    ways, count, rows, full, width = got.shape
    picks = column_picks(ways, cols)
    picks[:, WIN:SLOT] = 0.0
    return pl.pallas_call(
        unpack_kernel,
        in_specs=[whole_spec(picks.shape), whole_spec(got.shape)],
        out_specs=[whole_spec((rows, cols, width))] * count,
        grid=(1,),
        out_shape=[jax.ShapeDtypeStruct((rows, cols, width), dtype) for dtype in dtypes],
        cost_estimate=pl.CostEstimate(flops=0, bytes_accessed=0, transcendentals=0),
        name="unpack",
    )(jnp.asarray(picks, BF), got)


def exchanged(send):
    return lax.all_to_all(send, SEQ, split_axis=0, concat_axis=0, tiled=True)


def sent_back(up):
    bands = lax.axis_size("tok")
    return moved(up, "tok", [((i + 1) % bands, i) for i in range(bands)])


def band_rows_of(mid, ring):
    own = mid + jnp.pad(ring, ((0, 0), (8, 0), (0, 0), (0, 0)))
    ways = lax.axis_size("yy") * lax.axis_size("core")
    own = own.reshape(own.shape[0], ways, 16 // ways, SLOT + EDGE, own.shape[-1])
    return jnp.swapaxes(own, 0, 1)


def two_images():
    return lax.axis_size("img") == 2


def quarter(shard):
    if not two_images():
        return shard
    rows = shard.shape[0] // 4
    at = lax.axis_index("yy") * 2 + lax.axis_index("core")
    return lax.dynamic_slice_in_dim(shard, at * rows, rows, 0)


def half_of(shard, chunks=1):
    if not two_images():
        return [shard]
    rows = shard.shape[0] // (2 * chunks)
    first = lax.axis_index("core") * rows * chunks
    return [lax.dynamic_slice_in_dim(shard, first + i * rows, rows, 0) for i in range(chunks)]


def over_images(block):
    if two_images():
        return swapped(block, "img")
    return lax.all_gather(block, "img", axis=0, tiled=True)


def half_over_cores(block):
    return (block, swapped(block, "core")) if two_images() else block


def assembled_halves(shard, *parts):
    if not two_images():
        return parts[0]
    core, image = lax.axis_index("core"), lax.axis_index("img")
    other = jnp.concatenate(
        [pick(here, there, core) for here, there in parts]
        + [pick(there, here, core) for here, there in parts],
        axis=0,
    )
    return jnp.concatenate([pick(shard, other, image), pick(other, shard, image)], axis=0)


def over_cores(block):
    return swapped(block, "core") if two_images() else block


def gather_over_rows(block):
    return swapped(block, "yy") if two_images() else block


def assembled(shard, first, second, first_across, second_across):
    if not two_images():
        return first
    core, high, image = (lax.axis_index(a) for a in ("core", "yy", "img"))
    rows = []
    for a, b, c, d in ((first, second, first_across, second_across), (second, first, second_across, first_across)):
        here, there = pick(a, b, high), pick(c, d, high)
        rows += [pick(here, there, core), pick(there, here, core)]
    other = jnp.concatenate(rows, axis=0)
    return jnp.concatenate([pick(shard, other, image), pick(other, shard, image)], axis=0)


def part_of(terms, dim, axis, other):
    index = lax.axis_index(axis)
    index = 1 - index if other else index
    return [lax.dynamic_index_in_dim(t, index, dim, keepdims=False) for t in terms]


def added(terms):
    total = terms[0].astype(F32)
    for t in terms[1:]:
        total = total + t.astype(F32)
    return total.astype(BF)


def to_send(terms, dim, axis):
    if lax.axis_size(axis) != 2:
        return jnp.moveaxis(added(terms), dim, 0)
    return added(part_of(terms, dim, axis, True))


def sent(block, axis):
    if lax.axis_size(axis) != 2:
        return lax.all_to_all(block, axis, split_axis=0, concat_axis=0, tiled=True)
    return swapped(block, axis)


def kept(terms, dim, axis, got):
    if lax.axis_size(axis) != 2:
        return [got[i] for i in range(got.shape[0])]
    return part_of(terms, dim, axis, False) + [got]


def split_grad(left, right):
    images, bands = lax.axis_size("img"), lax.axis_size("tok")
    core = lax.axis_index("core")
    rows, cols = left.shape[1], right.shape[1] // 2
    shape = (images, 2, bands, rows // images // 2 // bands, cols)

    def one(index):
        half = lax.dynamic_slice_in_dim(right, index * cols, cols, 1)
        return mm_tn(left, half).astype(BF).reshape(shape)

    return one(1 - core), one(core)


def crossed(block, distance):
    size = lax.axis_size("tok")
    return lax.ppermute(block, "tok", [(i, i ^ distance) for i in range(size)])


def by_bits(block):
    return block.reshape((2, 2) + block.shape[1:])


def bit_of(terms, dim, bit, other):
    index = (lax.axis_index("tok") >> bit) & 1
    index = 1 - index if other else index
    return [lax.dynamic_index_in_dim(t, index, dim, keepdims=False) for t in terms]


def low_send(terms):
    return added(bit_of(terms, 1, 0, True))


def high_send(terms):
    return added(bit_of(terms, 0, 1, True))


def after_low(terms, got):
    return bit_of(terms, 1, 0, False) + [got]


def after_high(terms, got):
    return added(bit_of(terms, 0, 1, False) + [got])


def final_kernel(splits, unit, at, near_own, near_other, far_own, far_other, *outs):
    band, core = at[5], at[7]

    def write(own, other):
        for t in range(own.shape[0]):
            to = ((t >> 1) | ((t & 1) << 1)) ^ band
            for (rows, first, blocks), out in zip(splits, outs):
                size = blocks * unit
                a = own[t, :, first * unit : first * unit + size].astype(F32)
                b = other[t, :, first * unit : first * unit + size].astype(F32)
                out[0, to, :, :size] = jnp.where(core == 0, a, b)
                out[0, to, :, size:] = jnp.where(core == 0, b, a)

    @pl.when(pl.program_id(0) == 0)
    def near():
        write(near_own, near_other)

    @pl.when(pl.program_id(0) == 1)
    def far():
        write(far_own, far_other)


def final(marks, own, other_core, beside, beside_other_core, splits):
    bands, rows, cols = own.shape
    unit = cols // sum(blocks for _, _, blocks in splits)
    outs = pl.pallas_call(
        functools.partial(final_kernel, splits, unit),
        grid_spec=pltpu.PrefetchScalarGridSpec(
            num_scalar_prefetch=1,
            grid=(2,),
            in_specs=[whole_spec(own.shape)] * 4,
            out_specs=[
                pl.BlockSpec((1, bands, n, 2 * blocks * unit), lambda y, at: (y ^ at[6], 0, 0, 0))
                for n, _, blocks in splits
            ],
        ),
        out_shape=[
            jax.ShapeDtypeStruct((2, bands, n, 2 * blocks * unit), F32) for n, _, blocks in splits
        ],
        cost_estimate=pl.CostEstimate(flops=0, bytes_accessed=0, transcendentals=0),
        name="final",
    )(marks, own, other_core, beside, beside_other_core)
    return [o.reshape(-1, o.shape[-1]) for o in outs]


def paired(value, axis):
    if axis == "img" and not two_images():
        return lax.psum(value, "img")
    across = crossed(value, axis) if isinstance(axis, int) else swapped(value, axis)
    return value + across


def small_pack_kernel(*refs):
    vectors, up_bias, tables, squares, out = refs[:8], refs[8], refs[9], refs[10], refs[11]
    width = out.shape[1]
    for i, vector in enumerate(vectors):
        out[i, :] = vector[...]
    row = len(vectors)
    for i in range(up_bias.shape[0] // width):
        out[row, :] = up_bias[i * width : (i + 1) * width]
        row += 1
    fit = width // LANES
    for m in range(2 * WIN - 1):
        at = (m % fit) * LANES
        out[row + m // fit, at : at + LANES] = tables[m, :]
    row += -(-(2 * WIN - 1) // fit)
    out[row : row + 1, :LANES] = jnp.broadcast_to(squares[...], (1, LANES))


def small_packed(vectors, up_bias, tables, squares):
    width = vectors[0].shape[0]
    rows = len(vectors) + up_bias.shape[0] // width - (-(2 * WIN - 1) // (width // LANES)) + 1
    args = (*vectors, up_bias, tables, squares)
    return pl.pallas_call(
        small_pack_kernel,
        grid=(1,),
        in_specs=[whole_spec(a.shape) for a in args],
        out_specs=whole_spec((rows, width)),
        out_shape=jax.ShapeDtypeStruct((rows, width), F32),
        cost_estimate=pl.CostEstimate(flops=0, bytes_accessed=0, transcendentals=0),
        name="small_pack",
    )(*args)


def small_unpack_kernel(packed, *outs):
    vectors, up_bias, rows_out, cols_out, squares = outs[:8], outs[8], outs[9], outs[10], outs[11]
    width = packed.shape[1]
    for i, vector in enumerate(vectors):
        vector[...] = packed[i, :]
    row = len(vectors)
    for i in range(up_bias.shape[0] // width):
        up_bias[i * width : (i + 1) * width] = packed[row, :]
        row += 1
    fit = width // LANES
    for m in range(2 * WIN - 1):
        at = (m % fit) * LANES
        both = packed[row + m // fit : row + m // fit + 1, at : at + LANES]
        rows_out[m : m + 1, :] = both[:, :HD]
        cols_out[m : m + 1, :] = pltpu.roll(both, HD, 1)[:, :HD]
    row += -(-(2 * WIN - 1) // fit)
    squares[...] = packed[row, :LANES]


def small_unpacked(packed, vectors, up_width):
    width = packed.shape[1]
    table = (2 * WIN - 1, HD)
    shapes = [(width,)] * vectors + [(up_width,), table, table, (LANES,)]
    return pl.pallas_call(
        small_unpack_kernel,
        grid=(1,),
        in_specs=[whole_spec(packed.shape)],
        out_specs=[whole_spec(shape) for shape in shapes],
        out_shape=[jax.ShapeDtypeStruct(shape, F32) for shape in shapes],
        cost_estimate=pl.CostEstimate(flops=0, bytes_accessed=0, transcendentals=0),
        name="small_unpack",
    )(packed)


def rolled(block, amount):
    return pltpu.roll(block, amount, 1, stride=1, stride_axis=0)


def rel_places():
    size = 2 * WIN - 1
    out = np.zeros((4, LANES, size), np.float32)
    for m in range(size):
        out[0, size - 1 - m, m] = 1.0
        out[1, 32 + size - 1 - m, m] = 1.0
        out[2, m, m] = 1.0
        out[3, 64 + m, m] = 1.0
    return out


def head_places():
    out = np.zeros((2, HD, LANES), np.float32)
    for c in range(HD):
        out[0, c, c] = 1.0
        out[1, c, HD + c] = 1.0
    return out


def build_rel(tables, places, heads, out):
    for half in (0, 1):
        total = None
        for table, place in zip(tables, places):
            high = table.astype(BF)
            value = (table - high.astype(F32)).astype(BF) if half else high
            part = jnp.dot(place, value, preferred_element_type=F32)
            total = part if total is None else total + part
        for head in (0, 1):
            lanes = jnp.dot(total.astype(BF), heads[head], preferred_element_type=F32)
            out[head, :, half * LANES : (half + 1) * LANES] = lanes.astype(BF)


def build_both(at, rows, cols, places, heads, rel_a, rel_b):
    @pl.when(pl.program_id(0) == 0)
    def build():
        turned = at[2] == 1
        build_rel((rows[...], cols[...]), places, heads, rel_a)
        first = jnp.where(turned, cols[...], rows[...])
        second = jnp.where(turned, rows[...], cols[...])
        build_rel((first, second), places, heads, rel_b)


def rel_terms(q, rel):
    return lax.dot_general(
        jnp.concatenate([q, q], axis=1), rel, (((1,), (1,)), ((), ())), preferred_element_type=F32
    )


def wide_queries(q, terms, group):
    m = q.shape[0]
    lane = lax.broadcasted_iota(jnp.int32, (group, LANES), 1)
    blocks = []
    for i in range(WIN):
        t = terms[i * group : (i + 1) * group]
        by_row = pltpu.roll(t, (LANES - (WIN - 1) + i) % LANES, 1)
        by_col = rolled(t, 19)
        blocks.append(jnp.where(lane < 64, by_row, by_col))
    both = jnp.concatenate(blocks, axis=0)
    high = both.astype(BF).astype(F32)
    low = pltpu.roll(both - high, 32, 1)
    lane = lax.broadcasted_iota(jnp.int32, (m, LANES), 1)
    mixed = jnp.where((lane & 63) < 32, high, low)
    mixed = jnp.where(lane == LANES - 1, 1.0, mixed)
    return jnp.concatenate([q * BF(HD**-0.5), mixed.astype(BF)], axis=1)


def full_keys(k, v, v_pad):
    n = k.shape[0]
    zeros = jnp.zeros((KEYS - n, LANES), BF)
    if v_pad is None:
        return jnp.concatenate([k, zeros], axis=0), jnp.concatenate([v, zeros], axis=0)
    fill = jnp.broadcast_to(v_pad, (KEYS - n, LANES)).astype(BF)
    return jnp.concatenate([k, zeros], axis=0), jnp.concatenate([v, fill], axis=0)


def only(block, head):
    lane = lax.broadcasted_iota(jnp.int32, block.shape, 1)
    return jnp.where((lane < HD) == (head == 0), block, jnp.zeros_like(block))


def scored(wide, keys, hot, head):
    return lax.dot_general(
        wide,
        jnp.concatenate([only(keys, head), hot], axis=1),
        (((1,), (1,)), ((), ())),
        preferred_element_type=F32,
    )


def softmax_low(scores):
    e = jnp.exp(scores - jnp.max(scores, axis=1, keepdims=True))
    return (e * (1.0 / jnp.sum(e, axis=1, keepdims=True))).astype(BF)


def attend_kernel(
    at, q, k, v, v_pad, rows, cols, places, heads, hot_a, hot_b, out, probs_a, probs_b, rel_a, rel_b
):
    build_both(at, rows, cols, (places[0], places[1]), heads, rel_a, rel_b)
    n = WIN * SLOT
    pad = v_pad[...].astype(BF)
    slots = (
        (slice(0, n), None, rel_a, hot_a, SLOT, probs_a),
        (slice(n, n + WIN * EDGE), pad, rel_b, hot_b, EDGE, probs_b),
    )
    both = [(s, h) for s in (0, 1) for h in (0, 1)]
    queries = [q[slot[0]] for slot in slots]
    terms = [
        rel_terms(queries[i], slots[i][2][...].reshape(2 * LANES, 2 * LANES)) for i in (0, 1)
    ]
    filled = [full_keys(k[slot[0]], v[slot[0]], slot[1]) for slot in slots]
    wide = [
        wide_queries(queries[i], terms[i][:, h * LANES : (h + 1) * LANES], slots[i][4])
        for i, h in both
    ]
    scores = [scored(w, filled[i][0], slots[i][3][...], h) for w, (i, h) in zip(wide, both)]
    probs = [softmax_low(x) for x in scores]
    for p, (i, h) in zip(probs, both):
        slots[i][5][h] = p
    parts = [
        jnp.dot(p, only(filled[i][1], h), preferred_element_type=F32)
        for p, (i, h) in zip(probs, both)
    ]
    for i in (0, 1):
        out[slots[i][0]] = (parts[2 * i] + parts[2 * i + 1]).astype(BF)


def back_terms(both, group):
    lane = lax.broadcasted_iota(jnp.int32, (group, LANES), 1)
    blocks = []
    for i in range(WIN):
        t = both[i * group : (i + 1) * group, LANES:]
        by_row = jnp.where(lane < WIN, t, 0.0)
        by_row = pltpu.roll(by_row, i, 1) if i else by_row
        by_col = rolled(jnp.where((lane >= 64) & (lane < 64 + WIN), t, 0.0), 0)
        blocks.append(by_row + by_col)
    terms = jnp.concatenate(blocks, axis=0)
    high = terms.astype(BF)
    return jnp.concatenate([high, (terms - high.astype(F32)).astype(BF)], axis=1)


def over_rows(left, right):
    return lax.dot_general(left, right, (((0,), (0,)), ((), ())), preferred_element_type=F32)


def attend_back_kernel(
    at, q, k, v, v_pad, rows, cols, places, heads, hot_a, hot_b, grad, probs_a, probs_b,
    dqkv, pad_sum, rel_grad, rel_a, rel_b, acc_a, acc_b,
):
    step = pl.program_id(0)
    steps = dqkv.shape[1] // (3 * LANES)
    build_both(at, rows, cols, (places[2], places[3]), heads, rel_a, rel_b)

    @pl.when(step == 0)
    def clear():
        acc_a[...] = jnp.zeros_like(acc_a)
        acc_b[...] = jnp.zeros_like(acc_b)

    n = WIN * SLOT
    scale = HD**-0.5
    pad = v_pad[...].astype(BF)
    slots = (
        (slice(0, n), None, rel_a, hot_a, SLOT, probs_a, acc_a),
        (slice(n, n + WIN * EDGE), pad, rel_b, hot_b, EDGE, probs_b, acc_b),
    )
    both = [(s, h) for s in (0, 1) for h in (0, 1)]
    queries = [q[slot[0]] for slot in slots]
    grads = [grad[slot[0]] for slot in slots]
    filled = [full_keys(k[slot[0]], v[slot[0]], slot[1]) for slot in slots]
    probs_grad = [
        lax.dot_general(
            grads[i], only(filled[i][1], h), (((1,), (1,)), ((), ())), preferred_element_type=F32
        )
        for i, h in both
    ]
    dvs = [over_rows(slots[i][5][h], grads[i]) for i, h in both]
    scores_grad = []
    for dp, (i, h) in zip(probs_grad, both):
        wide = slots[i][5][h].astype(F32)
        inner = jnp.sum(wide * dp, axis=1, keepdims=True)
        scores_grad.append((wide * (dp - inner)).astype(BF))
    sums = [
        jnp.dot(
            ds,
            jnp.concatenate([only(filled[i][0], h), slots[i][3][...]], axis=1),
            preferred_element_type=F32,
        )
        for ds, (i, h) in zip(scores_grad, both)
    ]
    dks = [over_rows(ds, queries[i]) * scale for ds, (i, h) in zip(scores_grad, both)]
    split = [back_terms(x, slots[i][4]) for x, (i, h) in zip(sums, both)]
    parts = []
    for x, t, (i, h) in zip(sums, split, both):
        rel = slots[i][2][h]
        part = x[:, :LANES] * scale + jnp.dot(
            t,
            jnp.concatenate([rel[:, :LANES], rel[:, :LANES]], axis=0),
            preferred_element_type=F32,
        )
        parts.append(part + jnp.dot(t[:, :LANES], rel[:, LANES:], preferred_element_type=F32))
    for t, (i, h) in zip(split, both):
        slots[i][6][h] += over_rows(t, queries[i])
    lane = lax.broadcasted_iota(jnp.int32, (KEYS, LANES), 1)
    for i in (0, 1):
        here, size = slots[i][0], queries[i].shape[0]
        dk = jnp.where(lane < HD, dks[2 * i], dks[2 * i + 1]).astype(BF)
        dv = jnp.where(lane < HD, dvs[2 * i], dvs[2 * i + 1]).astype(BF)
        found = ((parts[2 * i] + parts[2 * i + 1]).astype(BF), dk[:size], dv[:size])
        for j, value in enumerate(found):
            to = pl.ds(pl.multiple_of((j * steps + step) * LANES, LANES), LANES)
            dqkv[here, to] = value
    pad_sum[...] = jnp.sum(dv[WIN * EDGE :].astype(F32), axis=0, keepdims=True)

    @pl.when(step == steps - 1)
    def tables():
        def table(acc):
            even = acc[0, :LANES] + acc[0, LANES:]
            odd = acc[1, :LANES] + acc[1, LANES:]
            return even + pltpu.roll(odd, HD, 1)

        a, b = table(acc_a), table(acc_b)
        turned = at[2] == 1
        low, high = slice(0, 32), slice(64, 96)
        rows_grad = a[low] + jnp.where(turned, b[high], b[low])
        cols_grad = a[high] + jnp.where(turned, b[low], b[high])
        lane = lax.broadcasted_iota(jnp.int32, (32, LANES), 1)
        rel_grad[...] = jnp.where(lane < HD, rows_grad, pltpu.roll(cols_grad, HD, 1))


def hot_tables():
    def table(place):
        out = np.zeros((2, KEYS, LANES), np.float32)
        for key in range(KEYS):
            at = place(key)
            if at is None:
                out[0, key, LANES - 1] = -1e30
            else:
                for base, index in ((0, at[0]), (32, at[0]), (64, at[1]), (96, at[1])):
                    out[0, key, base + index] = 1.0
                out[1, key, WIN - 1 - at[0]] = 1.0
                out[1, key, 64 + WIN - 1 - at[1]] = 1.0
        return out

    def whole(key):
        i, j = divmod(key, SLOT)
        return (i, j) if i < WIN and j < WIN else None

    def partial(key):
        if key < WIN * EDGE:
            return divmod(key, EDGE)
        i, j = divmod(key - WIN * EDGE, EDGE)
        return (i, EDGE + j) if i < WIN and EDGE + j < WIN else None

    return table(whole), table(partial)


def attention(qkv, v_pad, rel_rows, rel_cols, marks):
    tokens_a, tokens_b = WIN * SLOT, WIN * EDGE
    tokens, width = qkv.shape[0], qkv.shape[1] // 3
    pairs = width // LANES
    table = (2 * WIN - 1, HD)
    hots = [jnp.asarray(t, BF) for t in hot_tables()]
    places, heads = jnp.asarray(rel_places(), BF), jnp.asarray(head_places(), BF)

    def cols(n, base):
        return pl.BlockSpec((n, LANES), lambda p, at: (0, base * pairs + p))

    specs = [cols(tokens, i) for i in range(3)] + [
        pl.BlockSpec((LANES,), lambda p, at: (p,)),
        whole_spec(table),
        whole_spec(table),
        whole_spec(places.shape),
        whole_spec(heads.shape),
        whole_spec((KEYS, LANES)),
        whole_spec((KEYS, LANES)),
    ]
    probs_specs = [
        pl.BlockSpec((2, tokens_a, KEYS), lambda p, at: (p, 0, 0)),
        pl.BlockSpec((2, tokens_b, KEYS), lambda p, at: (p, 0, 0)),
    ]
    rel_scratch = [pltpu.VMEM((2, LANES, 2 * LANES), BF)] * 2
    shared = (marks, qkv, qkv, qkv, v_pad, rel_rows, rel_cols, places, heads)
    out, probs_a, probs_b = pl.pallas_call(
        attend_kernel,
        grid_spec=pltpu.PrefetchScalarGridSpec(
            num_scalar_prefetch=1,
            grid=(pairs,),
            in_specs=specs,
            out_specs=[cols(tokens, 0)] + probs_specs,
            scratch_shapes=rel_scratch,
        ),
        out_shape=[
            jax.ShapeDtypeStruct((tokens, width), BF),
            jax.ShapeDtypeStruct((2 * pairs, tokens_a, KEYS), BF),
            jax.ShapeDtypeStruct((2 * pairs, tokens_b, KEYS), BF),
        ],
        cost_estimate=pl.CostEstimate(flops=0, bytes_accessed=0, transcendentals=0),
        name="attend",
    )(*shared, hots[0][0], hots[1][0])

    def back(grad):
        return pl.pallas_call(
            attend_back_kernel,
            grid_spec=pltpu.PrefetchScalarGridSpec(
                num_scalar_prefetch=1,
                grid=(pairs,),
                in_specs=specs + [cols(tokens, 0)] + probs_specs,
                out_specs=[
                    whole_spec((tokens, 3 * width)),
                    cols(1, 0),
                    whole_spec((32, LANES)),
                ],
                scratch_shapes=rel_scratch + [pltpu.VMEM((2, 2 * LANES, LANES), F32)] * 2,
            ),
            out_shape=[
                jax.ShapeDtypeStruct((tokens, 3 * width), BF),
                jax.ShapeDtypeStruct((1, width), F32),
                jax.ShapeDtypeStruct((32, LANES), F32),
            ],
            cost_estimate=pl.CostEstimate(flops=0, bytes_accessed=0, transcendentals=0),
            name="attend_back",
        )(*shared, hots[0][1], hots[1][1], grad, probs_a, probs_b)

    return out, back


def norm_parts(values):
    centre = jnp.mean(values, axis=-1, keepdims=True)
    centred = values - centre
    spread = jnp.mean(centred * centred, axis=-1, keepdims=True)
    scale = lax.rsqrt(spread + EPS)
    return centred * scale, scale


def norm_back(grad, unit, scale, gain):
    g = grad * gain
    mean = jnp.mean(g, axis=-1, keepdims=True)
    along = jnp.mean(g * unit, axis=-1, keepdims=True)
    return scale * (g - mean - unit * along)


def mlp_back_kernel(
    pre, up, resid, result_grad, gain, proj, resid_grad, proj_in, attended_grad, gain_grad, shift_grad,
    proj_bias_grad, up_bias_grad, total,
):
    step = pl.program_id(0)
    part = mm_nt(pre[...], up[...])
    up_bias_grad[...] = jnp.sum(pre[...].astype(F32), axis=0)

    @pl.when(step == 0)
    def first():
        total[...] = part

    @pl.when(step > 0)
    def more():
        total[...] += part

    @pl.when(step == pl.num_programs(0) - 1)
    def last():
        grad = total[...]
        unit, scale = norm_parts(resid[...])
        gain_grad[...] = jnp.sum(grad * unit, axis=0)
        shift_grad[...] = jnp.sum(grad, axis=0)
        found = result_grad[...] + norm_back(grad, unit, scale, gain[...])
        resid_grad[...] = found
        low = found.astype(BF)
        proj_in[...] = low
        proj_bias_grad[...] = jnp.sum(low.astype(F32), axis=0)
        attended_grad[...] = mm_nt(low, proj[...]).astype(BF)


def mlp_back(pre_grad, up_full, resid, result_grad, gain, proj_full):
    tokens, hidden = pre_grad.shape
    width = resid.shape[1]
    size = 1024
    steps = hidden // size
    flat = jax.ShapeDtypeStruct((width,), F32)
    return pl.pallas_call(
        mlp_back_kernel,
        grid=(steps,),
        in_specs=[
            pl.BlockSpec((tokens, size), lambda k: (0, k)),
            pl.BlockSpec((width, size), lambda k: (0, k)),
            whole_spec(resid.shape),
            whole_spec(resid.shape),
            whole_spec((width,)),
            whole_spec(proj_full.shape),
        ],
        out_specs=[whole_spec(resid.shape)] * 3
        + [whole_spec((width,))] * 3
        + [pl.BlockSpec((size,), lambda k: (k,))],
        out_shape=[
            jax.ShapeDtypeStruct(resid.shape, F32),
            jax.ShapeDtypeStruct(resid.shape, BF),
            jax.ShapeDtypeStruct(resid.shape, BF),
            flat,
            flat,
            flat,
            jax.ShapeDtypeStruct((hidden,), F32),
        ],
        scratch_shapes=[pltpu.VMEM(resid.shape, F32)],
        cost_estimate=pl.CostEstimate(flops=0, bytes_accessed=0, transcendentals=0),
        name="mlp_back",
    )(pre_grad, up_full, resid, result_grad, gain, proj_full)


def input_back_kernel(
    at, dqkv, weight, low, resid_grad, gain, pad_sum, turn, up, mid, gain_grad, shift_grad,
    query_sum, value_sum, total,
):
    step = pl.program_id(0)
    part = mm_nt(dqkv[...], weight[...])
    sums = jnp.sum(dqkv[...].astype(F32), axis=0)

    @pl.when(step == 0)
    def first():
        total[...] = part
        query_sum[...] = sums

    @pl.when(step > 0)
    def more():
        total[...] += part

    @pl.when(step == pl.num_programs(0) - 1)
    def last():
        value_sum[...] = sums + pad_sum[0]
        row = lax.broadcasted_iota(jnp.int32, (total.shape[0], 1), 0)
        full = WIN * SLOT
        limit = jnp.where(row < full, row - (row & (SLOT - 1)) + WIN, full + at[3])
        real = row < limit
        grad = jnp.where(real, total[...], 0.0)
        unit, scale = norm_parts(low[...].astype(F32))
        gain_grad[...] = jnp.sum(grad * unit, axis=0)
        shift_grad[...] = jnp.sum(grad, axis=0)
        total[...] = resid_grad[...] + norm_back(grad, unit, scale, gain[...])
        unwindow(at, (total,), turn, up, mid)


def input_back(marks, dqkv, qkv_full, low, resid_grad, gain, pad_sum):
    tokens, width = low.shape
    full = SLOT + EDGE
    flat = jax.ShapeDtypeStruct((width,), F32)
    shapes = [(1, 8, full, width), (1, 16, full, width)]
    return pl.pallas_call(
        input_back_kernel,
        grid_spec=pltpu.PrefetchScalarGridSpec(
            num_scalar_prefetch=1,
            grid=(3,),
            in_specs=[
                pl.BlockSpec((tokens, width), lambda k, at: (0, k)),
                pl.BlockSpec((width, width), lambda k, at: (0, k)),
                whole_spec(low.shape),
                whole_spec(low.shape),
                whole_spec((width,)),
                whole_spec((1, width)),
                whole_spec((WIN * EDGE, EDGE * full)),
            ],
            out_specs=[whole_spec(shape) for shape in shapes] + [whole_spec((width,))] * 4,
            scratch_shapes=[pltpu.VMEM(low.shape, F32)],
        ),
        out_shape=[jax.ShapeDtypeStruct(shape, BF) for shape in shapes] + [flat] * 4,
        cost_estimate=pl.CostEstimate(flops=0, bytes_accessed=0, transcendentals=0),
        name="input_back",
    )(marks, dqkv, qkv_full, low, resid_grad, gain, pad_sum, jnp.asarray(turn_picks(), BF))


def result_rows_kernel(at, result, turn, up, mid, block):
    row = lax.broadcasted_iota(jnp.int32, (result.shape[0], 1), 0)
    full = WIN * SLOT
    limit = jnp.where(row < full, row - (row & (SLOT - 1)) + WIN, full + at[3])
    block[...] = jnp.where(row < limit, result[...], 0.0)
    unwindow(at, (block,), turn, up, mid)


def result_rows(marks, result):
    width, full = result.shape[1], SLOT + EDGE
    shapes = [(1, 8, full, width), (1, 16, full, width)]
    return pl.pallas_call(
        result_rows_kernel,
        grid_spec=pltpu.PrefetchScalarGridSpec(
            num_scalar_prefetch=1,
            grid=(1,),
            in_specs=[whole_spec(result.shape), whole_spec((WIN * EDGE, EDGE * full))],
            out_specs=[whole_spec(shape) for shape in shapes],
            scratch_shapes=[pltpu.VMEM(result.shape, F32)],
        ),
        out_shape=[jax.ShapeDtypeStruct(shape, BF) for shape in shapes],
        cost_estimate=pl.CostEstimate(flops=0, bytes_accessed=0, transcendentals=0),
        name="result_rows",
    )(marks, result, jnp.asarray(turn_picks(), BF))


def mm(a, b):
    return jnp.dot(a, b, preferred_element_type=F32)


def mm_nt(a, b):
    return lax.dot_general(a, b, (((1,), (1,)), ((), ())), preferred_element_type=F32)


def mm_tn(a, b):
    return lax.dot_general(a, b, (((0,), (0,)), ((), ())), preferred_element_type=F32)


def local(
    images, teacher, valid_mask, out_grad, attn_gain, attn_shift, qkv_weight, query_bias,
    value_bias, rel_rows, rel_cols, proj_weight, proj_bias, mlp_gain, mlp_shift, up_weight,
    up_bias, down_weight, down_bias,
):
    band = lax.axis_index("tok")
    bands = lax.axis_size("tok")
    place = lax.axis_index("yy") * lax.axis_size("core") + lax.axis_index("core")
    width = images.shape[-1]
    image_rows = images.shape[1] * bands * lax.axis_size("yy") * lax.axis_size("core")
    tokens_all = images.shape[0] * lax.axis_size("img") * image_rows * images.shape[2]

    marks = layout_marks(band, place)
    real_edge = marks[3]
    marks = jnp.stack(marks).astype(jnp.int32)
    x_got = exchanged(packed(images))
    qkv_1 = over_images(quarter(qkv_weight))
    proj_1 = [over_images(c) for c in half_of(proj_weight)]
    up_1 = [over_images(c) for c in half_of(up_weight)]
    down_1 = [over_images(c) for c in half_of(down_weight, 2)]
    count = jnp.broadcast_to(jnp.sum(valid_mask.astype(F32)), (8, LANES))
    count = paired(count, "img")
    x_got, qkv_1, marks, count = tie(x_got, qkv_1, marks, count)
    qkv_2 = gather_over_rows(qkv_1)
    x_ring = ring_rows(x_got, 1)
    qkv_3 = over_cores(qkv_1)
    count = paired(count, "core")
    marked = jnp.where(valid_mask[..., None] > 0, teacher, jnp.full_like(teacher, FAR))
    late_pack = packed(tie(jnp.concatenate([marked, out_grad], axis=0), qkv_1)[0])
    x_ring, x_got, late_pack, count = tie(x_ring, x_got, late_pack, count)
    x_low, tokens_low = windowed(x_got, x_ring, marks, (attn_gain, attn_shift))
    x_low = x_low[0]
    count = paired(count, "yy")
    qkv_2, x_low, tokens_low, qkv_3 = tie(qkv_2, x_low, tokens_low, qkv_3)
    qkv_4 = over_cores(qkv_2)
    late_got = exchanged(tie(late_pack, x_low)[0])
    qkv_4, proj_1[0], count, up_1[0] = tie(qkv_4, proj_1[0], count, up_1[0])
    up_2 = [half_over_cores(up_1[0])]
    proj_2 = half_over_cores(proj_1[0])
    count = paired(count, 1)

    row_a = lax.broadcasted_iota(jnp.int32, (WIN * SLOT, 1), 0)
    row_b = lax.broadcasted_iota(jnp.int32, (WIN * EDGE, 1), 0)
    real = jnp.concatenate(
        [(row_a & (SLOT - 1)) < WIN, row_b < real_edge], axis=0
    )
    inputs = x_low.astype(F32)
    qkv_bias = jnp.concatenate([query_bias, jnp.zeros_like(query_bias), value_bias])
    qkv_full = assembled(qkv_weight, qkv_1, qkv_2, qkv_3, qkv_4)
    qkv = (mm(tokens_low, qkv_full) + qkv_bias).astype(BF)
    proj_full = assembled_halves(proj_weight, proj_2)
    up_full = assembled_halves(up_weight, *up_2)
    qkv, late_got, proj_full, count, up_full, down_1[0] = tie(
        qkv, late_got, proj_full, count, up_full, down_1[0]
    )
    late_ring = ring_rows(late_got, 1)
    count = paired(count, 2)
    attended, attention_back = attention(qkv, value_bias, rel_rows, rel_cols, marks)
    down_2 = [half_over_cores(down_1[0])]
    attended, count, late_ring, down_1, down_2 = tie(attended, count, late_ring, down_1, down_2)
    resid = inputs + mm(attended, proj_full) + proj_bias
    unit2, scale2 = norm_parts(resid)
    normed2 = (unit2 * mlp_gain + mlp_shift).astype(BF)
    down_2 = down_2 + [half_over_cores(c) for c in down_1[1:]]
    hidden_pre = mm(normed2, up_full) + up_bias
    cdf = 0.5 * (1.0 + lax.erf(hidden_pre * (0.5**0.5)))
    hidden = (hidden_pre * cdf).astype(BF)
    slope = cdf + hidden_pre * jnp.exp(-0.5 * hidden_pre * hidden_pre) * ((2 * np.pi) ** -0.5)
    hidden, slope, down_2 = tie(hidden, slope, down_2)
    count_total = count[0, 0]
    (late,) = windowed(late_got, late_ring, marks)
    late, down_2 = tie(late, down_2)
    down_full = assembled_halves(down_weight, *down_2)
    result = resid + mm(hidden, down_full) + down_bias

    teach = late[0].astype(F32)
    valid = (real & (teach[:, :1] < 0.5 * FAR)).astype(F32)
    differ = valid * (result - teach)
    squares = jnp.sum(differ * differ)
    grads = jnp.where(real, late[1], jnp.zeros_like(late[1])).astype(F32)
    result_grad = grads + differ * (tokens_all / (4.0 * count_total))
    down_in = result_grad.astype(BF)

    d_send, d_keep = split_grad(hidden, down_in)
    d_send, down_in = tie(d_send, down_in)
    d_got = sent(d_send, "core")
    pre_grad = (slope * mm_nt(down_in, down_full)).astype(BF)
    d_got, d_keep, pre_grad = tie(d_got, d_keep, pre_grad)
    d_terms = [d_keep, d_got]
    d_out, pre_grad = tie(to_send(d_terms, 0, "img"), pre_grad)
    d_got = sent(d_out, "img")
    u_send, u_keep = split_grad(normed2, pre_grad)
    u_send, pre_grad = tie(u_send, pre_grad)
    u_got = sent(u_send, "core")
    u_got, u_keep, pre_grad = tie(u_got, u_keep, pre_grad)
    u_terms = [u_keep, u_got]
    u_out, pre_grad = tie(to_send(u_terms, 1, "yy"), pre_grad)
    u_got = sent(u_out, "yy")
    (
        resid_grad, proj_in, attended_grad, mlp_gain_grad, mlp_shift_grad, proj_bias_grad, up_bias_grad
    ) = mlp_back(pre_grad, up_full, resid, result_grad, mlp_gain, proj_full)
    p_send, p_keep = split_grad(attended, proj_in)
    p_send, proj_in = tie(p_send, proj_in)
    p_got = sent(p_send, "core")
    attended_grad, p_got, p_keep = tie(attended_grad, p_got, p_keep)
    p_terms = [p_keep, p_got]
    p_out, attended_grad = tie(to_send(p_terms, 0, "img"), attended_grad)
    p_got = sent(p_out, "img")

    dqkv, pad_sum, rel_grad = attention_back(attended_grad)
    dqkv, pad_sum, d_got, u_got = tie(dqkv, pad_sum, d_got, u_got)
    d_terms = kept(d_terms, 0, "img", d_got)
    u_terms = kept(u_terms, 1, "yy", u_got)
    d_out, u_out, dqkv = tie(to_send(d_terms, 0, "yy"), to_send(u_terms, 0, "img"), dqkv)
    d_got = sent(d_out, "yy")
    u_got = sent(u_out, "img")
    q_send, q_keep = split_grad(tokens_low, dqkv)
    q_send, dqkv = tie(q_send, dqkv)
    q_got = sent(q_send, "core")
    block_up, block_mid = result_rows(marks, tie(result, q_send)[0])
    block_ring = sent_back(block_up)
    q_got, q_keep, dqkv, p_got, block_mid = tie(q_got, q_keep, dqkv, p_got, block_mid)
    p_terms = kept(p_terms, 0, "img", p_got)
    half = bands // 2
    qa_terms = [q_keep[:, :, :half], q_got[:, :, :half]]
    qb_terms = [q_keep[:, :, half:], q_got[:, :, half:]]
    qa_out, qb_out, p_out = tie(
        to_send(qa_terms, 0, "img"), to_send(qb_terms, 1, "yy"), to_send(p_terms, 0, "yy")
    )
    p_got = sent(p_out, "yy")
    qa_got = sent(qa_out, "img")
    qb_got = sent(qb_out, "yy")
    qkv_parts = tie(qkv_1, qkv_2, qkv_3, qkv_4, qa_out)[:4]
    qkv_back = assembled(qkv_weight, *qkv_parts)
    d_got, qa_out, qkv_back = tie(d_got, qa_out, qkv_back)
    d_terms = [by_bits(t) for t in kept(d_terms, 0, "yy", d_got)]
    d_out, u_got, p_got = tie(low_send(d_terms), u_got, p_got)
    d_got = crossed(d_out, 1)
    u_sum = added(kept(u_terms, 0, "img", u_got))
    p_sum = added(kept(p_terms, 0, "yy", p_got))
    part, cols = p_sum.shape[1], p_sum.shape[2]
    blocks = u_sum.shape[-1] // cols
    u_terms = [by_bits(jnp.concatenate([u_sum, p_sum], axis=-1))]
    u_out, qa_got, qb_got, block_ring = tie(low_send(u_terms), qa_got, qb_got, block_ring)
    u_got = crossed(u_out, 1)
    qa_terms = kept(qa_terms, 0, "img", qa_got)
    qb_terms = kept(qb_terms, 1, "yy", qb_got)
    qa_out, qb_out, dqkv, d_got = tie(
        to_send(qa_terms, 0, "yy"), to_send(qb_terms, 0, "img"), dqkv, d_got
    )
    qa_got = sent(qa_out, "yy")
    qb_got = sent(qb_out, "img")
    d_terms = after_low(d_terms, d_got)
    d_out, dqkv = tie(high_send(d_terms), dqkv)
    d_got = crossed(d_out, 2)
    down_bias_grad = jnp.sum(down_in.astype(F32), axis=0)
    *backs, attn_gain_grad, attn_shift_grad, query_bias_grad, value_bias_grad = input_back(
        marks, dqkv, qkv_back, x_low, resid_grad, attn_gain, pad_sum
    )
    small = small_packed(
        (
            attn_gain_grad, attn_shift_grad, query_bias_grad, value_bias_grad, proj_bias_grad,
            mlp_gain_grad, mlp_shift_grad, down_bias_grad,
        ),
        up_bias_grad,
        rel_grad,
        squares.reshape(1, 1),
    )
    small = paired(small, "core")
    back_ring = sent_back(backs[0])
    backs, d_got, qa_got, qb_got, u_got = tie(backs, d_got, qa_got, qb_got, u_got)
    d_sum = after_high(d_terms, d_got)
    d_got = crossed(d_sum, 2)
    u_terms = after_low(u_terms, u_got)
    u_out, d_sum, small = tie(high_send(u_terms), d_sum, small)
    u_got = crossed(u_out, 2)
    q_whole = [
        by_bits(
            jnp.concatenate(
                [added(kept(qa_terms, 0, "yy", qa_got)), added(kept(qb_terms, 0, "img", qb_got))],
                axis=0,
            )
        )
    ]
    q_out, u_out = tie(low_send(q_whole), u_out)
    q_got = crossed(q_out, 1)
    small = paired(small, "img")
    d_got, q_out = tie(d_got, q_out)
    d_pair = jnp.stack([d_sum, d_got])
    d_got = crossed(d_pair, 1)
    u_got, d_pair, back_ring = tie(u_got, d_pair, back_ring)
    u_sum = after_high(u_terms, u_got)
    u_got = crossed(u_sum, 2)
    own_rows = band_rows_of(
        jnp.concatenate([block_mid, backs[1]]), jnp.concatenate([block_ring, back_ring])
    )
    q_got, u_sum, small, own_rows = tie(q_got, u_sum, small, own_rows)
    back_got = exchanged(own_rows)
    q_terms = after_low(q_whole, q_got)
    q_out, d_got, back_got = tie(high_send(q_terms), d_got, back_got)
    q_got = crossed(q_out, 2)
    small = paired(small, "yy")
    d_own = jnp.concatenate([d_pair, d_got], axis=0)
    d_beside, d_other = swapped(d_own, "yy"), swapped(d_own, "core")
    u_got, d_own = tie(u_got, d_own)
    u_pair = jnp.stack([u_sum, u_got])
    u_got = crossed(u_pair, 1)
    block_out, images_grad = unpacked(tie(back_got, u_pair)[0], images.shape[2], (BF, F32))
    q_got, u_pair, d_other, block_out, small = tie(q_got, u_pair, d_other, block_out, small)
    q_sum = after_high(q_terms, q_got)
    q_got = crossed(q_sum, 2)
    small = paired(small, 1)
    d_beside, u_got, q_sum = tie(d_beside, u_got, q_sum)
    d_last = swapped(d_beside, "core")
    u_own = jnp.concatenate([u_pair, u_got], axis=0)
    u_beside, u_other = swapped(u_own, "yy"), swapped(u_own, "core")
    q_got, u_own, small = tie(q_got, u_own, small)
    q_pair = jnp.stack([q_sum, q_got])
    q_got = crossed(q_pair, 1)
    small = paired(small, 2)
    q_pair, d_last = tie(q_pair, d_last)
    (down_grad,) = final(marks, d_own, d_other, d_beside, d_last, ((d_own.shape[1], 0, 1),))
    q_got, down_grad, u_other, small = tie(q_got, down_grad, u_other, small)
    q_own = jnp.concatenate([q_pair, q_got], axis=0)
    q_beside, q_other = swapped(q_own, "yy"), swapped(q_own, "core")
    u_beside, q_own = tie(u_beside, q_own)
    u_last = swapped(u_beside, "core")
    *sums, squares = small_unpacked(small, 8, up_bias.shape[0])
    u_last, squares = tie(u_last, squares)
    up_grad, proj_grad = final(
        marks, u_own, u_other, u_beside, u_last, ((part, 0, blocks), (part, blocks, 1))
    )
    q_beside, up_grad = tie(q_beside, up_grad)
    q_last = swapped(q_beside, "core")
    (qkv_grad,) = final(marks, q_own, q_other, q_beside, q_last, ((q_own.shape[1], 0, 1),))
    distill_loss = squares[0] / (count_total * width)
    return (
        block_out[None], distill_loss, images_grad[None], sums[0], sums[1], qkv_grad, sums[2], sums[3],
        sums[9], sums[10], proj_grad, sums[4], sums[5], sums[6], up_grad, sums[8], down_grad, sums[7],
    )


def solution(mesh):
    shape = dict(mesh.shape)
    fine = Mesh(
        mesh.devices.reshape(shape["img"], shape["tok"], shape["seq"] // 2, 2), EVERY
    )
    tokens = P("img", ("tok",) + SEQ, None, None)
    mask = P("img", ("tok",) + SEQ, None)
    split, whole = P("img", None), P()
    return jax.shard_map(
        local,
        mesh=fine,
        in_specs=(
            tokens, tokens, mask, tokens, whole, whole, split, whole, whole, whole, whole, split,
            whole, whole, whole, split, whole, split, whole,
        ),
        out_specs=(
            tokens, whole, tokens, whole, whole, split, whole, whole, whole, whole, split, whole,
            whole, whole, split, whole, split, whole,
        ),
        check_vma=False,
    )
```

```python
import functools

import jax
import jax.numpy as jnp
import numpy as np
from jax import lax
from jax.experimental import pallas as pl
from jax.experimental.pallas import tpu as pltpu
from jax.sharding import Mesh
from jax.sharding import PartitionSpec as P

HD = 64
WIN = 14
SLOT = 16
EDGE = 8
EPS = 1e-06
KEYS = 256
LANES = 128
FAR = 128.0
BF = jnp.bfloat16
F32 = jnp.float32
SEQ = ("yy", "core")
EVERY = ("img", "tok", "yy", "core")


def swapped(block, axis):
    size = lax.axis_size(axis)
    return lax.ppermute(block, axis, [(i, size - 1 - i) for i in range(size)])


def moved(block, axis, pairs):
    return lax.ppermute(block, axis, pairs)


def pick(pair_low, pair_high, flag):
    return jnp.where(flag == 0, pair_low, pair_high)


def tie(*values):
    return lax.optimization_barrier(values)


def layout_marks(band, place):
    first, last = band == 0, band == lax.axis_size("tok") - 1
    turned = (first & (place == 0)) | (last & (place > 0))
    corner = first & (place == 2)
    edge = turned | jnp.where(first, place == 1, place == 0)
    start = 8 - 2 * band
    real = jnp.where(edge, WIN * EDGE, jnp.where(corner, EDGE * EDGE, 0))
    return (
        start, jnp.where(corner, 0, start), turned.astype(jnp.int32), real, first.astype(jnp.int32),
        band, lax.axis_index("yy"), lax.axis_index("core"),
    )


def whole_spec(shape):
    return pl.BlockSpec(shape, lambda *_: (0,) * len(shape))


def column_picks(ways, cols):
    out = np.zeros((ways, SLOT + EDGE, cols), np.float32)
    for s in range(ways):
        for j in range(SLOT):
            out[s, j, WIN * s + j] = 1.0
        for j in range(EDGE):
            out[s, SLOT + j, WIN * ways + j] = 1.0
    return out


def turn_picks():
    out = np.zeros((WIN * EDGE, EDGE * (SLOT + EDGE)), np.float32)
    for i in range(WIN):
        for j in range(EDGE):
            out[i * EDGE + j, j * (SLOT + EDGE) + i] = 1.0
    return out


def pack_kernel(picks, block, out):
    ways, full = out.shape[0], SLOT + EDGE
    for r in range(block.shape[1]):
        both = jnp.dot(picks[...], block[0, r], preferred_element_type=F32)
        for s in range(ways):
            out[s, 0, r] = both[s * full : (s + 1) * full].astype(BF)


def packed(block):
    count, rows, cols, width = block.shape
    ways = lax.axis_size("yy") * lax.axis_size("core")
    full = SLOT + EDGE
    picks = jnp.asarray(column_picks(ways, cols).reshape(ways * full, cols), BF)
    return pl.pallas_call(
        pack_kernel,
        grid=(count,),
        in_specs=[
            whole_spec(picks.shape),
            pl.BlockSpec((1, rows, cols, width), lambda n: (n, 0, 0, 0)),
        ],
        out_specs=pl.BlockSpec((ways, 1, rows, full, width), lambda n: (0, n, 0, 0, 0)),
        out_shape=jax.ShapeDtypeStruct((ways, count, rows, full, width), BF),
        cost_estimate=pl.CostEstimate(flops=0, bytes_accessed=0, transcendentals=0),
        name="pack",
    )(picks, block)


def window_kernel(at, got, ring, turn, out):
    count, rows = got.shape[1], got.shape[2]
    start_a, start_e, turned, first = at[0], at[1], at[2], at[4]
    for n in range(count):

        def row_of(row, cols):
            own = jnp.maximum(row - 8, 0)
            before = ring[n, jnp.minimum(row, 7), cols].astype(F32)
            return jnp.where(row < 8, before, got[own // rows, n, own % rows, cols].astype(F32))

        for i in range(WIN):
            full = row_of(start_a + i, slice(0, SLOT))
            out[n, i * SLOT : (i + 1) * SLOT] = full.astype(BF)
        edge = jnp.concatenate(
            [row_of(start_e + i, slice(SLOT, SLOT + EDGE)) for i in range(WIN)], axis=0
        )
        tail = jnp.concatenate(
            [
                jnp.where(first == 1, ring[n, k], got[2 + k // rows, n, k % rows]).astype(F32)
                for k in range(EDGE)
            ],
            axis=0,
        ).astype(BF)
        bottom = jnp.dot(turn[...], tail, preferred_element_type=F32)
        out[n, WIN * SLOT :] = jnp.where(turned == 1, bottom, edge).astype(BF)


def window_norm_kernel(at, got, ring, turn, gain, shift, out, low):
    window_kernel(at, got, ring, turn, out)
    for start, size in ((0, WIN * SLOT), (WIN * SLOT, WIN * EDGE)):
        unit, _ = norm_parts(out[0, start : start + size].astype(F32))
        row = lax.broadcasted_iota(jnp.int32, (size, 1), 0)
        real = (row & (SLOT - 1)) < WIN if start == 0 else row < at[3]
        low[start : start + size] = jnp.where(real, unit * gain[...] + shift[...], 0.0).astype(BF)


def ring_rows(got, step):
    bands = lax.axis_size("tok")
    send = jnp.moveaxis(got[2:], 1, 0)
    send = send.reshape(send.shape[0], 8, SLOT + EDGE, send.shape[-1])
    return moved(send, "tok", [(i, (i + step) % bands) for i in range(bands)])


def windowed(got, ring, marks, norm=None):
    count, width = got.shape[1], got.shape[-1]
    tokens = WIN * (SLOT + EDGE)
    specs = [
        whole_spec(got.shape),
        whole_spec(ring.shape),
        whole_spec((WIN * EDGE, EDGE * (SLOT + EDGE))),
    ]
    out_specs = [whole_spec((count, tokens, width))]
    out_shape = [jax.ShapeDtypeStruct((count, tokens, width), BF)]
    if norm is not None:
        specs += [whole_spec((width,))] * 2
        out_specs.append(whole_spec((tokens, width)))
        out_shape.append(jax.ShapeDtypeStruct((tokens, width), BF))
    return pl.pallas_call(
        window_kernel if norm is None else window_norm_kernel,
        grid_spec=pltpu.PrefetchScalarGridSpec(
            num_scalar_prefetch=1, grid=(1,), in_specs=specs, out_specs=out_specs
        ),
        out_shape=out_shape,
        cost_estimate=pl.CostEstimate(flops=0, bytes_accessed=0, transcendentals=0),
        name="window",
    )(marks, got, ring, jnp.asarray(turn_picks(), BF), *(norm or ()))


def unwindow(at, flats, turn, up, mid):
    start_a, start_e, turned, first = at[0], at[1], at[2], at[4]
    full = SLOT + EDGE
    for n, flat in enumerate(flats):
        bottom = lax.dot_general(
            turn[...],
            flat[WIN * SLOT :].astype(BF),
            (((0,), (0,)), ((), ())),
            preferred_element_type=F32,
        )
        for row in range(24):
            i = row - start_e
            held = (i >= 0) & (i < WIN) & (turned == 0)
            at_row = pl.multiple_of(WIN * SLOT + EDGE * jnp.clip(i, 0, WIN - 1), EDGE)
            right = jnp.where(held, flat[pl.ds(at_row, EDGE)], 0.0)
            i = row - start_a
            at_row = pl.multiple_of(SLOT * jnp.clip(i, 0, WIN - 1), SLOT)
            left = jnp.where((i >= 0) & (i < WIN), flat[pl.ds(at_row, SLOT)], 0.0)
            if row < 8 or row >= 16:
                base = row % 8 * full
                here = (turned == 1) & (first == (1 if row < 8 else 0))
                left = jnp.where(here, bottom[base : base + SLOT], left)
            both = jnp.concatenate([left, right], axis=0).astype(BF)
            if row < 8:
                up[n, row] = both
            else:
                mid[n, row - 8] = both


def unpack_kernel(picks, got, *outs):
    for n, out in enumerate(outs):
        for r in range(got.shape[2]):
            total = None
            for s in range(got.shape[0]):
                part = lax.dot_general(
                    picks[s], got[s, n, r], (((0,), (0,)), ((), ())), preferred_element_type=F32
                )
                total = part if total is None else total + part
            out[r] = total.astype(out.dtype)


def unpacked(got, cols, dtypes):
    ways, count, rows, full, width = got.shape
    picks = column_picks(ways, cols)
    picks[:, WIN:SLOT] = 0.0
    return pl.pallas_call(
        unpack_kernel,
        in_specs=[whole_spec(picks.shape), whole_spec(got.shape)],
        out_specs=[whole_spec((rows, cols, width))] * count,
        grid=(1,),
        out_shape=[jax.ShapeDtypeStruct((rows, cols, width), dtype) for dtype in dtypes],
        cost_estimate=pl.CostEstimate(flops=0, bytes_accessed=0, transcendentals=0),
        name="unpack",
    )(jnp.asarray(picks, BF), got)


def exchanged(send):
    return lax.all_to_all(send, SEQ, split_axis=0, concat_axis=0, tiled=True)


def sent_back(up):
    bands = lax.axis_size("tok")
    return moved(up, "tok", [((i + 1) % bands, i) for i in range(bands)])


def band_rows_of(mid, ring):
    own = mid + jnp.pad(ring, ((0, 0), (8, 0), (0, 0), (0, 0)))
    ways = lax.axis_size("yy") * lax.axis_size("core")
    own = own.reshape(own.shape[0], ways, 16 // ways, SLOT + EDGE, own.shape[-1])
    return jnp.swapaxes(own, 0, 1)


def two_images():
    return lax.axis_size("img") == 2


def quarter(shard):
    if not two_images():
        return shard
    rows = shard.shape[0] // 4
    at = lax.axis_index("yy") * 2 + lax.axis_index("core")
    return lax.dynamic_slice_in_dim(shard, at * rows, rows, 0)


def half_of(shard, chunks=1):
    if not two_images():
        return [shard]
    rows = shard.shape[0] // (2 * chunks)
    first = lax.axis_index("core") * rows * chunks
    return [lax.dynamic_slice_in_dim(shard, first + i * rows, rows, 0) for i in range(chunks)]


def over_images(block):
    if two_images():
        return swapped(block, "img")
    return lax.all_gather(block, "img", axis=0, tiled=True)


def half_over_cores(block):
    return (block, swapped(block, "core")) if two_images() else block


def assembled_halves(shard, *parts):
    if not two_images():
        return parts[0]
    core, image = lax.axis_index("core"), lax.axis_index("img")
    other = jnp.concatenate(
        [pick(here, there, core) for here, there in parts]
        + [pick(there, here, core) for here, there in parts],
        axis=0,
    )
    return jnp.concatenate([pick(shard, other, image), pick(other, shard, image)], axis=0)


def over_cores(block):
    return swapped(block, "core") if two_images() else block


def gather_over_rows(block):
    return swapped(block, "yy") if two_images() else block


def assembled(shard, first, second, first_across, second_across):
    if not two_images():
        return first
    core, high, image = (lax.axis_index(a) for a in ("core", "yy", "img"))
    rows = []
    for a, b, c, d in ((first, second, first_across, second_across), (second, first, second_across, first_across)):
        here, there = pick(a, b, high), pick(c, d, high)
        rows += [pick(here, there, core), pick(there, here, core)]
    other = jnp.concatenate(rows, axis=0)
    return jnp.concatenate([pick(shard, other, image), pick(other, shard, image)], axis=0)


def part_of(terms, dim, axis, other):
    index = lax.axis_index(axis)
    index = 1 - index if other else index
    return [lax.dynamic_index_in_dim(t, index, dim, keepdims=False) for t in terms]


def added(terms):
    total = terms[0].astype(F32)
    for t in terms[1:]:
        total = total + t.astype(F32)
    return total.astype(BF)


def to_send(terms, dim, axis):
    if lax.axis_size(axis) != 2:
        return jnp.moveaxis(added(terms), dim, 0)
    return added(part_of(terms, dim, axis, True))


def sent(block, axis):
    if lax.axis_size(axis) != 2:
        return lax.all_to_all(block, axis, split_axis=0, concat_axis=0, tiled=True)
    return swapped(block, axis)


def kept(terms, dim, axis, got):
    if lax.axis_size(axis) != 2:
        return [got[i] for i in range(got.shape[0])]
    return part_of(terms, dim, axis, False) + [got]


def split_grad(left, right):
    images, bands = lax.axis_size("img"), lax.axis_size("tok")
    core = lax.axis_index("core")
    rows, cols = left.shape[1], right.shape[1] // 2
    shape = (images, 2, bands, rows // images // 2 // bands, cols)

    def one(index):
        half = lax.dynamic_slice_in_dim(right, index * cols, cols, 1)
        return mm_tn(left, half).astype(BF).reshape(shape)

    return one(1 - core), one(core)


def crossed(block, distance):
    size = lax.axis_size("tok")
    return lax.ppermute(block, "tok", [(i, i ^ distance) for i in range(size)])


def by_bits(block):
    return block.reshape((2, 2) + block.shape[1:])


def bit_of(terms, dim, bit, other):
    index = (lax.axis_index("tok") >> bit) & 1
    index = 1 - index if other else index
    return [lax.dynamic_index_in_dim(t, index, dim, keepdims=False) for t in terms]


def low_send(terms):
    return added(bit_of(terms, 1, 0, True))


def high_send(terms):
    return added(bit_of(terms, 0, 1, True))


def after_low(terms, got):
    return bit_of(terms, 1, 0, False) + [got]


def after_high(terms, got):
    return added(bit_of(terms, 0, 1, False) + [got])


def final_kernel(splits, unit, at, near_own, near_other, far_own, far_other, *outs):
    band, core = at[5], at[7]

    def write(own, other):
        for t in range(own.shape[0]):
            to = ((t >> 1) | ((t & 1) << 1)) ^ band
            for (rows, first, blocks), out in zip(splits, outs):
                size = blocks * unit
                a = own[t, :, first * unit : first * unit + size].astype(F32)
                b = other[t, :, first * unit : first * unit + size].astype(F32)
                out[0, to, :, :size] = jnp.where(core == 0, a, b)
                out[0, to, :, size:] = jnp.where(core == 0, b, a)

    @pl.when(pl.program_id(0) == 0)
    def near():
        write(near_own, near_other)

    @pl.when(pl.program_id(0) == 1)
    def far():
        write(far_own, far_other)


def final(marks, own, other_core, beside, beside_other_core, splits):
    bands, rows, cols = own.shape
    unit = cols // sum(blocks for _, _, blocks in splits)
    outs = pl.pallas_call(
        functools.partial(final_kernel, splits, unit),
        grid_spec=pltpu.PrefetchScalarGridSpec(
            num_scalar_prefetch=1,
            grid=(2,),
            in_specs=[whole_spec(own.shape)] * 4,
            out_specs=[
                pl.BlockSpec((1, bands, n, 2 * blocks * unit), lambda y, at: (y ^ at[6], 0, 0, 0))
                for n, _, blocks in splits
            ],
        ),
        out_shape=[
            jax.ShapeDtypeStruct((2, bands, n, 2 * blocks * unit), F32) for n, _, blocks in splits
        ],
        cost_estimate=pl.CostEstimate(flops=0, bytes_accessed=0, transcendentals=0),
        name="final",
    )(marks, own, other_core, beside, beside_other_core)
    return [o.reshape(-1, o.shape[-1]) for o in outs]


def paired(value, axis):
    if axis == "img" and not two_images():
        return lax.psum(value, "img")
    across = crossed(value, axis) if isinstance(axis, int) else swapped(value, axis)
    return value + across


def small_pack_kernel(*refs):
    vectors, up_bias, tables, squares, out = refs[:8], refs[8], refs[9], refs[10], refs[11]
    width = out.shape[1]
    for i, vector in enumerate(vectors):
        out[i, :] = vector[...]
    row = len(vectors)
    for i in range(up_bias.shape[0] // width):
        out[row, :] = up_bias[i * width : (i + 1) * width]
        row += 1
    fit = width // LANES
    for m in range(2 * WIN - 1):
        at = (m % fit) * LANES
        out[row + m // fit, at : at + LANES] = tables[m, :]
    row += -(-(2 * WIN - 1) // fit)
    out[row : row + 1, :LANES] = jnp.broadcast_to(squares[...], (1, LANES))


def small_packed(vectors, up_bias, tables, squares):
    width = vectors[0].shape[0]
    rows = len(vectors) + up_bias.shape[0] // width - (-(2 * WIN - 1) // (width // LANES)) + 1
    args = (*vectors, up_bias, tables, squares)
    return pl.pallas_call(
        small_pack_kernel,
        grid=(1,),
        in_specs=[whole_spec(a.shape) for a in args],
        out_specs=whole_spec((rows, width)),
        out_shape=jax.ShapeDtypeStruct((rows, width), F32),
        cost_estimate=pl.CostEstimate(flops=0, bytes_accessed=0, transcendentals=0),
        name="small_pack",
    )(*args)


def small_unpack_kernel(packed, *outs):
    vectors, up_bias, rows_out, cols_out, squares = outs[:8], outs[8], outs[9], outs[10], outs[11]
    width = packed.shape[1]
    for i, vector in enumerate(vectors):
        vector[...] = packed[i, :]
    row = len(vectors)
    for i in range(up_bias.shape[0] // width):
        up_bias[i * width : (i + 1) * width] = packed[row, :]
        row += 1
    fit = width // LANES
    for m in range(2 * WIN - 1):
        at = (m % fit) * LANES
        both = packed[row + m // fit : row + m // fit + 1, at : at + LANES]
        rows_out[m : m + 1, :] = both[:, :HD]
        cols_out[m : m + 1, :] = pltpu.roll(both, HD, 1)[:, :HD]
    row += -(-(2 * WIN - 1) // fit)
    squares[...] = packed[row, :LANES]


def small_unpacked(packed, vectors, up_width):
    width = packed.shape[1]
    table = (2 * WIN - 1, HD)
    shapes = [(width,)] * vectors + [(up_width,), table, table, (LANES,)]
    return pl.pallas_call(
        small_unpack_kernel,
        grid=(1,),
        in_specs=[whole_spec(packed.shape)],
        out_specs=[whole_spec(shape) for shape in shapes],
        out_shape=[jax.ShapeDtypeStruct(shape, F32) for shape in shapes],
        cost_estimate=pl.CostEstimate(flops=0, bytes_accessed=0, transcendentals=0),
        name="small_unpack",
    )(packed)


def rolled(block, amount):
    return pltpu.roll(block, amount, 1, stride=1, stride_axis=0)


def rel_places():
    size = 2 * WIN - 1
    out = np.zeros((4, LANES, size), np.float32)
    for m in range(size):
        out[0, size - 1 - m, m] = 1.0
        out[1, 32 + size - 1 - m, m] = 1.0
        out[2, m, m] = 1.0
        out[3, 64 + m, m] = 1.0
    return out


def head_places():
    out = np.zeros((2, HD, LANES), np.float32)
    for c in range(HD):
        out[0, c, c] = 1.0
        out[1, c, HD + c] = 1.0
    return out


def build_rel(tables, places, heads, out):
    for half in (0, 1):
        total = None
        for table, place in zip(tables, places):
            high = table.astype(BF)
            value = (table - high.astype(F32)).astype(BF) if half else high
            part = jnp.dot(place, value, preferred_element_type=F32)
            total = part if total is None else total + part
        for head in (0, 1):
            lanes = jnp.dot(total.astype(BF), heads[head], preferred_element_type=F32)
            out[head, :, half * LANES : (half + 1) * LANES] = lanes.astype(BF)


def build_both(at, rows, cols, places, heads, rel_a, rel_b):
    @pl.when(pl.program_id(0) == 0)
    def build():
        turned = at[2] == 1
        build_rel((rows[...], cols[...]), places, heads, rel_a)
        first = jnp.where(turned, cols[...], rows[...])
        second = jnp.where(turned, rows[...], cols[...])
        build_rel((first, second), places, heads, rel_b)


def rel_terms(q, rel):
    return lax.dot_general(
        jnp.concatenate([q, q], axis=1), rel, (((1,), (1,)), ((), ())), preferred_element_type=F32
    )


def wide_queries(q, terms, group):
    m = q.shape[0]
    lane = lax.broadcasted_iota(jnp.int32, (group, LANES), 1)
    blocks = []
    for i in range(WIN):
        t = terms[i * group : (i + 1) * group]
        by_row = pltpu.roll(t, (LANES - (WIN - 1) + i) % LANES, 1)
        by_col = rolled(t, 19)
        blocks.append(jnp.where(lane < 64, by_row, by_col))
    both = jnp.concatenate(blocks, axis=0)
    high = both.astype(BF).astype(F32)
    low = pltpu.roll(both - high, 32, 1)
    lane = lax.broadcasted_iota(jnp.int32, (m, LANES), 1)
    mixed = jnp.where((lane & 63) < 32, high, low)
    mixed = jnp.where(lane == LANES - 1, 1.0, mixed)
    return jnp.concatenate([q * BF(HD**-0.5), mixed.astype(BF)], axis=1)


def full_keys(k, v, v_pad):
    n = k.shape[0]
    zeros = jnp.zeros((KEYS - n, LANES), BF)
    if v_pad is None:
        return jnp.concatenate([k, zeros], axis=0), jnp.concatenate([v, zeros], axis=0)
    fill = jnp.broadcast_to(v_pad, (KEYS - n, LANES)).astype(BF)
    return jnp.concatenate([k, zeros], axis=0), jnp.concatenate([v, fill], axis=0)


def only(block, head):
    lane = lax.broadcasted_iota(jnp.int32, block.shape, 1)
    return jnp.where((lane < HD) == (head == 0), block, jnp.zeros_like(block))


def scored(wide, keys, hot, head):
    return lax.dot_general(
        wide,
        jnp.concatenate([only(keys, head), hot], axis=1),
        (((1,), (1,)), ((), ())),
        preferred_element_type=F32,
    )


def softmax_low(scores):
    e = jnp.exp(scores - jnp.max(scores, axis=1, keepdims=True))
    return (e * (1.0 / jnp.sum(e, axis=1, keepdims=True))).astype(BF)


def attend_kernel(
    at, q, k, v, v_pad, rows, cols, places, heads, hot_a, hot_b, out, probs_a, probs_b, rel_a, rel_b
):
    build_both(at, rows, cols, (places[0], places[1]), heads, rel_a, rel_b)
    n = WIN * SLOT
    pad = v_pad[...].astype(BF)
    slots = (
        (slice(0, n), None, rel_a, hot_a, SLOT, probs_a),
        (slice(n, n + WIN * EDGE), pad, rel_b, hot_b, EDGE, probs_b),
    )
    both = [(s, h) for s in (0, 1) for h in (0, 1)]
    queries = [q[slot[0]] for slot in slots]
    terms = [
        rel_terms(queries[i], slots[i][2][...].reshape(2 * LANES, 2 * LANES)) for i in (0, 1)
    ]
    filled = [full_keys(k[slot[0]], v[slot[0]], slot[1]) for slot in slots]
    wide = [
        wide_queries(queries[i], terms[i][:, h * LANES : (h + 1) * LANES], slots[i][4])
        for i, h in both
    ]
    scores = [scored(w, filled[i][0], slots[i][3][...], h) for w, (i, h) in zip(wide, both)]
    probs = [softmax_low(x) for x in scores]
    for p, (i, h) in zip(probs, both):
        slots[i][5][h] = p
    parts = [
        jnp.dot(p, only(filled[i][1], h), preferred_element_type=F32)
        for p, (i, h) in zip(probs, both)
    ]
    for i in (0, 1):
        out[slots[i][0]] = (parts[2 * i] + parts[2 * i + 1]).astype(BF)


def back_terms(both, group):
    lane = lax.broadcasted_iota(jnp.int32, (group, LANES), 1)
    blocks = []
    for i in range(WIN):
        t = both[i * group : (i + 1) * group, LANES:]
        by_row = jnp.where(lane < WIN, t, 0.0)
        by_row = pltpu.roll(by_row, i, 1) if i else by_row
        by_col = rolled(jnp.where((lane >= 64) & (lane < 64 + WIN), t, 0.0), 0)
        blocks.append(by_row + by_col)
    terms = jnp.concatenate(blocks, axis=0)
    high = terms.astype(BF)
    return jnp.concatenate([high, (terms - high.astype(F32)).astype(BF)], axis=1)


def over_rows(left, right):
    return lax.dot_general(left, right, (((0,), (0,)), ((), ())), preferred_element_type=F32)


def attend_back_kernel(
    at, q, k, v, v_pad, rows, cols, places, heads, hot_a, hot_b, grad, probs_a, probs_b,
    dqkv, pad_sum, rel_grad, rel_a, rel_b, acc_a, acc_b,
):
    step = pl.program_id(0)
    steps = dqkv.shape[1] // (3 * LANES)
    build_both(at, rows, cols, (places[2], places[3]), heads, rel_a, rel_b)

    @pl.when(step == 0)
    def clear():
        acc_a[...] = jnp.zeros_like(acc_a)
        acc_b[...] = jnp.zeros_like(acc_b)

    n = WIN * SLOT
    scale = HD**-0.5
    pad = v_pad[...].astype(BF)
    slots = (
        (slice(0, n), None, rel_a, hot_a, SLOT, probs_a, acc_a),
        (slice(n, n + WIN * EDGE), pad, rel_b, hot_b, EDGE, probs_b, acc_b),
    )
    both = [(s, h) for s in (0, 1) for h in (0, 1)]
    queries = [q[slot[0]] for slot in slots]
    grads = [grad[slot[0]] for slot in slots]
    filled = [full_keys(k[slot[0]], v[slot[0]], slot[1]) for slot in slots]
    probs_grad = [
        lax.dot_general(
            grads[i], only(filled[i][1], h), (((1,), (1,)), ((), ())), preferred_element_type=F32
        )
        for i, h in both
    ]
    dvs = [over_rows(slots[i][5][h], grads[i]) for i, h in both]
    scores_grad = []
    for dp, (i, h) in zip(probs_grad, both):
        wide = slots[i][5][h].astype(F32)
        inner = jnp.sum(wide * dp, axis=1, keepdims=True)
        scores_grad.append((wide * (dp - inner)).astype(BF))
    sums = [
        jnp.dot(
            ds,
            jnp.concatenate([only(filled[i][0], h), slots[i][3][...]], axis=1),
            preferred_element_type=F32,
        )
        for ds, (i, h) in zip(scores_grad, both)
    ]
    dks = [over_rows(ds, queries[i]) * scale for ds, (i, h) in zip(scores_grad, both)]
    split = [back_terms(x, slots[i][4]) for x, (i, h) in zip(sums, both)]
    parts = []
    for x, t, (i, h) in zip(sums, split, both):
        rel = slots[i][2][h]
        part = x[:, :LANES] * scale + jnp.dot(
            t,
            jnp.concatenate([rel[:, :LANES], rel[:, :LANES]], axis=0),
            preferred_element_type=F32,
        )
        parts.append(part + jnp.dot(t[:, :LANES], rel[:, LANES:], preferred_element_type=F32))
    for t, (i, h) in zip(split, both):
        slots[i][6][h] += over_rows(t, queries[i])
    lane = lax.broadcasted_iota(jnp.int32, (KEYS, LANES), 1)
    for i in (0, 1):
        here, size = slots[i][0], queries[i].shape[0]
        dk = jnp.where(lane < HD, dks[2 * i], dks[2 * i + 1]).astype(BF)
        dv = jnp.where(lane < HD, dvs[2 * i], dvs[2 * i + 1]).astype(BF)
        found = ((parts[2 * i] + parts[2 * i + 1]).astype(BF), dk[:size], dv[:size])
        for j, value in enumerate(found):
            to = pl.ds(pl.multiple_of((j * steps + step) * LANES, LANES), LANES)
            dqkv[here, to] = value
    pad_sum[...] = jnp.sum(dv[WIN * EDGE :].astype(F32), axis=0, keepdims=True)

    @pl.when(step == steps - 1)
    def tables():
        def table(acc):
            even = acc[0, :LANES] + acc[0, LANES:]
            odd = acc[1, :LANES] + acc[1, LANES:]
            return even + pltpu.roll(odd, HD, 1)

        a, b = table(acc_a), table(acc_b)
        turned = at[2] == 1
        low, high = slice(0, 32), slice(64, 96)
        rows_grad = a[low] + jnp.where(turned, b[high], b[low])
        cols_grad = a[high] + jnp.where(turned, b[low], b[high])
        lane = lax.broadcasted_iota(jnp.int32, (32, LANES), 1)
        rel_grad[...] = jnp.where(lane < HD, rows_grad, pltpu.roll(cols_grad, HD, 1))


def hot_tables():
    def table(place):
        out = np.zeros((2, KEYS, LANES), np.float32)
        for key in range(KEYS):
            at = place(key)
            if at is None:
                out[0, key, LANES - 1] = -1e30
            else:
                for base, index in ((0, at[0]), (32, at[0]), (64, at[1]), (96, at[1])):
                    out[0, key, base + index] = 1.0
                out[1, key, WIN - 1 - at[0]] = 1.0
                out[1, key, 64 + WIN - 1 - at[1]] = 1.0
        return out

    def whole(key):
        i, j = divmod(key, SLOT)
        return (i, j) if i < WIN and j < WIN else None

    def partial(key):
        if key < WIN * EDGE:
            return divmod(key, EDGE)
        i, j = divmod(key - WIN * EDGE, EDGE)
        return (i, EDGE + j) if i < WIN and EDGE + j < WIN else None

    return table(whole), table(partial)


def attention(qkv, v_pad, rel_rows, rel_cols, marks):
    tokens_a, tokens_b = WIN * SLOT, WIN * EDGE
    tokens, width = qkv.shape[0], qkv.shape[1] // 3
    pairs = width // LANES
    table = (2 * WIN - 1, HD)
    hots = [jnp.asarray(t, BF) for t in hot_tables()]
    places, heads = jnp.asarray(rel_places(), BF), jnp.asarray(head_places(), BF)

    def cols(n, base):
        return pl.BlockSpec((n, LANES), lambda p, at: (0, base * pairs + p))

    specs = [cols(tokens, i) for i in range(3)] + [
        pl.BlockSpec((LANES,), lambda p, at: (p,)),
        whole_spec(table),
        whole_spec(table),
        whole_spec(places.shape),
        whole_spec(heads.shape),
        whole_spec((KEYS, LANES)),
        whole_spec((KEYS, LANES)),
    ]
    probs_specs = [
        pl.BlockSpec((2, tokens_a, KEYS), lambda p, at: (p, 0, 0)),
        pl.BlockSpec((2, tokens_b, KEYS), lambda p, at: (p, 0, 0)),
    ]
    rel_scratch = [pltpu.VMEM((2, LANES, 2 * LANES), BF)] * 2
    shared = (marks, qkv, qkv, qkv, v_pad, rel_rows, rel_cols, places, heads)
    out, probs_a, probs_b = pl.pallas_call(
        attend_kernel,
        grid_spec=pltpu.PrefetchScalarGridSpec(
            num_scalar_prefetch=1,
            grid=(pairs,),
            in_specs=specs,
            out_specs=[cols(tokens, 0)] + probs_specs,
            scratch_shapes=rel_scratch,
        ),
        out_shape=[
            jax.ShapeDtypeStruct((tokens, width), BF),
            jax.ShapeDtypeStruct((2 * pairs, tokens_a, KEYS), BF),
            jax.ShapeDtypeStruct((2 * pairs, tokens_b, KEYS), BF),
        ],
        cost_estimate=pl.CostEstimate(flops=0, bytes_accessed=0, transcendentals=0),
        name="attend",
    )(*shared, hots[0][0], hots[1][0])

    def back(grad):
        return pl.pallas_call(
            attend_back_kernel,
            grid_spec=pltpu.PrefetchScalarGridSpec(
                num_scalar_prefetch=1,
                grid=(pairs,),
                in_specs=specs + [cols(tokens, 0)] + probs_specs,
                out_specs=[
                    whole_spec((tokens, 3 * width)),
                    cols(1, 0),
                    whole_spec((32, LANES)),
                ],
                scratch_shapes=rel_scratch + [pltpu.VMEM((2, 2 * LANES, LANES), F32)] * 2,
            ),
            out_shape=[
                jax.ShapeDtypeStruct((tokens, 3 * width), BF),
                jax.ShapeDtypeStruct((1, width), F32),
                jax.ShapeDtypeStruct((32, LANES), F32),
            ],
            cost_estimate=pl.CostEstimate(flops=0, bytes_accessed=0, transcendentals=0),
            name="attend_back",
        )(*shared, hots[0][1], hots[1][1], grad, probs_a, probs_b)

    return out, back


def norm_parts(values):
    centre = jnp.mean(values, axis=-1, keepdims=True)
    centred = values - centre
    spread = jnp.mean(centred * centred, axis=-1, keepdims=True)
    scale = lax.rsqrt(spread + EPS)
    return centred * scale, scale


def norm_back(grad, unit, scale, gain):
    g = grad * gain
    mean = jnp.mean(g, axis=-1, keepdims=True)
    along = jnp.mean(g * unit, axis=-1, keepdims=True)
    return scale * (g - mean - unit * along)


def mlp_back_kernel(
    pre, up, resid, result_grad, gain, proj, resid_grad, proj_in, attended_grad, gain_grad, shift_grad,
    proj_bias_grad, up_bias_grad, total,
):
    step = pl.program_id(0)
    part = mm_nt(pre[...], up[...])
    up_bias_grad[...] = jnp.sum(pre[...].astype(F32), axis=0)

    @pl.when(step == 0)
    def first():
        total[...] = part

    @pl.when(step > 0)
    def more():
        total[...] += part

    @pl.when(step == pl.num_programs(0) - 1)
    def last():
        grad = total[...]
        unit, scale = norm_parts(resid[...])
        gain_grad[...] = jnp.sum(grad * unit, axis=0)
        shift_grad[...] = jnp.sum(grad, axis=0)
        found = result_grad[...] + norm_back(grad, unit, scale, gain[...])
        resid_grad[...] = found
        low = found.astype(BF)
        proj_in[...] = low
        proj_bias_grad[...] = jnp.sum(low.astype(F32), axis=0)
        attended_grad[...] = mm_nt(low, proj[...]).astype(BF)


def mlp_back(pre_grad, up_full, resid, result_grad, gain, proj_full):
    tokens, hidden = pre_grad.shape
    width = resid.shape[1]
    size = 1024
    steps = hidden // size
    flat = jax.ShapeDtypeStruct((width,), F32)
    return pl.pallas_call(
        mlp_back_kernel,
        grid=(steps,),
        in_specs=[
            pl.BlockSpec((tokens, size), lambda k: (0, k)),
            pl.BlockSpec((width, size), lambda k: (0, k)),
            whole_spec(resid.shape),
            whole_spec(resid.shape),
            whole_spec((width,)),
            whole_spec(proj_full.shape),
        ],
        out_specs=[whole_spec(resid.shape)] * 3
        + [whole_spec((width,))] * 3
        + [pl.BlockSpec((size,), lambda k: (k,))],
        out_shape=[
            jax.ShapeDtypeStruct(resid.shape, F32),
            jax.ShapeDtypeStruct(resid.shape, BF),
            jax.ShapeDtypeStruct(resid.shape, BF),
            flat,
            flat,
            flat,
            jax.ShapeDtypeStruct((hidden,), F32),
        ],
        scratch_shapes=[pltpu.VMEM(resid.shape, F32)],
        cost_estimate=pl.CostEstimate(flops=0, bytes_accessed=0, transcendentals=0),
        name="mlp_back",
    )(pre_grad, up_full, resid, result_grad, gain, proj_full)


def input_back_kernel(
    at, dqkv, weight, low, resid_grad, gain, pad_sum, turn, up, mid, gain_grad, shift_grad,
    query_sum, value_sum, total,
):
    step = pl.program_id(0)
    part = mm_nt(dqkv[...], weight[...])
    sums = jnp.sum(dqkv[...].astype(F32), axis=0)

    @pl.when(step == 0)
    def first():
        total[...] = part
        query_sum[...] = sums

    @pl.when(step > 0)
    def more():
        total[...] += part

    @pl.when(step == pl.num_programs(0) - 1)
    def last():
        value_sum[...] = sums + pad_sum[0]
        row = lax.broadcasted_iota(jnp.int32, (total.shape[0], 1), 0)
        full = WIN * SLOT
        limit = jnp.where(row < full, row - (row & (SLOT - 1)) + WIN, full + at[3])
        real = row < limit
        grad = jnp.where(real, total[...], 0.0)
        unit, scale = norm_parts(low[...].astype(F32))
        gain_grad[...] = jnp.sum(grad * unit, axis=0)
        shift_grad[...] = jnp.sum(grad, axis=0)
        total[...] = resid_grad[...] + norm_back(grad, unit, scale, gain[...])
        unwindow(at, (total,), turn, up, mid)


def input_back(marks, dqkv, qkv_full, low, resid_grad, gain, pad_sum):
    tokens, width = low.shape
    full = SLOT + EDGE
    flat = jax.ShapeDtypeStruct((width,), F32)
    shapes = [(1, 8, full, width), (1, 16, full, width)]
    return pl.pallas_call(
        input_back_kernel,
        grid_spec=pltpu.PrefetchScalarGridSpec(
            num_scalar_prefetch=1,
            grid=(3,),
            in_specs=[
                pl.BlockSpec((tokens, width), lambda k, at: (0, k)),
                pl.BlockSpec((width, width), lambda k, at: (0, k)),
                whole_spec(low.shape),
                whole_spec(low.shape),
                whole_spec((width,)),
                whole_spec((1, width)),
                whole_spec((WIN * EDGE, EDGE * full)),
            ],
            out_specs=[whole_spec(shape) for shape in shapes] + [whole_spec((width,))] * 4,
            scratch_shapes=[pltpu.VMEM(low.shape, F32)],
        ),
        out_shape=[jax.ShapeDtypeStruct(shape, BF) for shape in shapes] + [flat] * 4,
        cost_estimate=pl.CostEstimate(flops=0, bytes_accessed=0, transcendentals=0),
        name="input_back",
    )(marks, dqkv, qkv_full, low, resid_grad, gain, pad_sum, jnp.asarray(turn_picks(), BF))


def result_rows_kernel(at, result, turn, up, mid, block):
    row = lax.broadcasted_iota(jnp.int32, (result.shape[0], 1), 0)
    full = WIN * SLOT
    limit = jnp.where(row < full, row - (row & (SLOT - 1)) + WIN, full + at[3])
    block[...] = jnp.where(row < limit, result[...], 0.0)
    unwindow(at, (block,), turn, up, mid)


def result_rows(marks, result):
    width, full = result.shape[1], SLOT + EDGE
    shapes = [(1, 8, full, width), (1, 16, full, width)]
    return pl.pallas_call(
        result_rows_kernel,
        grid_spec=pltpu.PrefetchScalarGridSpec(
            num_scalar_prefetch=1,
            grid=(1,),
            in_specs=[whole_spec(result.shape), whole_spec((WIN * EDGE, EDGE * full))],
            out_specs=[whole_spec(shape) for shape in shapes],
            scratch_shapes=[pltpu.VMEM(result.shape, F32)],
        ),
        out_shape=[jax.ShapeDtypeStruct(shape, BF) for shape in shapes],
        cost_estimate=pl.CostEstimate(flops=0, bytes_accessed=0, transcendentals=0),
        name="result_rows",
    )(marks, result, jnp.asarray(turn_picks(), BF))


def mm(a, b):
    return jnp.dot(a, b, preferred_element_type=F32)


def mm_nt(a, b):
    return lax.dot_general(a, b, (((1,), (1,)), ((), ())), preferred_element_type=F32)


def mm_tn(a, b):
    return lax.dot_general(a, b, (((0,), (0,)), ((), ())), preferred_element_type=F32)


def local(
    images, teacher, valid_mask, out_grad, attn_gain, attn_shift, qkv_weight, query_bias,
    value_bias, rel_rows, rel_cols, proj_weight, proj_bias, mlp_gain, mlp_shift, up_weight,
    up_bias, down_weight, down_bias,
):
    band = lax.axis_index("tok")
    bands = lax.axis_size("tok")
    place = lax.axis_index("yy") * lax.axis_size("core") + lax.axis_index("core")
    width = images.shape[-1]
    image_rows = images.shape[1] * bands * lax.axis_size("yy") * lax.axis_size("core")
    tokens_all = images.shape[0] * lax.axis_size("img") * image_rows * images.shape[2]

    marks = layout_marks(band, place)
    real_edge = marks[3]
    marks = jnp.stack(marks).astype(jnp.int32)
    x_got = exchanged(packed(images))
    qkv_1 = over_images(quarter(qkv_weight))
    proj_1 = [over_images(c) for c in half_of(proj_weight)]
    up_1 = [over_images(c) for c in half_of(up_weight)]
    down_1 = [over_images(c) for c in half_of(down_weight, 2)]
    count = jnp.broadcast_to(jnp.sum(valid_mask.astype(F32)), (8, LANES))
    count = paired(count, "img")
    x_got, qkv_1, marks, count = tie(x_got, qkv_1, marks, count)
    qkv_2 = gather_over_rows(qkv_1)
    x_ring = ring_rows(x_got, 1)
    qkv_3 = over_cores(qkv_1)
    count = paired(count, "core")
    marked = jnp.where(valid_mask[..., None] > 0, teacher, jnp.full_like(teacher, FAR))
    late_pack = packed(tie(jnp.concatenate([marked, out_grad], axis=0), qkv_1)[0])
    x_ring, x_got, late_pack, count = tie(x_ring, x_got, late_pack, count)
    x_low, tokens_low = windowed(x_got, x_ring, marks, (attn_gain, attn_shift))
    x_low = x_low[0]
    count = paired(count, "yy")
    qkv_2, x_low, tokens_low, qkv_3 = tie(qkv_2, x_low, tokens_low, qkv_3)
    qkv_4 = over_cores(qkv_2)
    late_got = exchanged(tie(late_pack, x_low)[0])
    qkv_4, proj_1[0], count, up_1[0] = tie(qkv_4, proj_1[0], count, up_1[0])
    up_2 = [half_over_cores(up_1[0])]
    proj_2 = half_over_cores(proj_1[0])
    count = paired(count, 1)

    row_a = lax.broadcasted_iota(jnp.int32, (WIN * SLOT, 1), 0)
    row_b = lax.broadcasted_iota(jnp.int32, (WIN * EDGE, 1), 0)
    real = jnp.concatenate(
        [(row_a & (SLOT - 1)) < WIN, row_b < real_edge], axis=0
    )
    inputs = x_low.astype(F32)
    qkv_bias = jnp.concatenate([query_bias, jnp.zeros_like(query_bias), value_bias])
    qkv_full = assembled(qkv_weight, qkv_1, qkv_2, qkv_3, qkv_4)
    qkv = (mm(tokens_low, qkv_full) + qkv_bias).astype(BF)
    proj_full = assembled_halves(proj_weight, proj_2)
    up_full = assembled_halves(up_weight, *up_2)
    qkv, late_got, proj_full, count, up_full, down_1[0] = tie(
        qkv, late_got, proj_full, count, up_full, down_1[0]
    )
    late_ring = ring_rows(late_got, 1)
    count = paired(count, 2)
    attended, attention_back = attention(qkv, value_bias, rel_rows, rel_cols, marks)
    down_2 = [half_over_cores(down_1[0])]
    attended, count, late_ring, down_1, down_2 = tie(attended, count, late_ring, down_1, down_2)
    resid = inputs + mm(attended, proj_full) + proj_bias
    unit2, scale2 = norm_parts(resid)
    normed2 = (unit2 * mlp_gain + mlp_shift).astype(BF)
    down_2 = down_2 + [half_over_cores(c) for c in down_1[1:]]
    hidden_pre = mm(normed2, up_full) + up_bias
    cdf = 0.5 * (1.0 + lax.erf(hidden_pre * (0.5**0.5)))
    hidden = (hidden_pre * cdf).astype(BF)
    slope = cdf + hidden_pre * jnp.exp(-0.5 * hidden_pre * hidden_pre) * ((2 * np.pi) ** -0.5)
    hidden, slope, down_2 = tie(hidden, slope, down_2)
    count_total = count[0, 0]
    (late,) = windowed(late_got, late_ring, marks)
    late, down_2 = tie(late, down_2)
    down_full = assembled_halves(down_weight, *down_2)
    result = resid + mm(hidden, down_full) + down_bias

    teach = late[0].astype(F32)
    valid = (real & (teach[:, :1] < 0.5 * FAR)).astype(F32)
    differ = valid * (result - teach)
    squares = jnp.sum(differ * differ)
    grads = jnp.where(real, late[1], jnp.zeros_like(late[1])).astype(F32)
    result_grad = grads + differ * (tokens_all / (4.0 * count_total))
    down_in = result_grad.astype(BF)

    d_send, d_keep = split_grad(hidden, down_in)
    d_send, down_in = tie(d_send, down_in)
    d_got = sent(d_send, "core")
    pre_grad = (slope * mm_nt(down_in, down_full)).astype(BF)
    d_got, d_keep, pre_grad = tie(d_got, d_keep, pre_grad)
    d_terms = [d_keep, d_got]
    d_out, pre_grad = tie(to_send(d_terms, 0, "img"), pre_grad)
    d_got = sent(d_out, "img")
    u_send, u_keep = split_grad(normed2, pre_grad)
    u_send, pre_grad = tie(u_send, pre_grad)
    u_got = sent(u_send, "core")
    u_got, u_keep, pre_grad = tie(u_got, u_keep, pre_grad)
    u_terms = [u_keep, u_got]
    u_out, pre_grad = tie(to_send(u_terms, 1, "yy"), pre_grad)
    u_got = sent(u_out, "yy")
    (
        resid_grad, proj_in, attended_grad, mlp_gain_grad, mlp_shift_grad, proj_bias_grad, up_bias_grad
    ) = mlp_back(pre_grad, up_full, resid, result_grad, mlp_gain, proj_full)
    p_send, p_keep = split_grad(attended, proj_in)
    p_send, proj_in = tie(p_send, proj_in)
    p_got = sent(p_send, "core")
    attended_grad, p_got, p_keep = tie(attended_grad, p_got, p_keep)
    p_terms = [p_keep, p_got]
    p_out, attended_grad = tie(to_send(p_terms, 0, "img"), attended_grad)
    p_got = sent(p_out, "img")

    dqkv, pad_sum, rel_grad = attention_back(attended_grad)
    dqkv, pad_sum, d_got, u_got = tie(dqkv, pad_sum, d_got, u_got)
    d_terms = kept(d_terms, 0, "img", d_got)
    u_terms = kept(u_terms, 1, "yy", u_got)
    d_out, u_out, dqkv = tie(to_send(d_terms, 0, "yy"), to_send(u_terms, 0, "img"), dqkv)
    d_got = sent(d_out, "yy")
    u_got = sent(u_out, "img")
    q_send, q_keep = split_grad(tokens_low, dqkv)
    q_send, dqkv = tie(q_send, dqkv)
    q_got = sent(q_send, "core")
    block_up, block_mid = result_rows(marks, tie(result, q_send)[0])
    block_ring = sent_back(block_up)
    q_got, q_keep, dqkv, p_got, block_mid = tie(q_got, q_keep, dqkv, p_got, block_mid)
    p_terms = kept(p_terms, 0, "img", p_got)
    half = bands // 2
    qa_terms = [q_keep[:, :, :half], q_got[:, :, :half]]
    qb_terms = [q_keep[:, :, half:], q_got[:, :, half:]]
    qa_out, qb_out, p_out = tie(
        to_send(qa_terms, 0, "img"), to_send(qb_terms, 1, "yy"), to_send(p_terms, 0, "yy")
    )
    p_got = sent(p_out, "yy")
    qa_got = sent(qa_out, "img")
    qb_got = sent(qb_out, "yy")
    qkv_parts = tie(qkv_1, qkv_2, qkv_3, qkv_4, qa_out)[:4]
    qkv_back = assembled(qkv_weight, *qkv_parts)
    d_got, qa_out, qkv_back = tie(d_got, qa_out, qkv_back)
    d_terms = [by_bits(t) for t in kept(d_terms, 0, "yy", d_got)]
    d_out, u_got, p_got = tie(low_send(d_terms), u_got, p_got)
    d_got = crossed(d_out, 1)
    u_sum = added(kept(u_terms, 0, "img", u_got))
    p_sum = added(kept(p_terms, 0, "yy", p_got))
    part, cols = p_sum.shape[1], p_sum.shape[2]
    blocks = u_sum.shape[-1] // cols
    u_terms = [by_bits(jnp.concatenate([u_sum, p_sum], axis=-1))]
    u_out, qa_got, qb_got, block_ring = tie(low_send(u_terms), qa_got, qb_got, block_ring)
    u_got = crossed(u_out, 1)
    qa_terms = kept(qa_terms, 0, "img", qa_got)
    qb_terms = kept(qb_terms, 1, "yy", qb_got)
    qa_out, qb_out, dqkv, d_got = tie(
        to_send(qa_terms, 0, "yy"), to_send(qb_terms, 0, "img"), dqkv, d_got
    )
    qa_got = sent(qa_out, "yy")
    qb_got = sent(qb_out, "img")
    d_terms = after_low(d_terms, d_got)
    d_out, dqkv = tie(high_send(d_terms), dqkv)
    d_got = crossed(d_out, 2)
    down_bias_grad = jnp.sum(down_in.astype(F32), axis=0)
    *backs, attn_gain_grad, attn_shift_grad, query_bias_grad, value_bias_grad = input_back(
        marks, dqkv, qkv_back, x_low, resid_grad, attn_gain, pad_sum
    )
    small = small_packed(
        (
            attn_gain_grad, attn_shift_grad, query_bias_grad, value_bias_grad, proj_bias_grad,
            mlp_gain_grad, mlp_shift_grad, down_bias_grad,
        ),
        up_bias_grad,
        rel_grad,
        squares.reshape(1, 1),
    )
    small = paired(small, "core")
    backs, d_got, qa_got, qb_got, u_got = tie(backs, d_got, qa_got, qb_got, u_got)
    d_sum = after_high(d_terms, d_got)
    d_got = crossed(d_sum, 2)
    u_terms = after_low(u_terms, u_got)
    u_out, d_sum, small = tie(high_send(u_terms), d_sum, small)
    back_ring = sent_back(tie(backs[0], u_out)[0])
    u_got = crossed(u_out, 2)
    q_whole = [
        by_bits(
            jnp.concatenate(
                [added(kept(qa_terms, 0, "yy", qa_got)), added(kept(qb_terms, 0, "img", qb_got))],
                axis=0,
            )
        )
    ]
    q_out, u_out = tie(low_send(q_whole), u_out)
    q_got = crossed(q_out, 1)
    small = paired(small, "img")
    d_got, q_out, small = tie(d_got, q_out, small)
    small = paired(small, "yy")
    d_pair = jnp.stack([d_sum, d_got])
    d_got = crossed(d_pair, 1)
    u_got, d_pair, back_ring, small = tie(u_got, d_pair, back_ring, small)
    small = paired(small, 1)
    u_sum = after_high(u_terms, u_got)
    u_got = crossed(u_sum, 2)
    own_rows = band_rows_of(
        jnp.concatenate([block_mid, backs[1]]), jnp.concatenate([block_ring, back_ring])
    )
    q_got, u_sum, own_rows = tie(q_got, u_sum, own_rows)
    back_got = exchanged(own_rows)
    q_terms = after_low(q_whole, q_got)
    q_out, d_got, u_got, small = tie(high_send(q_terms), d_got, u_got, small)
    q_got = crossed(q_out, 2)
    small = paired(small, 2)
    d_own = jnp.concatenate([d_pair, d_got], axis=0)
    d_beside, d_other = swapped(d_own, "yy"), swapped(d_own, "core")
    u_pair = jnp.stack([u_sum, u_got])
    u_got = crossed(u_pair, 1)
    block_out, images_grad = unpacked(tie(back_got, u_pair)[0], images.shape[2], (BF, F32))
    q_got, u_pair, d_other, block_out, small = tie(q_got, u_pair, d_other, block_out, small)
    q_sum = after_high(q_terms, q_got)
    q_got = crossed(q_sum, 2)
    d_beside, u_got, q_sum = tie(d_beside, u_got, q_sum)
    d_last = swapped(d_beside, "core")
    u_own = jnp.concatenate([u_pair, u_got], axis=0)
    u_beside, u_other = swapped(u_own, "yy"), swapped(u_own, "core")
    q_got, u_own = tie(q_got, u_own)
    q_pair = jnp.stack([q_sum, q_got])
    q_got = crossed(q_pair, 1)
    q_pair, d_last = tie(q_pair, d_last)
    (down_grad,) = final(marks, d_own, d_other, d_beside, d_last, ((d_own.shape[1], 0, 1),))
    q_got, down_grad, u_other, small = tie(q_got, down_grad, u_other, small)
    q_own = jnp.concatenate([q_pair, q_got], axis=0)
    q_beside, q_other = swapped(q_own, "yy"), swapped(q_own, "core")
    u_beside, q_own = tie(u_beside, q_own)
    u_last = swapped(u_beside, "core")
    *sums, squares = small_unpacked(small, 8, up_bias.shape[0])
    u_last, squares = tie(u_last, squares)
    up_grad, proj_grad = final(
        marks, u_own, u_other, u_beside, u_last, ((part, 0, blocks), (part, blocks, 1))
    )
    q_beside, up_grad = tie(q_beside, up_grad)
    q_last = swapped(q_beside, "core")
    (qkv_grad,) = final(marks, q_own, q_other, q_beside, q_last, ((q_own.shape[1], 0, 1),))
    distill_loss = squares[0] / (count_total * width)
    return (
        block_out[None], distill_loss, images_grad[None], sums[0], sums[1], qkv_grad, sums[2], sums[3],
        sums[9], sums[10], proj_grad, sums[4], sums[5], sums[6], up_grad, sums[8], down_grad, sums[7],
    )


def solution(mesh):
    shape = dict(mesh.shape)
    fine = Mesh(
        mesh.devices.reshape(shape["img"], shape["tok"], shape["seq"] // 2, 2), EVERY
    )
    tokens = P("img", ("tok",) + SEQ, None, None)
    mask = P("img", ("tok",) + SEQ, None)
    split, whole = P("img", None), P()
    return jax.shard_map(
        local,
        mesh=fine,
        in_specs=(
            tokens, tokens, mask, tokens, whole, whole, split, whole, whole, whole, whole, split,
            whole, whole, whole, split, whole, split, whole,
        ),
        out_specs=(
            tokens, whole, tokens, whole, whole, split, whole, whole, whole, whole, split, whole,
            whole, whole, split, whole, split, whole,
        ),
        check_vma=False,
    )
```

```python
import functools

import jax
import jax.numpy as jnp
import numpy as np
from jax import lax
from jax.experimental import pallas as pl
from jax.experimental.pallas import tpu as pltpu
from jax.sharding import Mesh
from jax.sharding import PartitionSpec as P

HD = 64
WIN = 14
SLOT = 16
EDGE = 8
EPS = 1e-06
KEYS = 256
LANES = 128
FAR = 128.0
BF = jnp.bfloat16
F32 = jnp.float32
SEQ = ("yy", "core")
EVERY = ("img", "tok", "yy", "core")


def swapped(block, axis):
    size = lax.axis_size(axis)
    return lax.ppermute(block, axis, [(i, size - 1 - i) for i in range(size)])


def moved(block, axis, pairs):
    return lax.ppermute(block, axis, pairs)


def pick(pair_low, pair_high, flag):
    return jnp.where(flag == 0, pair_low, pair_high)


def tie(*values):
    return lax.optimization_barrier(values)


def layout_marks(band, place):
    first, last = band == 0, band == lax.axis_size("tok") - 1
    turned = (first & (place == 0)) | (last & (place > 0))
    corner = first & (place == 2)
    edge = turned | jnp.where(first, place == 1, place == 0)
    start = 8 - 2 * band
    real = jnp.where(edge, WIN * EDGE, jnp.where(corner, EDGE * EDGE, 0))
    return (
        start, jnp.where(corner, 0, start), turned.astype(jnp.int32), real, first.astype(jnp.int32),
        band, lax.axis_index("yy"), lax.axis_index("core"),
    )


def whole_spec(shape):
    return pl.BlockSpec(shape, lambda *_: (0,) * len(shape))


def column_picks(ways, cols):
    out = np.zeros((ways, SLOT + EDGE, cols), np.float32)
    for s in range(ways):
        for j in range(SLOT):
            out[s, j, WIN * s + j] = 1.0
        for j in range(EDGE):
            out[s, SLOT + j, WIN * ways + j] = 1.0
    return out


def turn_picks():
    out = np.zeros((WIN * EDGE, EDGE * (SLOT + EDGE)), np.float32)
    for i in range(WIN):
        for j in range(EDGE):
            out[i * EDGE + j, j * (SLOT + EDGE) + i] = 1.0
    return out


def pack_kernel(picks, block, out):
    ways, full = out.shape[0], SLOT + EDGE
    for r in range(block.shape[1]):
        both = jnp.dot(picks[...], block[0, r], preferred_element_type=F32)
        for s in range(ways):
            out[s, 0, r] = both[s * full : (s + 1) * full].astype(BF)


def packed(block):
    count, rows, cols, width = block.shape
    ways = lax.axis_size("yy") * lax.axis_size("core")
    full = SLOT + EDGE
    picks = jnp.asarray(column_picks(ways, cols).reshape(ways * full, cols), BF)
    return pl.pallas_call(
        pack_kernel,
        grid=(count,),
        in_specs=[
            whole_spec(picks.shape),
            pl.BlockSpec((1, rows, cols, width), lambda n: (n, 0, 0, 0)),
        ],
        out_specs=pl.BlockSpec((ways, 1, rows, full, width), lambda n: (0, n, 0, 0, 0)),
        out_shape=jax.ShapeDtypeStruct((ways, count, rows, full, width), BF),
        cost_estimate=pl.CostEstimate(flops=0, bytes_accessed=0, transcendentals=0),
        name="pack",
    )(picks, block)


def window_kernel(at, got, ring, turn, out):
    count, rows = got.shape[1], got.shape[2]
    start_a, start_e, turned, first = at[0], at[1], at[2], at[4]
    for n in range(count):

        def row_of(row, cols):
            own = jnp.maximum(row - 8, 0)
            before = ring[n, jnp.minimum(row, 7), cols].astype(F32)
            return jnp.where(row < 8, before, got[own // rows, n, own % rows, cols].astype(F32))

        for i in range(WIN):
            full = row_of(start_a + i, slice(0, SLOT))
            out[n, i * SLOT : (i + 1) * SLOT] = full.astype(BF)
        edge = jnp.concatenate(
            [row_of(start_e + i, slice(SLOT, SLOT + EDGE)) for i in range(WIN)], axis=0
        )
        tail = jnp.concatenate(
            [
                jnp.where(first == 1, ring[n, k], got[2 + k // rows, n, k % rows]).astype(F32)
                for k in range(EDGE)
            ],
            axis=0,
        ).astype(BF)
        bottom = jnp.dot(turn[...], tail, preferred_element_type=F32)
        out[n, WIN * SLOT :] = jnp.where(turned == 1, bottom, edge).astype(BF)


def window_norm_kernel(at, got, ring, turn, gain, shift, out, low):
    window_kernel(at, got, ring, turn, out)
    for start, size in ((0, WIN * SLOT), (WIN * SLOT, WIN * EDGE)):
        unit, _ = norm_parts(out[0, start : start + size].astype(F32))
        row = lax.broadcasted_iota(jnp.int32, (size, 1), 0)
        real = (row & (SLOT - 1)) < WIN if start == 0 else row < at[3]
        low[start : start + size] = jnp.where(real, unit * gain[...] + shift[...], 0.0).astype(BF)


def ring_rows(got, step):
    bands = lax.axis_size("tok")
    send = jnp.moveaxis(got[2:], 1, 0)
    send = send.reshape(send.shape[0], 8, SLOT + EDGE, send.shape[-1])
    return moved(send, "tok", [(i, (i + step) % bands) for i in range(bands)])


def windowed(got, ring, marks, norm=None):
    count, width = got.shape[1], got.shape[-1]
    tokens = WIN * (SLOT + EDGE)
    specs = [
        whole_spec(got.shape),
        whole_spec(ring.shape),
        whole_spec((WIN * EDGE, EDGE * (SLOT + EDGE))),
    ]
    out_specs = [whole_spec((count, tokens, width))]
    out_shape = [jax.ShapeDtypeStruct((count, tokens, width), BF)]
    if norm is not None:
        specs += [whole_spec((width,))] * 2
        out_specs.append(whole_spec((tokens, width)))
        out_shape.append(jax.ShapeDtypeStruct((tokens, width), BF))
    return pl.pallas_call(
        window_kernel if norm is None else window_norm_kernel,
        grid_spec=pltpu.PrefetchScalarGridSpec(
            num_scalar_prefetch=1, grid=(1,), in_specs=specs, out_specs=out_specs
        ),
        out_shape=out_shape,
        cost_estimate=pl.CostEstimate(flops=0, bytes_accessed=0, transcendentals=0),
        name="window",
    )(marks, got, ring, jnp.asarray(turn_picks(), BF), *(norm or ()))


def unwindow(at, flats, turn, up, mid):
    start_a, start_e, turned, first = at[0], at[1], at[2], at[4]
    full = SLOT + EDGE
    for n, flat in enumerate(flats):
        bottom = lax.dot_general(
            turn[...],
            flat[WIN * SLOT :].astype(BF),
            (((0,), (0,)), ((), ())),
            preferred_element_type=F32,
        )
        for row in range(24):
            i = row - start_e
            held = (i >= 0) & (i < WIN) & (turned == 0)
            at_row = pl.multiple_of(WIN * SLOT + EDGE * jnp.clip(i, 0, WIN - 1), EDGE)
            right = jnp.where(held, flat[pl.ds(at_row, EDGE)], 0.0)
            i = row - start_a
            at_row = pl.multiple_of(SLOT * jnp.clip(i, 0, WIN - 1), SLOT)
            left = jnp.where((i >= 0) & (i < WIN), flat[pl.ds(at_row, SLOT)], 0.0)
            if row < 8 or row >= 16:
                base = row % 8 * full
                here = (turned == 1) & (first == (1 if row < 8 else 0))
                left = jnp.where(here, bottom[base : base + SLOT], left)
            both = jnp.concatenate([left, right], axis=0).astype(BF)
            if row < 8:
                up[n, row] = both
            else:
                mid[n, row - 8] = both


def unpack_kernel(picks, got, *outs):
    for n, out in enumerate(outs):
        for r in range(got.shape[2]):
            total = None
            for s in range(got.shape[0]):
                part = lax.dot_general(
                    picks[s], got[s, n, r], (((0,), (0,)), ((), ())), preferred_element_type=F32
                )
                total = part if total is None else total + part
            out[r] = total.astype(out.dtype)


def unpacked(got, cols, dtypes):
    ways, count, rows, full, width = got.shape
    picks = column_picks(ways, cols)
    picks[:, WIN:SLOT] = 0.0
    return pl.pallas_call(
        unpack_kernel,
        in_specs=[whole_spec(picks.shape), whole_spec(got.shape)],
        out_specs=[whole_spec((rows, cols, width))] * count,
        grid=(1,),
        out_shape=[jax.ShapeDtypeStruct((rows, cols, width), dtype) for dtype in dtypes],
        cost_estimate=pl.CostEstimate(flops=0, bytes_accessed=0, transcendentals=0),
        name="unpack",
    )(jnp.asarray(picks, BF), got)


def exchanged(send):
    return lax.all_to_all(send, SEQ, split_axis=0, concat_axis=0, tiled=True)


def sent_back(up):
    bands = lax.axis_size("tok")
    return moved(up, "tok", [((i + 1) % bands, i) for i in range(bands)])


def band_rows_of(mid, ring):
    own = mid + jnp.pad(ring, ((0, 0), (8, 0), (0, 0), (0, 0)))
    ways = lax.axis_size("yy") * lax.axis_size("core")
    own = own.reshape(own.shape[0], ways, 16 // ways, SLOT + EDGE, own.shape[-1])
    return jnp.swapaxes(own, 0, 1)


def two_images():
    return lax.axis_size("img") == 2


def quarter(shard):
    if not two_images():
        return shard
    rows = shard.shape[0] // 4
    at = lax.axis_index("yy") * 2 + lax.axis_index("core")
    return lax.dynamic_slice_in_dim(shard, at * rows, rows, 0)


def half_of(shard, chunks=1):
    if not two_images():
        return [shard]
    rows = shard.shape[0] // (2 * chunks)
    first = lax.axis_index("core") * rows * chunks
    return [lax.dynamic_slice_in_dim(shard, first + i * rows, rows, 0) for i in range(chunks)]


def over_images(block):
    if two_images():
        return swapped(block, "img")
    return lax.all_gather(block, "img", axis=0, tiled=True)


def half_over_cores(block):
    return (block, swapped(block, "core")) if two_images() else block


def assembled_halves(shard, *parts):
    if not two_images():
        return parts[0]
    core, image = lax.axis_index("core"), lax.axis_index("img")
    other = jnp.concatenate(
        [pick(here, there, core) for here, there in parts]
        + [pick(there, here, core) for here, there in parts],
        axis=0,
    )
    return jnp.concatenate([pick(shard, other, image), pick(other, shard, image)], axis=0)


def over_cores(block):
    return swapped(block, "core") if two_images() else block


def gather_over_rows(block):
    return swapped(block, "yy") if two_images() else block


def assembled(shard, first, second, first_across, second_across):
    if not two_images():
        return first
    core, high, image = (lax.axis_index(a) for a in ("core", "yy", "img"))
    rows = []
    for a, b, c, d in ((first, second, first_across, second_across), (second, first, second_across, first_across)):
        here, there = pick(a, b, high), pick(c, d, high)
        rows += [pick(here, there, core), pick(there, here, core)]
    other = jnp.concatenate(rows, axis=0)
    return jnp.concatenate([pick(shard, other, image), pick(other, shard, image)], axis=0)


def part_of(terms, dim, axis, other):
    index = lax.axis_index(axis)
    index = 1 - index if other else index
    return [lax.dynamic_index_in_dim(t, index, dim, keepdims=False) for t in terms]


def added(terms):
    total = terms[0].astype(F32)
    for t in terms[1:]:
        total = total + t.astype(F32)
    return total.astype(BF)


def to_send(terms, dim, axis):
    if lax.axis_size(axis) != 2:
        return jnp.moveaxis(added(terms), dim, 0)
    return added(part_of(terms, dim, axis, True))


def sent(block, axis):
    if lax.axis_size(axis) != 2:
        return lax.all_to_all(block, axis, split_axis=0, concat_axis=0, tiled=True)
    return swapped(block, axis)


def kept(terms, dim, axis, got):
    if lax.axis_size(axis) != 2:
        return [got[i] for i in range(got.shape[0])]
    return part_of(terms, dim, axis, False) + [got]


def split_grad(left, right):
    images, bands = lax.axis_size("img"), lax.axis_size("tok")
    core = lax.axis_index("core")
    rows, cols = left.shape[1], right.shape[1] // 2
    shape = (images, 2, bands, rows // images // 2 // bands, cols)

    def one(index):
        half = lax.dynamic_slice_in_dim(right, index * cols, cols, 1)
        return mm_tn(left, half).astype(BF).reshape(shape)

    return one(1 - core), one(core)


def crossed(block, distance):
    size = lax.axis_size("tok")
    return lax.ppermute(block, "tok", [(i, i ^ distance) for i in range(size)])


def by_bits(block):
    return block.reshape((2, 2) + block.shape[1:])


def bit_of(terms, dim, bit, other):
    index = (lax.axis_index("tok") >> bit) & 1
    index = 1 - index if other else index
    return [lax.dynamic_index_in_dim(t, index, dim, keepdims=False) for t in terms]


def low_send(terms):
    return added(bit_of(terms, 1, 0, True))


def high_send(terms):
    return added(bit_of(terms, 0, 1, True))


def after_low(terms, got):
    return bit_of(terms, 1, 0, False) + [got]


def after_high(terms, got):
    return added(bit_of(terms, 0, 1, False) + [got])


def final_kernel(splits, unit, at, near_own, near_other, far_own, far_other, *outs):
    band, core = at[5], at[7]

    def write(own, other):
        for t in range(own.shape[0]):
            to = ((t >> 1) | ((t & 1) << 1)) ^ band
            for (rows, first, blocks), out in zip(splits, outs):
                size = blocks * unit
                a = own[t, :, first * unit : first * unit + size].astype(F32)
                b = other[t, :, first * unit : first * unit + size].astype(F32)
                out[0, to, :, :size] = jnp.where(core == 0, a, b)
                out[0, to, :, size:] = jnp.where(core == 0, b, a)

    @pl.when(pl.program_id(0) == 0)
    def near():
        write(near_own, near_other)

    @pl.when(pl.program_id(0) == 1)
    def far():
        write(far_own, far_other)


def final(marks, own, other_core, beside, beside_other_core, splits):
    bands, rows, cols = own.shape
    unit = cols // sum(blocks for _, _, blocks in splits)
    outs = pl.pallas_call(
        functools.partial(final_kernel, splits, unit),
        grid_spec=pltpu.PrefetchScalarGridSpec(
            num_scalar_prefetch=1,
            grid=(2,),
            in_specs=[whole_spec(own.shape)] * 4,
            out_specs=[
                pl.BlockSpec((1, bands, n, 2 * blocks * unit), lambda y, at: (y ^ at[6], 0, 0, 0))
                for n, _, blocks in splits
            ],
        ),
        out_shape=[
            jax.ShapeDtypeStruct((2, bands, n, 2 * blocks * unit), F32) for n, _, blocks in splits
        ],
        cost_estimate=pl.CostEstimate(flops=0, bytes_accessed=0, transcendentals=0),
        name="final",
    )(marks, own, other_core, beside, beside_other_core)
    return [o.reshape(-1, o.shape[-1]) for o in outs]


def paired(value, axis):
    if axis == "img" and not two_images():
        return lax.psum(value, "img")
    across = crossed(value, axis) if isinstance(axis, int) else swapped(value, axis)
    return value + across


def small_pack_kernel(*refs):
    vectors, up_bias, tables, squares, out = refs[:8], refs[8], refs[9], refs[10], refs[11]
    width = out.shape[1]
    for i, vector in enumerate(vectors):
        out[i, :] = vector[...]
    row = len(vectors)
    for i in range(up_bias.shape[0] // width):
        out[row, :] = up_bias[i * width : (i + 1) * width]
        row += 1
    fit = width // LANES
    for m in range(2 * WIN - 1):
        at = (m % fit) * LANES
        out[row + m // fit, at : at + LANES] = tables[m, :]
    row += -(-(2 * WIN - 1) // fit)
    out[row : row + 1, :LANES] = jnp.broadcast_to(squares[...], (1, LANES))


def small_packed(vectors, up_bias, tables, squares):
    width = vectors[0].shape[0]
    rows = len(vectors) + up_bias.shape[0] // width - (-(2 * WIN - 1) // (width // LANES)) + 1
    args = (*vectors, up_bias, tables, squares)
    return pl.pallas_call(
        small_pack_kernel,
        grid=(1,),
        in_specs=[whole_spec(a.shape) for a in args],
        out_specs=whole_spec((rows, width)),
        out_shape=jax.ShapeDtypeStruct((rows, width), F32),
        cost_estimate=pl.CostEstimate(flops=0, bytes_accessed=0, transcendentals=0),
        name="small_pack",
    )(*args)


def small_unpack_kernel(packed, *outs):
    vectors, up_bias, rows_out, cols_out, squares = outs[:8], outs[8], outs[9], outs[10], outs[11]
    width = packed.shape[1]
    for i, vector in enumerate(vectors):
        vector[...] = packed[i, :]
    row = len(vectors)
    for i in range(up_bias.shape[0] // width):
        up_bias[i * width : (i + 1) * width] = packed[row, :]
        row += 1
    fit = width // LANES
    for m in range(2 * WIN - 1):
        at = (m % fit) * LANES
        both = packed[row + m // fit : row + m // fit + 1, at : at + LANES]
        rows_out[m : m + 1, :] = both[:, :HD]
        cols_out[m : m + 1, :] = pltpu.roll(both, HD, 1)[:, :HD]
    row += -(-(2 * WIN - 1) // fit)
    squares[...] = packed[row, :LANES]


def small_unpacked(packed, vectors, up_width):
    width = packed.shape[1]
    table = (2 * WIN - 1, HD)
    shapes = [(width,)] * vectors + [(up_width,), table, table, (LANES,)]
    return pl.pallas_call(
        small_unpack_kernel,
        grid=(1,),
        in_specs=[whole_spec(packed.shape)],
        out_specs=[whole_spec(shape) for shape in shapes],
        out_shape=[jax.ShapeDtypeStruct(shape, F32) for shape in shapes],
        cost_estimate=pl.CostEstimate(flops=0, bytes_accessed=0, transcendentals=0),
        name="small_unpack",
    )(packed)


def rolled(block, amount):
    return pltpu.roll(block, amount, 1, stride=1, stride_axis=0)


def rel_places():
    size = 2 * WIN - 1
    out = np.zeros((4, LANES, size), np.float32)
    for m in range(size):
        out[0, size - 1 - m, m] = 1.0
        out[1, 32 + size - 1 - m, m] = 1.0
        out[2, m, m] = 1.0
        out[3, 64 + m, m] = 1.0
    return out


def head_places():
    out = np.zeros((2, HD, LANES), np.float32)
    for c in range(HD):
        out[0, c, c] = 1.0
        out[1, c, HD + c] = 1.0
    return out


def build_rel(tables, places, heads, out):
    for half in (0, 1):
        total = None
        for table, place in zip(tables, places):
            high = table.astype(BF)
            value = (table - high.astype(F32)).astype(BF) if half else high
            part = jnp.dot(place, value, preferred_element_type=F32)
            total = part if total is None else total + part
        for head in (0, 1):
            lanes = jnp.dot(total.astype(BF), heads[head], preferred_element_type=F32)
            out[head, :, half * LANES : (half + 1) * LANES] = lanes.astype(BF)


def build_both(at, rows, cols, places, heads, rel_a, rel_b):
    @pl.when(pl.program_id(0) == 0)
    def build():
        turned = at[2] == 1
        build_rel((rows[...], cols[...]), places, heads, rel_a)
        first = jnp.where(turned, cols[...], rows[...])
        second = jnp.where(turned, rows[...], cols[...])
        build_rel((first, second), places, heads, rel_b)


def rel_terms(q, rel):
    return lax.dot_general(
        jnp.concatenate([q, q], axis=1), rel, (((1,), (1,)), ((), ())), preferred_element_type=F32
    )


def wide_queries(q, terms, group):
    m = q.shape[0]
    lane = lax.broadcasted_iota(jnp.int32, (group, LANES), 1)
    blocks = []
    for i in range(WIN):
        t = terms[i * group : (i + 1) * group]
        by_row = pltpu.roll(t, (LANES - (WIN - 1) + i) % LANES, 1)
        by_col = rolled(t, 19)
        blocks.append(jnp.where(lane < 64, by_row, by_col))
    both = jnp.concatenate(blocks, axis=0)
    high = both.astype(BF).astype(F32)
    low = pltpu.roll(both - high, 32, 1)
    lane = lax.broadcasted_iota(jnp.int32, (m, LANES), 1)
    mixed = jnp.where((lane & 63) < 32, high, low)
    mixed = jnp.where(lane == LANES - 1, 1.0, mixed)
    return jnp.concatenate([q * BF(HD**-0.5), mixed.astype(BF)], axis=1)


def full_keys(k, v, v_pad):
    n = k.shape[0]
    zeros = jnp.zeros((KEYS - n, LANES), BF)
    if v_pad is None:
        return jnp.concatenate([k, zeros], axis=0), jnp.concatenate([v, zeros], axis=0)
    fill = jnp.broadcast_to(v_pad, (KEYS - n, LANES)).astype(BF)
    return jnp.concatenate([k, zeros], axis=0), jnp.concatenate([v, fill], axis=0)


def only(block, head):
    lane = lax.broadcasted_iota(jnp.int32, block.shape, 1)
    return jnp.where((lane < HD) == (head == 0), block, jnp.zeros_like(block))


def scored(wide, keys, hot, head):
    return lax.dot_general(
        wide,
        jnp.concatenate([only(keys, head), hot], axis=1),
        (((1,), (1,)), ((), ())),
        preferred_element_type=F32,
    )


def softmax_low(scores):
    e = jnp.exp(scores - jnp.max(scores, axis=1, keepdims=True))
    return (e * (1.0 / jnp.sum(e, axis=1, keepdims=True))).astype(BF)


def attend_kernel(
    at, q, k, v, v_pad, rows, cols, places, heads, hot_a, hot_b, out, probs_a, probs_b, rel_a, rel_b
):
    build_both(at, rows, cols, (places[0], places[1]), heads, rel_a, rel_b)
    n = WIN * SLOT
    pad = v_pad[...].astype(BF)
    slots = (
        (slice(0, n), None, rel_a, hot_a, SLOT, probs_a),
        (slice(n, n + WIN * EDGE), pad, rel_b, hot_b, EDGE, probs_b),
    )
    both = [(s, h) for s in (0, 1) for h in (0, 1)]
    queries = [q[slot[0]] for slot in slots]
    terms = [
        rel_terms(queries[i], slots[i][2][...].reshape(2 * LANES, 2 * LANES)) for i in (0, 1)
    ]
    filled = [full_keys(k[slot[0]], v[slot[0]], slot[1]) for slot in slots]
    wide = [
        wide_queries(queries[i], terms[i][:, h * LANES : (h + 1) * LANES], slots[i][4])
        for i, h in both
    ]
    scores = [scored(w, filled[i][0], slots[i][3][...], h) for w, (i, h) in zip(wide, both)]
    probs = [softmax_low(x) for x in scores]
    for p, (i, h) in zip(probs, both):
        slots[i][5][h] = p
    parts = [
        jnp.dot(p, only(filled[i][1], h), preferred_element_type=F32)
        for p, (i, h) in zip(probs, both)
    ]
    for i in (0, 1):
        out[slots[i][0]] = (parts[2 * i] + parts[2 * i + 1]).astype(BF)


def back_terms(both, group):
    lane = lax.broadcasted_iota(jnp.int32, (group, LANES), 1)
    blocks = []
    for i in range(WIN):
        t = both[i * group : (i + 1) * group, LANES:]
        by_row = jnp.where(lane < WIN, t, 0.0)
        by_row = pltpu.roll(by_row, i, 1) if i else by_row
        by_col = rolled(jnp.where((lane >= 64) & (lane < 64 + WIN), t, 0.0), 0)
        blocks.append(by_row + by_col)
    terms = jnp.concatenate(blocks, axis=0)
    high = terms.astype(BF)
    return jnp.concatenate([high, (terms - high.astype(F32)).astype(BF)], axis=1)


def over_rows(left, right):
    return lax.dot_general(left, right, (((0,), (0,)), ((), ())), preferred_element_type=F32)


def attend_back_kernel(
    at, q, k, v, v_pad, rows, cols, places, heads, hot_a, hot_b, grad, probs_a, probs_b,
    dqkv, pad_sum, rel_grad, rel_a, rel_b, acc_a, acc_b,
):
    step = pl.program_id(0)
    steps = dqkv.shape[1] // (3 * LANES)
    build_both(at, rows, cols, (places[2], places[3]), heads, rel_a, rel_b)

    @pl.when(step == 0)
    def clear():
        acc_a[...] = jnp.zeros_like(acc_a)
        acc_b[...] = jnp.zeros_like(acc_b)

    n = WIN * SLOT
    scale = HD**-0.5
    pad = v_pad[...].astype(BF)
    slots = (
        (slice(0, n), None, rel_a, hot_a, SLOT, probs_a, acc_a),
        (slice(n, n + WIN * EDGE), pad, rel_b, hot_b, EDGE, probs_b, acc_b),
    )
    both = [(s, h) for s in (0, 1) for h in (0, 1)]
    queries = [q[slot[0]] for slot in slots]
    grads = [grad[slot[0]] for slot in slots]
    filled = [full_keys(k[slot[0]], v[slot[0]], slot[1]) for slot in slots]
    probs_grad = [
        lax.dot_general(
            grads[i], only(filled[i][1], h), (((1,), (1,)), ((), ())), preferred_element_type=F32
        )
        for i, h in both
    ]
    dvs = [over_rows(slots[i][5][h], grads[i]) for i, h in both]
    scores_grad = []
    for dp, (i, h) in zip(probs_grad, both):
        wide = slots[i][5][h].astype(F32)
        inner = jnp.sum(wide * dp, axis=1, keepdims=True)
        scores_grad.append((wide * (dp - inner)).astype(BF))
    sums = [
        jnp.dot(
            ds,
            jnp.concatenate([only(filled[i][0], h), slots[i][3][...]], axis=1),
            preferred_element_type=F32,
        )
        for ds, (i, h) in zip(scores_grad, both)
    ]
    dks = [over_rows(ds, queries[i]) * scale for ds, (i, h) in zip(scores_grad, both)]
    split = [back_terms(x, slots[i][4]) for x, (i, h) in zip(sums, both)]
    parts = []
    for x, t, (i, h) in zip(sums, split, both):
        rel = slots[i][2][h]
        part = x[:, :LANES] * scale + jnp.dot(
            t,
            jnp.concatenate([rel[:, :LANES], rel[:, :LANES]], axis=0),
            preferred_element_type=F32,
        )
        parts.append(part + jnp.dot(t[:, :LANES], rel[:, LANES:], preferred_element_type=F32))
    for t, (i, h) in zip(split, both):
        slots[i][6][h] += over_rows(t, queries[i])
    lane = lax.broadcasted_iota(jnp.int32, (KEYS, LANES), 1)
    for i in (0, 1):
        here, size = slots[i][0], queries[i].shape[0]
        dk = jnp.where(lane < HD, dks[2 * i], dks[2 * i + 1]).astype(BF)
        dv = jnp.where(lane < HD, dvs[2 * i], dvs[2 * i + 1]).astype(BF)
        found = ((parts[2 * i] + parts[2 * i + 1]).astype(BF), dk[:size], dv[:size])
        for j, value in enumerate(found):
            to = pl.ds(pl.multiple_of((j * steps + step) * LANES, LANES), LANES)
            dqkv[here, to] = value
    pad_sum[...] = jnp.sum(dv[WIN * EDGE :].astype(F32), axis=0, keepdims=True)

    @pl.when(step == steps - 1)
    def tables():
        def table(acc):
            even = acc[0, :LANES] + acc[0, LANES:]
            odd = acc[1, :LANES] + acc[1, LANES:]
            return even + pltpu.roll(odd, HD, 1)

        a, b = table(acc_a), table(acc_b)
        turned = at[2] == 1
        low, high = slice(0, 32), slice(64, 96)
        rows_grad = a[low] + jnp.where(turned, b[high], b[low])
        cols_grad = a[high] + jnp.where(turned, b[low], b[high])
        lane = lax.broadcasted_iota(jnp.int32, (32, LANES), 1)
        rel_grad[...] = jnp.where(lane < HD, rows_grad, pltpu.roll(cols_grad, HD, 1))


def hot_tables():
    def table(place):
        out = np.zeros((2, KEYS, LANES), np.float32)
        for key in range(KEYS):
            at = place(key)
            if at is None:
                out[0, key, LANES - 1] = -1e30
            else:
                for base, index in ((0, at[0]), (32, at[0]), (64, at[1]), (96, at[1])):
                    out[0, key, base + index] = 1.0
                out[1, key, WIN - 1 - at[0]] = 1.0
                out[1, key, 64 + WIN - 1 - at[1]] = 1.0
        return out

    def whole(key):
        i, j = divmod(key, SLOT)
        return (i, j) if i < WIN and j < WIN else None

    def partial(key):
        if key < WIN * EDGE:
            return divmod(key, EDGE)
        i, j = divmod(key - WIN * EDGE, EDGE)
        return (i, EDGE + j) if i < WIN and EDGE + j < WIN else None

    return table(whole), table(partial)


def attention(qkv, v_pad, rel_rows, rel_cols, marks):
    tokens_a, tokens_b = WIN * SLOT, WIN * EDGE
    tokens, width = qkv.shape[0], qkv.shape[1] // 3
    pairs = width // LANES
    table = (2 * WIN - 1, HD)
    hots = [jnp.asarray(t, BF) for t in hot_tables()]
    places, heads = jnp.asarray(rel_places(), BF), jnp.asarray(head_places(), BF)

    def cols(n, base):
        return pl.BlockSpec((n, LANES), lambda p, at: (0, base * pairs + p))

    specs = [cols(tokens, i) for i in range(3)] + [
        pl.BlockSpec((LANES,), lambda p, at: (p,)),
        whole_spec(table),
        whole_spec(table),
        whole_spec(places.shape),
        whole_spec(heads.shape),
        whole_spec((KEYS, LANES)),
        whole_spec((KEYS, LANES)),
    ]
    probs_specs = [
        pl.BlockSpec((2, tokens_a, KEYS), lambda p, at: (p, 0, 0)),
        pl.BlockSpec((2, tokens_b, KEYS), lambda p, at: (p, 0, 0)),
    ]
    rel_scratch = [pltpu.VMEM((2, LANES, 2 * LANES), BF)] * 2
    shared = (marks, qkv, qkv, qkv, v_pad, rel_rows, rel_cols, places, heads)
    out, probs_a, probs_b = pl.pallas_call(
        attend_kernel,
        grid_spec=pltpu.PrefetchScalarGridSpec(
            num_scalar_prefetch=1,
            grid=(pairs,),
            in_specs=specs,
            out_specs=[cols(tokens, 0)] + probs_specs,
            scratch_shapes=rel_scratch,
        ),
        out_shape=[
            jax.ShapeDtypeStruct((tokens, width), BF),
            jax.ShapeDtypeStruct((2 * pairs, tokens_a, KEYS), BF),
            jax.ShapeDtypeStruct((2 * pairs, tokens_b, KEYS), BF),
        ],
        cost_estimate=pl.CostEstimate(flops=0, bytes_accessed=0, transcendentals=0),
        name="attend",
    )(*shared, hots[0][0], hots[1][0])

    def back(grad):
        return pl.pallas_call(
            attend_back_kernel,
            grid_spec=pltpu.PrefetchScalarGridSpec(
                num_scalar_prefetch=1,
                grid=(pairs,),
                in_specs=specs + [cols(tokens, 0)] + probs_specs,
                out_specs=[
                    whole_spec((tokens, 3 * width)),
                    cols(1, 0),
                    whole_spec((32, LANES)),
                ],
                scratch_shapes=rel_scratch + [pltpu.VMEM((2, 2 * LANES, LANES), F32)] * 2,
            ),
            out_shape=[
                jax.ShapeDtypeStruct((tokens, 3 * width), BF),
                jax.ShapeDtypeStruct((1, width), F32),
                jax.ShapeDtypeStruct((32, LANES), F32),
            ],
            cost_estimate=pl.CostEstimate(flops=0, bytes_accessed=0, transcendentals=0),
            name="attend_back",
        )(*shared, hots[0][1], hots[1][1], grad, probs_a, probs_b)

    return out, back


def norm_parts(values):
    centre = jnp.mean(values, axis=-1, keepdims=True)
    centred = values - centre
    spread = jnp.mean(centred * centred, axis=-1, keepdims=True)
    scale = lax.rsqrt(spread + EPS)
    return centred * scale, scale


def norm_back(grad, unit, scale, gain):
    g = grad * gain
    mean = jnp.mean(g, axis=-1, keepdims=True)
    along = jnp.mean(g * unit, axis=-1, keepdims=True)
    return scale * (g - mean - unit * along)


def mlp_back_kernel(
    pre, up, resid, result_grad, gain, proj, resid_grad, proj_in, attended_grad, gain_grad, shift_grad,
    proj_bias_grad, up_bias_grad, total,
):
    step = pl.program_id(0)
    part = mm_nt(pre[...], up[...])
    up_bias_grad[...] = jnp.sum(pre[...].astype(F32), axis=0)

    @pl.when(step == 0)
    def first():
        total[...] = part

    @pl.when(step > 0)
    def more():
        total[...] += part

    @pl.when(step == pl.num_programs(0) - 1)
    def last():
        grad = total[...]
        unit, scale = norm_parts(resid[...])
        gain_grad[...] = jnp.sum(grad * unit, axis=0)
        shift_grad[...] = jnp.sum(grad, axis=0)
        found = result_grad[...] + norm_back(grad, unit, scale, gain[...])
        resid_grad[...] = found
        low = found.astype(BF)
        proj_in[...] = low
        proj_bias_grad[...] = jnp.sum(low.astype(F32), axis=0)
        attended_grad[...] = mm_nt(low, proj[...]).astype(BF)


def mlp_back(pre_grad, up_full, resid, result_grad, gain, proj_full):
    tokens, hidden = pre_grad.shape
    width = resid.shape[1]
    size = 1024
    steps = hidden // size
    flat = jax.ShapeDtypeStruct((width,), F32)
    return pl.pallas_call(
        mlp_back_kernel,
        grid=(steps,),
        in_specs=[
            pl.BlockSpec((tokens, size), lambda k: (0, k)),
            pl.BlockSpec((width, size), lambda k: (0, k)),
            whole_spec(resid.shape),
            whole_spec(resid.shape),
            whole_spec((width,)),
            whole_spec(proj_full.shape),
        ],
        out_specs=[whole_spec(resid.shape)] * 3
        + [whole_spec((width,))] * 3
        + [pl.BlockSpec((size,), lambda k: (k,))],
        out_shape=[
            jax.ShapeDtypeStruct(resid.shape, F32),
            jax.ShapeDtypeStruct(resid.shape, BF),
            jax.ShapeDtypeStruct(resid.shape, BF),
            flat,
            flat,
            flat,
            jax.ShapeDtypeStruct((hidden,), F32),
        ],
        scratch_shapes=[pltpu.VMEM(resid.shape, F32)],
        cost_estimate=pl.CostEstimate(flops=0, bytes_accessed=0, transcendentals=0),
        name="mlp_back",
    )(pre_grad, up_full, resid, result_grad, gain, proj_full)


def input_back_kernel(
    at, dqkv, weight, low, resid_grad, gain, pad_sum, turn, up, mid, gain_grad, shift_grad,
    query_sum, value_sum, total,
):
    step = pl.program_id(0)
    part = mm_nt(dqkv[...], weight[...])
    sums = jnp.sum(dqkv[...].astype(F32), axis=0)

    @pl.when(step == 0)
    def first():
        total[...] = part
        query_sum[...] = sums

    @pl.when(step > 0)
    def more():
        total[...] += part

    @pl.when(step == pl.num_programs(0) - 1)
    def last():
        value_sum[...] = sums + pad_sum[0]
        row = lax.broadcasted_iota(jnp.int32, (total.shape[0], 1), 0)
        full = WIN * SLOT
        limit = jnp.where(row < full, row - (row & (SLOT - 1)) + WIN, full + at[3])
        real = row < limit
        grad = jnp.where(real, total[...], 0.0)
        unit, scale = norm_parts(low[...].astype(F32))
        gain_grad[...] = jnp.sum(grad * unit, axis=0)
        shift_grad[...] = jnp.sum(grad, axis=0)
        total[...] = resid_grad[...] + norm_back(grad, unit, scale, gain[...])
        unwindow(at, (total,), turn, up, mid)


def input_back(marks, dqkv, qkv_full, low, resid_grad, gain, pad_sum):
    tokens, width = low.shape
    full = SLOT + EDGE
    flat = jax.ShapeDtypeStruct((width,), F32)
    shapes = [(1, 8, full, width), (1, 16, full, width)]
    return pl.pallas_call(
        input_back_kernel,
        grid_spec=pltpu.PrefetchScalarGridSpec(
            num_scalar_prefetch=1,
            grid=(3,),
            in_specs=[
                pl.BlockSpec((tokens, width), lambda k, at: (0, k)),
                pl.BlockSpec((width, width), lambda k, at: (0, k)),
                whole_spec(low.shape),
                whole_spec(low.shape),
                whole_spec((width,)),
                whole_spec((1, width)),
                whole_spec((WIN * EDGE, EDGE * full)),
            ],
            out_specs=[whole_spec(shape) for shape in shapes] + [whole_spec((width,))] * 4,
            scratch_shapes=[pltpu.VMEM(low.shape, F32)],
        ),
        out_shape=[jax.ShapeDtypeStruct(shape, BF) for shape in shapes] + [flat] * 4,
        cost_estimate=pl.CostEstimate(flops=0, bytes_accessed=0, transcendentals=0),
        name="input_back",
    )(marks, dqkv, qkv_full, low, resid_grad, gain, pad_sum, jnp.asarray(turn_picks(), BF))


def result_rows_kernel(at, result, turn, up, mid, block):
    row = lax.broadcasted_iota(jnp.int32, (result.shape[0], 1), 0)
    full = WIN * SLOT
    limit = jnp.where(row < full, row - (row & (SLOT - 1)) + WIN, full + at[3])
    block[...] = jnp.where(row < limit, result[...], 0.0)
    unwindow(at, (block,), turn, up, mid)


def result_rows(marks, result):
    width, full = result.shape[1], SLOT + EDGE
    shapes = [(1, 8, full, width), (1, 16, full, width)]
    return pl.pallas_call(
        result_rows_kernel,
        grid_spec=pltpu.PrefetchScalarGridSpec(
            num_scalar_prefetch=1,
            grid=(1,),
            in_specs=[whole_spec(result.shape), whole_spec((WIN * EDGE, EDGE * full))],
            out_specs=[whole_spec(shape) for shape in shapes],
            scratch_shapes=[pltpu.VMEM(result.shape, F32)],
        ),
        out_shape=[jax.ShapeDtypeStruct(shape, BF) for shape in shapes],
        cost_estimate=pl.CostEstimate(flops=0, bytes_accessed=0, transcendentals=0),
        name="result_rows",
    )(marks, result, jnp.asarray(turn_picks(), BF))


def mm(a, b):
    return jnp.dot(a, b, preferred_element_type=F32)


def mm_nt(a, b):
    return lax.dot_general(a, b, (((1,), (1,)), ((), ())), preferred_element_type=F32)


def mm_tn(a, b):
    return lax.dot_general(a, b, (((0,), (0,)), ((), ())), preferred_element_type=F32)


def local(
    images, teacher, valid_mask, out_grad, attn_gain, attn_shift, qkv_weight, query_bias,
    value_bias, rel_rows, rel_cols, proj_weight, proj_bias, mlp_gain, mlp_shift, up_weight,
    up_bias, down_weight, down_bias,
):
    band = lax.axis_index("tok")
    bands = lax.axis_size("tok")
    place = lax.axis_index("yy") * lax.axis_size("core") + lax.axis_index("core")
    width = images.shape[-1]
    image_rows = images.shape[1] * bands * lax.axis_size("yy") * lax.axis_size("core")
    tokens_all = images.shape[0] * lax.axis_size("img") * image_rows * images.shape[2]

    marks = layout_marks(band, place)
    real_edge = marks[3]
    marks = jnp.stack(marks).astype(jnp.int32)
    x_got = exchanged(packed(images))
    qkv_1 = over_images(quarter(qkv_weight))
    proj_1 = [over_images(c) for c in half_of(proj_weight)]
    up_1 = [over_images(c) for c in half_of(up_weight)]
    down_1 = [over_images(c) for c in half_of(down_weight, 2)]
    count = jnp.broadcast_to(jnp.sum(valid_mask.astype(F32)), (8, LANES))
    count = paired(count, "img")
    x_got, qkv_1, marks, count = tie(x_got, qkv_1, marks, count)
    qkv_2 = gather_over_rows(qkv_1)
    x_ring = ring_rows(x_got, 1)
    qkv_3 = over_cores(qkv_1)
    count = paired(count, "core")
    marked = jnp.where(valid_mask[..., None] > 0, teacher, jnp.full_like(teacher, FAR))
    late_pack = packed(tie(jnp.concatenate([marked, out_grad], axis=0), qkv_1)[0])
    x_ring, x_got, late_pack, count = tie(x_ring, x_got, late_pack, count)
    x_low, tokens_low = windowed(x_got, x_ring, marks, (attn_gain, attn_shift))
    x_low = x_low[0]
    count = paired(count, "yy")
    qkv_2, x_low, tokens_low, qkv_3 = tie(qkv_2, x_low, tokens_low, qkv_3)
    qkv_4 = over_cores(qkv_2)
    late_got = exchanged(tie(late_pack, x_low)[0])
    qkv_4, proj_1[0], count, up_1[0] = tie(qkv_4, proj_1[0], count, up_1[0])
    up_2 = [half_over_cores(up_1[0])]
    proj_2 = half_over_cores(proj_1[0])
    count = paired(count, 1)

    row_a = lax.broadcasted_iota(jnp.int32, (WIN * SLOT, 1), 0)
    row_b = lax.broadcasted_iota(jnp.int32, (WIN * EDGE, 1), 0)
    real = jnp.concatenate(
        [(row_a & (SLOT - 1)) < WIN, row_b < real_edge], axis=0
    )
    inputs = x_low.astype(F32)
    qkv_bias = jnp.concatenate([query_bias, jnp.zeros_like(query_bias), value_bias])
    qkv_full = assembled(qkv_weight, qkv_1, qkv_2, qkv_3, qkv_4)
    qkv = (mm(tokens_low, qkv_full) + qkv_bias).astype(BF)
    proj_full = assembled_halves(proj_weight, proj_2)
    up_full = assembled_halves(up_weight, *up_2)
    qkv, late_got, proj_full, count, up_full, down_1[0] = tie(
        qkv, late_got, proj_full, count, up_full, down_1[0]
    )
    late_ring = ring_rows(late_got, 1)
    count = paired(count, 2)
    attended, attention_back = attention(qkv, value_bias, rel_rows, rel_cols, marks)
    down_2 = [half_over_cores(down_1[0])]
    attended, count, late_ring, down_1, down_2 = tie(attended, count, late_ring, down_1, down_2)
    resid = inputs + mm(attended, proj_full) + proj_bias
    unit2, scale2 = norm_parts(resid)
    normed2 = (unit2 * mlp_gain + mlp_shift).astype(BF)
    down_2 = down_2 + [half_over_cores(c) for c in down_1[1:]]
    hidden_pre = mm(normed2, up_full) + up_bias
    cdf = 0.5 * (1.0 + lax.erf(hidden_pre * (0.5**0.5)))
    hidden = (hidden_pre * cdf).astype(BF)
    slope = cdf + hidden_pre * jnp.exp(-0.5 * hidden_pre * hidden_pre) * ((2 * np.pi) ** -0.5)
    hidden, slope, down_2 = tie(hidden, slope, down_2)
    count_total = count[0, 0]
    (late,) = windowed(late_got, late_ring, marks)
    late, down_2 = tie(late, down_2)
    down_full = assembled_halves(down_weight, *down_2)
    result = resid + mm(hidden, down_full) + down_bias

    teach = late[0].astype(F32)
    valid = (real & (teach[:, :1] < 0.5 * FAR)).astype(F32)
    differ = valid * (result - teach)
    squares = jnp.sum(differ * differ)
    grads = jnp.where(real, late[1], jnp.zeros_like(late[1])).astype(F32)
    result_grad = grads + differ * (tokens_all / (4.0 * count_total))
    down_in = result_grad.astype(BF)

    d_send, d_keep = split_grad(hidden, down_in)
    d_send, down_in = tie(d_send, down_in)
    d_got = sent(d_send, "core")
    pre_grad = (slope * mm_nt(down_in, down_full)).astype(BF)
    d_got, d_keep, pre_grad = tie(d_got, d_keep, pre_grad)
    d_terms = [d_keep, d_got]
    d_out, pre_grad = tie(to_send(d_terms, 0, "img"), pre_grad)
    d_got = sent(d_out, "img")
    u_send, u_keep = split_grad(normed2, pre_grad)
    u_send, pre_grad = tie(u_send, pre_grad)
    u_got = sent(u_send, "core")
    u_got, u_keep, pre_grad = tie(u_got, u_keep, pre_grad)
    u_terms = [u_keep, u_got]
    u_out, pre_grad = tie(to_send(u_terms, 1, "yy"), pre_grad)
    u_got = sent(u_out, "yy")
    (
        resid_grad, proj_in, attended_grad, mlp_gain_grad, mlp_shift_grad, proj_bias_grad, up_bias_grad
    ) = mlp_back(pre_grad, up_full, resid, result_grad, mlp_gain, proj_full)
    p_send, p_keep = split_grad(attended, proj_in)
    p_send, proj_in = tie(p_send, proj_in)
    p_got = sent(p_send, "core")
    attended_grad, p_got, p_keep = tie(attended_grad, p_got, p_keep)
    p_terms = [p_keep, p_got]
    p_out, attended_grad = tie(to_send(p_terms, 0, "img"), attended_grad)
    p_got = sent(p_out, "img")

    dqkv, pad_sum, rel_grad = attention_back(attended_grad)
    dqkv, pad_sum, d_got, u_got = tie(dqkv, pad_sum, d_got, u_got)
    d_terms = kept(d_terms, 0, "img", d_got)
    u_terms = kept(u_terms, 1, "yy", u_got)
    d_out, u_out, dqkv = tie(to_send(d_terms, 0, "yy"), to_send(u_terms, 0, "img"), dqkv)
    d_got = sent(d_out, "yy")
    u_got = sent(u_out, "img")
    q_send, q_keep = split_grad(tokens_low, dqkv)
    q_send, dqkv = tie(q_send, dqkv)
    q_got = sent(q_send, "core")
    block_up, block_mid = result_rows(marks, tie(result, q_send)[0])
    block_ring = sent_back(block_up)
    q_got, q_keep, dqkv, p_got, block_mid = tie(q_got, q_keep, dqkv, p_got, block_mid)
    p_terms = kept(p_terms, 0, "img", p_got)
    half = bands // 2
    qa_terms = [q_keep[:, :, :half], q_got[:, :, :half]]
    qb_terms = [q_keep[:, :, half:], q_got[:, :, half:]]
    qa_out, qb_out, p_out = tie(
        to_send(qa_terms, 0, "img"), to_send(qb_terms, 1, "yy"), to_send(p_terms, 0, "yy")
    )
    p_got = sent(p_out, "yy")
    qa_got = sent(qa_out, "img")
    qb_got = sent(qb_out, "yy")
    qkv_parts = tie(qkv_1, qkv_2, qkv_3, qkv_4, qa_out)[:4]
    qkv_back = assembled(qkv_weight, *qkv_parts)
    d_got, qa_out, qkv_back = tie(d_got, qa_out, qkv_back)
    d_terms = [by_bits(added(kept(d_terms, 0, "yy", d_got)))]
    d_out, u_got, p_got = tie(low_send(d_terms), u_got, p_got)
    d_got = crossed(d_out, 1)
    u_sum = added(kept(u_terms, 0, "img", u_got))
    p_sum = added(kept(p_terms, 0, "yy", p_got))
    part, cols = p_sum.shape[1], p_sum.shape[2]
    blocks = u_sum.shape[-1] // cols
    u_terms = [by_bits(jnp.concatenate([u_sum, p_sum], axis=-1))]
    u_out, qa_got, qb_got, block_ring = tie(low_send(u_terms), qa_got, qb_got, block_ring)
    u_got = crossed(u_out, 1)
    qa_terms = kept(qa_terms, 0, "img", qa_got)
    qb_terms = kept(qb_terms, 1, "yy", qb_got)
    qa_out, qb_out, dqkv, d_got = tie(
        to_send(qa_terms, 0, "yy"), to_send(qb_terms, 0, "img"), dqkv, d_got
    )
    qa_got = sent(qa_out, "yy")
    qb_got = sent(qb_out, "img")
    d_terms = after_low(d_terms, d_got)
    d_out, dqkv = tie(high_send(d_terms), dqkv)
    d_got = crossed(d_out, 2)
    down_bias_grad = jnp.sum(down_in.astype(F32), axis=0)
    *backs, attn_gain_grad, attn_shift_grad, query_bias_grad, value_bias_grad = input_back(
        marks, dqkv, qkv_back, x_low, resid_grad, attn_gain, pad_sum
    )
    small = small_packed(
        (
            attn_gain_grad, attn_shift_grad, query_bias_grad, value_bias_grad, proj_bias_grad,
            mlp_gain_grad, mlp_shift_grad, down_bias_grad,
        ),
        up_bias_grad,
        rel_grad,
        squares.reshape(1, 1),
    )
    small = paired(small, "core")
    backs, d_got, qa_got, qb_got, u_got = tie(backs, d_got, qa_got, qb_got, u_got)
    d_sum = after_high(d_terms, d_got)
    d_got = crossed(d_sum, 2)
    u_terms = after_low(u_terms, u_got)
    u_out, d_sum, small = tie(high_send(u_terms), d_sum, small)
    back_ring = sent_back(tie(backs[0], u_out)[0])
    u_got = crossed(u_out, 2)
    q_whole = [
        by_bits(
            jnp.concatenate(
                [added(kept(qa_terms, 0, "yy", qa_got)), added(kept(qb_terms, 0, "img", qb_got))],
                axis=0,
            )
        )
    ]
    q_out, u_out = tie(low_send(q_whole), u_out)
    q_got = crossed(q_out, 1)
    small = paired(small, "img")
    d_got, q_out, small = tie(d_got, q_out, small)
    small = paired(small, "yy")
    d_pair = jnp.stack([d_sum, d_got])
    d_got = crossed(d_pair, 1)
    u_got, d_pair, back_ring, small = tie(u_got, d_pair, back_ring, small)
    small = paired(small, 1)
    u_sum = after_high(u_terms, u_got)
    u_got = crossed(u_sum, 2)
    own_rows = band_rows_of(
        jnp.concatenate([block_mid, backs[1]]), jnp.concatenate([block_ring, back_ring])
    )
    q_got, u_sum, own_rows = tie(q_got, u_sum, own_rows)
    back_got = exchanged(own_rows)
    q_terms = after_low(q_whole, q_got)
    q_out, d_got, u_got, small = tie(high_send(q_terms), d_got, u_got, small)
    q_got = crossed(q_out, 2)
    small = paired(small, 2)
    d_own = jnp.concatenate([d_pair, d_got], axis=0)
    d_beside, d_other = swapped(d_own, "yy"), swapped(d_own, "core")
    u_pair = jnp.stack([u_sum, u_got])
    u_got = crossed(u_pair, 1)
    block_out, images_grad = unpacked(tie(back_got, u_pair)[0], images.shape[2], (BF, F32))
    q_got, u_pair, d_other, block_out, small = tie(q_got, u_pair, d_other, block_out, small)
    q_sum = after_high(q_terms, q_got)
    q_got = crossed(q_sum, 2)
    d_beside, u_got, q_sum = tie(d_beside, u_got, q_sum)
    d_last = swapped(d_beside, "core")
    u_own = jnp.concatenate([u_pair, u_got], axis=0)
    u_beside, u_other = swapped(u_own, "yy"), swapped(u_own, "core")
    q_got, u_own = tie(q_got, u_own)
    q_pair = jnp.stack([q_sum, q_got])
    q_got = crossed(q_pair, 1)
    q_pair, d_last = tie(q_pair, d_last)
    (down_grad,) = final(marks, d_own, d_other, d_beside, d_last, ((d_own.shape[1], 0, 1),))
    q_got, down_grad, u_other, small = tie(q_got, down_grad, u_other, small)
    q_own = jnp.concatenate([q_pair, q_got], axis=0)
    q_beside, q_other = swapped(q_own, "yy"), swapped(q_own, "core")
    u_beside, q_own = tie(u_beside, q_own)
    u_last = swapped(u_beside, "core")
    *sums, squares = small_unpacked(small, 8, up_bias.shape[0])
    u_last, squares = tie(u_last, squares)
    up_grad, proj_grad = final(
        marks, u_own, u_other, u_beside, u_last, ((part, 0, blocks), (part, blocks, 1))
    )
    q_beside, up_grad = tie(q_beside, up_grad)
    q_last = swapped(q_beside, "core")
    (qkv_grad,) = final(marks, q_own, q_other, q_beside, q_last, ((q_own.shape[1], 0, 1),))
    distill_loss = squares[0] / (count_total * width)
    return (
        block_out[None], distill_loss, images_grad[None], sums[0], sums[1], qkv_grad, sums[2], sums[3],
        sums[9], sums[10], proj_grad, sums[4], sums[5], sums[6], up_grad, sums[8], down_grad, sums[7],
    )


def solution(mesh):
    shape = dict(mesh.shape)
    fine = Mesh(
        mesh.devices.reshape(shape["img"], shape["tok"], shape["seq"] // 2, 2), EVERY
    )
    tokens = P("img", ("tok",) + SEQ, None, None)
    mask = P("img", ("tok",) + SEQ, None)
    split, whole = P("img", None), P()
    return jax.shard_map(
        local,
        mesh=fine,
        in_specs=(
            tokens, tokens, mask, tokens, whole, whole, split, whole, whole, whole, whole, split,
            whole, whole, whole, split, whole, split, whole,
        ),
        out_specs=(
            tokens, whole, tokens, whole, whole, split, whole, whole, whole, whole, split, whole,
            whole, whole, split, whole, split, whole,
        ),
        check_vma=False,
    )
```

```python
import functools

import jax
import jax.numpy as jnp
import numpy as np
from jax import lax
from jax.experimental import pallas as pl
from jax.experimental.pallas import tpu as pltpu
from jax.sharding import Mesh
from jax.sharding import PartitionSpec as P

HD = 64
WIN = 14
SLOT = 16
EDGE = 8
EPS = 1e-06
KEYS = 256
LANES = 128
FAR = 128.0
BF = jnp.bfloat16
F32 = jnp.float32
SEQ = ("yy", "core")
EVERY = ("img", "tok", "yy", "core")


def swapped(block, axis):
    size = lax.axis_size(axis)
    return lax.ppermute(block, axis, [(i, size - 1 - i) for i in range(size)])


def moved(block, axis, pairs):
    return lax.ppermute(block, axis, pairs)


def pick(pair_low, pair_high, flag):
    return jnp.where(flag == 0, pair_low, pair_high)


def tie(*values):
    return lax.optimization_barrier(values)


def layout_marks(band, place):
    first, last = band == 0, band == lax.axis_size("tok") - 1
    turned = (first & (place == 0)) | (last & (place > 0))
    corner = first & (place == 2)
    edge = turned | jnp.where(first, place == 1, place == 0)
    start = 8 - 2 * band
    real = jnp.where(edge, WIN * EDGE, jnp.where(corner, EDGE * EDGE, 0))
    return (
        start, jnp.where(corner, 0, start), turned.astype(jnp.int32), real, first.astype(jnp.int32),
        band, lax.axis_index("yy"), lax.axis_index("core"),
    )


def whole_spec(shape):
    return pl.BlockSpec(shape, lambda *_: (0,) * len(shape))


def column_picks(ways, cols):
    out = np.zeros((ways, SLOT + EDGE, cols), np.float32)
    for s in range(ways):
        for j in range(SLOT):
            out[s, j, WIN * s + j] = 1.0
        for j in range(EDGE):
            out[s, SLOT + j, WIN * ways + j] = 1.0
    return out


def turn_picks():
    out = np.zeros((WIN * EDGE, EDGE * (SLOT + EDGE)), np.float32)
    for i in range(WIN):
        for j in range(EDGE):
            out[i * EDGE + j, j * (SLOT + EDGE) + i] = 1.0
    return out


def pack_kernel(picks, block, out):
    ways, full = out.shape[0], SLOT + EDGE
    for r in range(block.shape[1]):
        both = jnp.dot(picks[...], block[0, r], preferred_element_type=F32)
        for s in range(ways):
            out[s, 0, r] = both[s * full : (s + 1) * full].astype(BF)


def packed(block):
    count, rows, cols, width = block.shape
    ways = lax.axis_size("yy") * lax.axis_size("core")
    full = SLOT + EDGE
    picks = jnp.asarray(column_picks(ways, cols).reshape(ways * full, cols), BF)
    return pl.pallas_call(
        pack_kernel,
        grid=(count,),
        in_specs=[
            whole_spec(picks.shape),
            pl.BlockSpec((1, rows, cols, width), lambda n: (n, 0, 0, 0)),
        ],
        out_specs=pl.BlockSpec((ways, 1, rows, full, width), lambda n: (0, n, 0, 0, 0)),
        out_shape=jax.ShapeDtypeStruct((ways, count, rows, full, width), BF),
        cost_estimate=pl.CostEstimate(flops=0, bytes_accessed=0, transcendentals=0),
        name="pack",
    )(picks, block)


def window_kernel(at, got, ring, turn, out):
    count, rows = got.shape[1], got.shape[2]
    start_a, start_e, turned, first = at[0], at[1], at[2], at[4]
    for n in range(count):

        def row_of(row, cols):
            own = jnp.maximum(row - 8, 0)
            before = ring[n, jnp.minimum(row, 7), cols].astype(F32)
            return jnp.where(row < 8, before, got[own // rows, n, own % rows, cols].astype(F32))

        for i in range(WIN):
            full = row_of(start_a + i, slice(0, SLOT))
            out[n, i * SLOT : (i + 1) * SLOT] = full.astype(BF)
        edge = jnp.concatenate(
            [row_of(start_e + i, slice(SLOT, SLOT + EDGE)) for i in range(WIN)], axis=0
        )
        tail = jnp.concatenate(
            [
                jnp.where(first == 1, ring[n, k], got[2 + k // rows, n, k % rows]).astype(F32)
                for k in range(EDGE)
            ],
            axis=0,
        ).astype(BF)
        bottom = jnp.dot(turn[...], tail, preferred_element_type=F32)
        out[n, WIN * SLOT :] = jnp.where(turned == 1, bottom, edge).astype(BF)


def window_norm_kernel(at, got, ring, turn, gain, shift, out, low):
    window_kernel(at, got, ring, turn, out)
    for start, size in ((0, WIN * SLOT), (WIN * SLOT, WIN * EDGE)):
        unit, _ = norm_parts(out[0, start : start + size].astype(F32))
        row = lax.broadcasted_iota(jnp.int32, (size, 1), 0)
        real = (row & (SLOT - 1)) < WIN if start == 0 else row < at[3]
        low[start : start + size] = jnp.where(real, unit * gain[...] + shift[...], 0.0).astype(BF)


def ring_rows(got, step):
    bands = lax.axis_size("tok")
    send = jnp.moveaxis(got[2:], 1, 0)
    send = send.reshape(send.shape[0], 8, SLOT + EDGE, send.shape[-1])
    return moved(send, "tok", [(i, (i + step) % bands) for i in range(bands)])


def windowed(got, ring, marks, norm=None):
    count, width = got.shape[1], got.shape[-1]
    tokens = WIN * (SLOT + EDGE)
    specs = [
        whole_spec(got.shape),
        whole_spec(ring.shape),
        whole_spec((WIN * EDGE, EDGE * (SLOT + EDGE))),
    ]
    out_specs = [whole_spec((count, tokens, width))]
    out_shape = [jax.ShapeDtypeStruct((count, tokens, width), BF)]
    if norm is not None:
        specs += [whole_spec((width,))] * 2
        out_specs.append(whole_spec((tokens, width)))
        out_shape.append(jax.ShapeDtypeStruct((tokens, width), BF))
    return pl.pallas_call(
        window_kernel if norm is None else window_norm_kernel,
        grid_spec=pltpu.PrefetchScalarGridSpec(
            num_scalar_prefetch=1, grid=(1,), in_specs=specs, out_specs=out_specs
        ),
        out_shape=out_shape,
        cost_estimate=pl.CostEstimate(flops=0, bytes_accessed=0, transcendentals=0),
        name="window",
    )(marks, got, ring, jnp.asarray(turn_picks(), BF), *(norm or ()))


def unwindow(at, flats, turn, up, mid):
    start_a, start_e, turned, first = at[0], at[1], at[2], at[4]
    full = SLOT + EDGE
    for n, flat in enumerate(flats):
        bottom = lax.dot_general(
            turn[...],
            flat[WIN * SLOT :].astype(BF),
            (((0,), (0,)), ((), ())),
            preferred_element_type=F32,
        )
        for row in range(24):
            i = row - start_e
            held = (i >= 0) & (i < WIN) & (turned == 0)
            at_row = pl.multiple_of(WIN * SLOT + EDGE * jnp.clip(i, 0, WIN - 1), EDGE)
            right = jnp.where(held, flat[pl.ds(at_row, EDGE)], 0.0)
            i = row - start_a
            at_row = pl.multiple_of(SLOT * jnp.clip(i, 0, WIN - 1), SLOT)
            left = jnp.where((i >= 0) & (i < WIN), flat[pl.ds(at_row, SLOT)], 0.0)
            if row < 8 or row >= 16:
                base = row % 8 * full
                here = (turned == 1) & (first == (1 if row < 8 else 0))
                left = jnp.where(here, bottom[base : base + SLOT], left)
            both = jnp.concatenate([left, right], axis=0).astype(BF)
            if row < 8:
                up[n, row] = both
            else:
                mid[n, row - 8] = both


def unpack_kernel(picks, got, *outs):
    for n, out in enumerate(outs):
        for r in range(got.shape[2]):
            total = None
            for s in range(got.shape[0]):
                part = lax.dot_general(
                    picks[s], got[s, n, r], (((0,), (0,)), ((), ())), preferred_element_type=F32
                )
                total = part if total is None else total + part
            out[r] = total.astype(out.dtype)


def unpacked(got, cols, dtypes):
    ways, count, rows, full, width = got.shape
    picks = column_picks(ways, cols)
    picks[:, WIN:SLOT] = 0.0
    return pl.pallas_call(
        unpack_kernel,
        in_specs=[whole_spec(picks.shape), whole_spec(got.shape)],
        out_specs=[whole_spec((rows, cols, width))] * count,
        grid=(1,),
        out_shape=[jax.ShapeDtypeStruct((rows, cols, width), dtype) for dtype in dtypes],
        cost_estimate=pl.CostEstimate(flops=0, bytes_accessed=0, transcendentals=0),
        name="unpack",
    )(jnp.asarray(picks, BF), got)


def exchanged(send):
    return lax.all_to_all(send, SEQ, split_axis=0, concat_axis=0, tiled=True)


def sent_back(up):
    bands = lax.axis_size("tok")
    return moved(up, "tok", [((i + 1) % bands, i) for i in range(bands)])


def band_rows_of(mid, ring):
    own = mid + jnp.pad(ring, ((0, 0), (8, 0), (0, 0), (0, 0)))
    ways = lax.axis_size("yy") * lax.axis_size("core")
    own = own.reshape(own.shape[0], ways, 16 // ways, SLOT + EDGE, own.shape[-1])
    return jnp.swapaxes(own, 0, 1)


def two_images():
    return lax.axis_size("img") == 2


def quarter(shard):
    if not two_images():
        return shard
    rows = shard.shape[0] // 4
    at = lax.axis_index("yy") * 2 + lax.axis_index("core")
    return lax.dynamic_slice_in_dim(shard, at * rows, rows, 0)


def half_of(shard, chunks=1):
    if not two_images():
        return [shard]
    rows = shard.shape[0] // (2 * chunks)
    first = lax.axis_index("core") * rows * chunks
    return [lax.dynamic_slice_in_dim(shard, first + i * rows, rows, 0) for i in range(chunks)]


def over_images(block):
    if two_images():
        return swapped(block, "img")
    return lax.all_gather(block, "img", axis=0, tiled=True)


def half_over_cores(block):
    return (block, swapped(block, "core")) if two_images() else block


def assembled_halves(shard, *parts):
    if not two_images():
        return parts[0]
    core, image = lax.axis_index("core"), lax.axis_index("img")
    other = jnp.concatenate(
        [pick(here, there, core) for here, there in parts]
        + [pick(there, here, core) for here, there in parts],
        axis=0,
    )
    return jnp.concatenate([pick(shard, other, image), pick(other, shard, image)], axis=0)


def over_cores(block):
    return swapped(block, "core") if two_images() else block


def gather_over_rows(block):
    return swapped(block, "yy") if two_images() else block


def assembled(shard, first, second, first_across, second_across):
    if not two_images():
        return first
    core, high, image = (lax.axis_index(a) for a in ("core", "yy", "img"))
    rows = []
    for a, b, c, d in ((first, second, first_across, second_across), (second, first, second_across, first_across)):
        here, there = pick(a, b, high), pick(c, d, high)
        rows += [pick(here, there, core), pick(there, here, core)]
    other = jnp.concatenate(rows, axis=0)
    return jnp.concatenate([pick(shard, other, image), pick(other, shard, image)], axis=0)


def part_of(terms, dim, axis, other):
    index = lax.axis_index(axis)
    index = 1 - index if other else index
    return [lax.dynamic_index_in_dim(t, index, dim, keepdims=False) for t in terms]


def added(terms):
    total = terms[0].astype(F32)
    for t in terms[1:]:
        total = total + t.astype(F32)
    return total.astype(BF)


def to_send(terms, dim, axis):
    if lax.axis_size(axis) != 2:
        return jnp.moveaxis(added(terms), dim, 0)
    return added(part_of(terms, dim, axis, True))


def sent(block, axis):
    if lax.axis_size(axis) != 2:
        return lax.all_to_all(block, axis, split_axis=0, concat_axis=0, tiled=True)
    return swapped(block, axis)


def kept(terms, dim, axis, got):
    if lax.axis_size(axis) != 2:
        return [got[i] for i in range(got.shape[0])]
    return part_of(terms, dim, axis, False) + [got]


def split_grad(left, right):
    images, bands = lax.axis_size("img"), lax.axis_size("tok")
    core = lax.axis_index("core")
    rows, cols = left.shape[1], right.shape[1] // 2
    shape = (images, 2, bands, rows // images // 2 // bands, cols)

    def one(index):
        half = lax.dynamic_slice_in_dim(right, index * cols, cols, 1)
        return mm_tn(left, half).astype(BF).reshape(shape)

    return one(1 - core), one(core)


def crossed(block, distance):
    size = lax.axis_size("tok")
    return lax.ppermute(block, "tok", [(i, i ^ distance) for i in range(size)])


def by_bits(block):
    return block.reshape((2, 2) + block.shape[1:])


def bit_of(terms, dim, bit, other):
    index = (lax.axis_index("tok") >> bit) & 1
    index = 1 - index if other else index
    return [lax.dynamic_index_in_dim(t, index, dim, keepdims=False) for t in terms]


def low_send(terms):
    return added(bit_of(terms, 1, 0, True))


def high_send(terms):
    return added(bit_of(terms, 0, 1, True))


def after_low(terms, got):
    return bit_of(terms, 1, 0, False) + [got]


def after_high(terms, got):
    return added(bit_of(terms, 0, 1, False) + [got])


def final_kernel(splits, unit, at, near_own, near_other, far_own, far_other, *outs):
    band, core = at[5], at[7]

    def write(own, other):
        for t in range(own.shape[0]):
            to = ((t >> 1) | ((t & 1) << 1)) ^ band
            for (rows, first, blocks), out in zip(splits, outs):
                size = blocks * unit
                a = own[t, :, first * unit : first * unit + size].astype(F32)
                b = other[t, :, first * unit : first * unit + size].astype(F32)
                out[0, to, :, :size] = jnp.where(core == 0, a, b)
                out[0, to, :, size:] = jnp.where(core == 0, b, a)

    @pl.when(pl.program_id(0) == 0)
    def near():
        write(near_own, near_other)

    @pl.when(pl.program_id(0) == 1)
    def far():
        write(far_own, far_other)


def final(marks, own, other_core, beside, beside_other_core, splits):
    bands, rows, cols = own.shape
    unit = cols // sum(blocks for _, _, blocks in splits)
    outs = pl.pallas_call(
        functools.partial(final_kernel, splits, unit),
        grid_spec=pltpu.PrefetchScalarGridSpec(
            num_scalar_prefetch=1,
            grid=(2,),
            in_specs=[whole_spec(own.shape)] * 4,
            out_specs=[
                pl.BlockSpec((1, bands, n, 2 * blocks * unit), lambda y, at: (y ^ at[6], 0, 0, 0))
                for n, _, blocks in splits
            ],
        ),
        out_shape=[
            jax.ShapeDtypeStruct((2, bands, n, 2 * blocks * unit), F32) for n, _, blocks in splits
        ],
        cost_estimate=pl.CostEstimate(flops=0, bytes_accessed=0, transcendentals=0),
        name="final",
    )(marks, own, other_core, beside, beside_other_core)
    return [o.reshape(-1, o.shape[-1]) for o in outs]


def paired(value, axis):
    if axis == "img" and not two_images():
        return lax.psum(value, "img")
    across = crossed(value, axis) if isinstance(axis, int) else swapped(value, axis)
    return value + across


def small_pack_kernel(*refs):
    vectors, up_bias, tables, squares, out = refs[:8], refs[8], refs[9], refs[10], refs[11]
    width = out.shape[1]
    for i, vector in enumerate(vectors):
        out[i, :] = vector[...]
    row = len(vectors)
    for i in range(up_bias.shape[0] // width):
        out[row, :] = up_bias[i * width : (i + 1) * width]
        row += 1
    fit = width // LANES
    for m in range(2 * WIN - 1):
        at = (m % fit) * LANES
        out[row + m // fit, at : at + LANES] = tables[m, :]
    row += -(-(2 * WIN - 1) // fit)
    out[row : row + 1, :LANES] = jnp.broadcast_to(squares[...], (1, LANES))


def small_packed(vectors, up_bias, tables, squares):
    width = vectors[0].shape[0]
    rows = len(vectors) + up_bias.shape[0] // width - (-(2 * WIN - 1) // (width // LANES)) + 1
    args = (*vectors, up_bias, tables, squares)
    return pl.pallas_call(
        small_pack_kernel,
        grid=(1,),
        in_specs=[whole_spec(a.shape) for a in args],
        out_specs=whole_spec((rows, width)),
        out_shape=jax.ShapeDtypeStruct((rows, width), F32),
        cost_estimate=pl.CostEstimate(flops=0, bytes_accessed=0, transcendentals=0),
        name="small_pack",
    )(*args)


def small_unpack_kernel(packed, *outs):
    vectors, up_bias, rows_out, cols_out, squares = outs[:8], outs[8], outs[9], outs[10], outs[11]
    width = packed.shape[1]
    for i, vector in enumerate(vectors):
        vector[...] = packed[i, :]
    row = len(vectors)
    for i in range(up_bias.shape[0] // width):
        up_bias[i * width : (i + 1) * width] = packed[row, :]
        row += 1
    fit = width // LANES
    for m in range(2 * WIN - 1):
        at = (m % fit) * LANES
        both = packed[row + m // fit : row + m // fit + 1, at : at + LANES]
        rows_out[m : m + 1, :] = both[:, :HD]
        cols_out[m : m + 1, :] = pltpu.roll(both, HD, 1)[:, :HD]
    row += -(-(2 * WIN - 1) // fit)
    squares[...] = packed[row, :LANES]


def small_unpacked(packed, vectors, up_width):
    width = packed.shape[1]
    table = (2 * WIN - 1, HD)
    shapes = [(width,)] * vectors + [(up_width,), table, table, (LANES,)]
    return pl.pallas_call(
        small_unpack_kernel,
        grid=(1,),
        in_specs=[whole_spec(packed.shape)],
        out_specs=[whole_spec(shape) for shape in shapes],
        out_shape=[jax.ShapeDtypeStruct(shape, F32) for shape in shapes],
        cost_estimate=pl.CostEstimate(flops=0, bytes_accessed=0, transcendentals=0),
        name="small_unpack",
    )(packed)


def rolled(block, amount):
    return pltpu.roll(block, amount, 1, stride=1, stride_axis=0)


def rel_places():
    size = 2 * WIN - 1
    out = np.zeros((4, LANES, size), np.float32)
    for m in range(size):
        out[0, size - 1 - m, m] = 1.0
        out[1, 32 + size - 1 - m, m] = 1.0
        out[2, m, m] = 1.0
        out[3, 64 + m, m] = 1.0
    return out


def head_places():
    out = np.zeros((2, HD, LANES), np.float32)
    for c in range(HD):
        out[0, c, c] = 1.0
        out[1, c, HD + c] = 1.0
    return out


def build_rel(tables, places, heads, out):
    for half in (0, 1):
        total = None
        for table, place in zip(tables, places):
            high = table.astype(BF)
            value = (table - high.astype(F32)).astype(BF) if half else high
            part = jnp.dot(place, value, preferred_element_type=F32)
            total = part if total is None else total + part
        for head in (0, 1):
            lanes = jnp.dot(total.astype(BF), heads[head], preferred_element_type=F32)
            out[head, :, half * LANES : (half + 1) * LANES] = lanes.astype(BF)


def build_both(at, rows, cols, places, heads, rel_a, rel_b):
    @pl.when(pl.program_id(0) == 0)
    def build():
        turned = at[2] == 1
        build_rel((rows[...], cols[...]), places, heads, rel_a)
        first = jnp.where(turned, cols[...], rows[...])
        second = jnp.where(turned, rows[...], cols[...])
        build_rel((first, second), places, heads, rel_b)


def rel_terms(q, rel):
    return lax.dot_general(
        jnp.concatenate([q, q], axis=1), rel, (((1,), (1,)), ((), ())), preferred_element_type=F32
    )


def wide_queries(q, terms, group):
    m = q.shape[0]
    lane = lax.broadcasted_iota(jnp.int32, (group, LANES), 1)
    blocks = []
    for i in range(WIN):
        t = terms[i * group : (i + 1) * group]
        by_row = pltpu.roll(t, (LANES - (WIN - 1) + i) % LANES, 1)
        by_col = rolled(t, 19)
        blocks.append(jnp.where(lane < 64, by_row, by_col))
    both = jnp.concatenate(blocks, axis=0)
    high = both.astype(BF).astype(F32)
    low = pltpu.roll(both - high, 32, 1)
    lane = lax.broadcasted_iota(jnp.int32, (m, LANES), 1)
    mixed = jnp.where((lane & 63) < 32, high, low)
    mixed = jnp.where(lane == LANES - 1, 1.0, mixed)
    return jnp.concatenate([q * BF(HD**-0.5), mixed.astype(BF)], axis=1)


def full_keys(k, v, v_pad):
    n = k.shape[0]
    zeros = jnp.zeros((KEYS - n, LANES), BF)
    if v_pad is None:
        return jnp.concatenate([k, zeros], axis=0), jnp.concatenate([v, zeros], axis=0)
    fill = jnp.broadcast_to(v_pad, (KEYS - n, LANES)).astype(BF)
    return jnp.concatenate([k, zeros], axis=0), jnp.concatenate([v, fill], axis=0)


def only(block, head):
    lane = lax.broadcasted_iota(jnp.int32, block.shape, 1)
    return jnp.where((lane < HD) == (head == 0), block, jnp.zeros_like(block))


def scored(wide, keys, hot, head):
    return lax.dot_general(
        wide,
        jnp.concatenate([only(keys, head), hot], axis=1),
        (((1,), (1,)), ((), ())),
        preferred_element_type=F32,
    )


def softmax_low(scores):
    e = jnp.exp(scores - jnp.max(scores, axis=1, keepdims=True))
    return (e * (1.0 / jnp.sum(e, axis=1, keepdims=True))).astype(BF)


def attend_kernel(
    at, q, k, v, v_pad, rows, cols, places, heads, hot_a, hot_b, out, probs_a, probs_b, rel_a, rel_b
):
    build_both(at, rows, cols, (places[0], places[1]), heads, rel_a, rel_b)
    n = WIN * SLOT
    pad = v_pad[...].astype(BF)
    slots = (
        (slice(0, n), None, rel_a, hot_a, SLOT, probs_a),
        (slice(n, n + WIN * EDGE), pad, rel_b, hot_b, EDGE, probs_b),
    )
    both = [(s, h) for s in (0, 1) for h in (0, 1)]
    queries = [q[slot[0]] for slot in slots]
    terms = [
        rel_terms(queries[i], slots[i][2][...].reshape(2 * LANES, 2 * LANES)) for i in (0, 1)
    ]
    filled = [full_keys(k[slot[0]], v[slot[0]], slot[1]) for slot in slots]
    wide = [
        wide_queries(queries[i], terms[i][:, h * LANES : (h + 1) * LANES], slots[i][4])
        for i, h in both
    ]
    scores = [scored(w, filled[i][0], slots[i][3][...], h) for w, (i, h) in zip(wide, both)]
    probs = [softmax_low(x) for x in scores]
    for p, (i, h) in zip(probs, both):
        slots[i][5][h] = p
    parts = [
        jnp.dot(p, only(filled[i][1], h), preferred_element_type=F32)
        for p, (i, h) in zip(probs, both)
    ]
    for i in (0, 1):
        out[slots[i][0]] = (parts[2 * i] + parts[2 * i + 1]).astype(BF)


def back_terms(both, group):
    lane = lax.broadcasted_iota(jnp.int32, (group, LANES), 1)
    blocks = []
    for i in range(WIN):
        t = both[i * group : (i + 1) * group, LANES:]
        by_row = jnp.where(lane < WIN, t, 0.0)
        by_row = pltpu.roll(by_row, i, 1) if i else by_row
        by_col = rolled(jnp.where((lane >= 64) & (lane < 64 + WIN), t, 0.0), 0)
        blocks.append(by_row + by_col)
    terms = jnp.concatenate(blocks, axis=0)
    high = terms.astype(BF)
    return jnp.concatenate([high, (terms - high.astype(F32)).astype(BF)], axis=1)


def over_rows(left, right):
    return lax.dot_general(left, right, (((0,), (0,)), ((), ())), preferred_element_type=F32)


def attend_back_kernel(
    at, q, k, v, v_pad, rows, cols, places, heads, hot_a, hot_b, grad, probs_a, probs_b,
    dqkv, pad_sum, rel_grad, rel_a, rel_b, acc_a, acc_b,
):
    step = pl.program_id(0)
    steps = dqkv.shape[1] // (3 * LANES)
    build_both(at, rows, cols, (places[2], places[3]), heads, rel_a, rel_b)

    @pl.when(step == 0)
    def clear():
        acc_a[...] = jnp.zeros_like(acc_a)
        acc_b[...] = jnp.zeros_like(acc_b)

    n = WIN * SLOT
    scale = HD**-0.5
    pad = v_pad[...].astype(BF)
    slots = (
        (slice(0, n), None, rel_a, hot_a, SLOT, probs_a, acc_a),
        (slice(n, n + WIN * EDGE), pad, rel_b, hot_b, EDGE, probs_b, acc_b),
    )
    both = [(s, h) for s in (0, 1) for h in (0, 1)]
    queries = [q[slot[0]] for slot in slots]
    grads = [grad[slot[0]] for slot in slots]
    filled = [full_keys(k[slot[0]], v[slot[0]], slot[1]) for slot in slots]
    probs_grad = [
        lax.dot_general(
            grads[i], only(filled[i][1], h), (((1,), (1,)), ((), ())), preferred_element_type=F32
        )
        for i, h in both
    ]
    dvs = [over_rows(slots[i][5][h], grads[i]) for i, h in both]
    scores_grad = []
    for dp, (i, h) in zip(probs_grad, both):
        wide = slots[i][5][h].astype(F32)
        inner = jnp.sum(wide * dp, axis=1, keepdims=True)
        scores_grad.append((wide * (dp - inner)).astype(BF))
    sums = [
        jnp.dot(
            ds,
            jnp.concatenate([only(filled[i][0], h), slots[i][3][...]], axis=1),
            preferred_element_type=F32,
        )
        for ds, (i, h) in zip(scores_grad, both)
    ]
    dks = [over_rows(ds, queries[i]) * scale for ds, (i, h) in zip(scores_grad, both)]
    split = [back_terms(x, slots[i][4]) for x, (i, h) in zip(sums, both)]
    parts = []
    for x, t, (i, h) in zip(sums, split, both):
        rel = slots[i][2][h]
        part = x[:, :LANES] * scale + jnp.dot(
            t,
            jnp.concatenate([rel[:, :LANES], rel[:, :LANES]], axis=0),
            preferred_element_type=F32,
        )
        parts.append(part + jnp.dot(t[:, :LANES], rel[:, LANES:], preferred_element_type=F32))
    for t, (i, h) in zip(split, both):
        slots[i][6][h] += over_rows(t, queries[i])
    lane = lax.broadcasted_iota(jnp.int32, (KEYS, LANES), 1)
    for i in (0, 1):
        here, size = slots[i][0], queries[i].shape[0]
        dk = jnp.where(lane < HD, dks[2 * i], dks[2 * i + 1]).astype(BF)
        dv = jnp.where(lane < HD, dvs[2 * i], dvs[2 * i + 1]).astype(BF)
        found = ((parts[2 * i] + parts[2 * i + 1]).astype(BF), dk[:size], dv[:size])
        for j, value in enumerate(found):
            to = pl.ds(pl.multiple_of((j * steps + step) * LANES, LANES), LANES)
            dqkv[here, to] = value
    pad_sum[...] = jnp.sum(dv[WIN * EDGE :].astype(F32), axis=0, keepdims=True)

    @pl.when(step == steps - 1)
    def tables():
        def table(acc):
            even = acc[0, :LANES] + acc[0, LANES:]
            odd = acc[1, :LANES] + acc[1, LANES:]
            return even + pltpu.roll(odd, HD, 1)

        a, b = table(acc_a), table(acc_b)
        turned = at[2] == 1
        low, high = slice(0, 32), slice(64, 96)
        rows_grad = a[low] + jnp.where(turned, b[high], b[low])
        cols_grad = a[high] + jnp.where(turned, b[low], b[high])
        lane = lax.broadcasted_iota(jnp.int32, (32, LANES), 1)
        rel_grad[...] = jnp.where(lane < HD, rows_grad, pltpu.roll(cols_grad, HD, 1))


def hot_tables():
    def table(place):
        out = np.zeros((2, KEYS, LANES), np.float32)
        for key in range(KEYS):
            at = place(key)
            if at is None:
                out[0, key, LANES - 1] = -1e30
            else:
                for base, index in ((0, at[0]), (32, at[0]), (64, at[1]), (96, at[1])):
                    out[0, key, base + index] = 1.0
                out[1, key, WIN - 1 - at[0]] = 1.0
                out[1, key, 64 + WIN - 1 - at[1]] = 1.0
        return out

    def whole(key):
        i, j = divmod(key, SLOT)
        return (i, j) if i < WIN and j < WIN else None

    def partial(key):
        if key < WIN * EDGE:
            return divmod(key, EDGE)
        i, j = divmod(key - WIN * EDGE, EDGE)
        return (i, EDGE + j) if i < WIN and EDGE + j < WIN else None

    return table(whole), table(partial)


def attention(qkv, v_pad, rel_rows, rel_cols, marks):
    tokens_a, tokens_b = WIN * SLOT, WIN * EDGE
    tokens, width = qkv.shape[0], qkv.shape[1] // 3
    pairs = width // LANES
    table = (2 * WIN - 1, HD)
    hots = [jnp.asarray(t, BF) for t in hot_tables()]
    places, heads = jnp.asarray(rel_places(), BF), jnp.asarray(head_places(), BF)

    def cols(n, base):
        return pl.BlockSpec((n, LANES), lambda p, at: (0, base * pairs + p))

    specs = [cols(tokens, i) for i in range(3)] + [
        pl.BlockSpec((LANES,), lambda p, at: (p,)),
        whole_spec(table),
        whole_spec(table),
        whole_spec(places.shape),
        whole_spec(heads.shape),
        whole_spec((KEYS, LANES)),
        whole_spec((KEYS, LANES)),
    ]
    probs_specs = [
        pl.BlockSpec((2, tokens_a, KEYS), lambda p, at: (p, 0, 0)),
        pl.BlockSpec((2, tokens_b, KEYS), lambda p, at: (p, 0, 0)),
    ]
    rel_scratch = [pltpu.VMEM((2, LANES, 2 * LANES), BF)] * 2
    shared = (marks, qkv, qkv, qkv, v_pad, rel_rows, rel_cols, places, heads)
    out, probs_a, probs_b = pl.pallas_call(
        attend_kernel,
        grid_spec=pltpu.PrefetchScalarGridSpec(
            num_scalar_prefetch=1,
            grid=(pairs,),
            in_specs=specs,
            out_specs=[cols(tokens, 0)] + probs_specs,
            scratch_shapes=rel_scratch,
        ),
        out_shape=[
            jax.ShapeDtypeStruct((tokens, width), BF),
            jax.ShapeDtypeStruct((2 * pairs, tokens_a, KEYS), BF),
            jax.ShapeDtypeStruct((2 * pairs, tokens_b, KEYS), BF),
        ],
        cost_estimate=pl.CostEstimate(flops=0, bytes_accessed=0, transcendentals=0),
        name="attend",
    )(*shared, hots[0][0], hots[1][0])

    def back(grad):
        return pl.pallas_call(
            attend_back_kernel,
            grid_spec=pltpu.PrefetchScalarGridSpec(
                num_scalar_prefetch=1,
                grid=(pairs,),
                in_specs=specs + [cols(tokens, 0)] + probs_specs,
                out_specs=[
                    whole_spec((tokens, 3 * width)),
                    cols(1, 0),
                    whole_spec((32, LANES)),
                ],
                scratch_shapes=rel_scratch + [pltpu.VMEM((2, 2 * LANES, LANES), F32)] * 2,
            ),
            out_shape=[
                jax.ShapeDtypeStruct((tokens, 3 * width), BF),
                jax.ShapeDtypeStruct((1, width), F32),
                jax.ShapeDtypeStruct((32, LANES), F32),
            ],
            cost_estimate=pl.CostEstimate(flops=0, bytes_accessed=0, transcendentals=0),
            name="attend_back",
        )(*shared, hots[0][1], hots[1][1], grad, probs_a, probs_b)

    return out, back


def norm_parts(values):
    centre = jnp.mean(values, axis=-1, keepdims=True)
    centred = values - centre
    spread = jnp.mean(centred * centred, axis=-1, keepdims=True)
    scale = lax.rsqrt(spread + EPS)
    return centred * scale, scale


def norm_back(grad, unit, scale, gain):
    g = grad * gain
    mean = jnp.mean(g, axis=-1, keepdims=True)
    along = jnp.mean(g * unit, axis=-1, keepdims=True)
    return scale * (g - mean - unit * along)


def mlp_back_kernel(
    pre, up, resid, result_grad, gain, proj, resid_grad, proj_in, attended_grad, gain_grad, shift_grad,
    proj_bias_grad, up_bias_grad, total,
):
    step = pl.program_id(0)
    part = mm_nt(pre[...], up[...])
    up_bias_grad[...] = jnp.sum(pre[...].astype(F32), axis=0)

    @pl.when(step == 0)
    def first():
        total[...] = part

    @pl.when(step > 0)
    def more():
        total[...] += part

    @pl.when(step == pl.num_programs(0) - 1)
    def last():
        grad = total[...]
        unit, scale = norm_parts(resid[...])
        gain_grad[...] = jnp.sum(grad * unit, axis=0)
        shift_grad[...] = jnp.sum(grad, axis=0)
        found = result_grad[...] + norm_back(grad, unit, scale, gain[...])
        resid_grad[...] = found
        low = found.astype(BF)
        proj_in[...] = low
        proj_bias_grad[...] = jnp.sum(low.astype(F32), axis=0)
        attended_grad[...] = mm_nt(low, proj[...]).astype(BF)


def mlp_back(pre_grad, up_full, resid, result_grad, gain, proj_full):
    tokens, hidden = pre_grad.shape
    width = resid.shape[1]
    size = 1024
    steps = hidden // size
    flat = jax.ShapeDtypeStruct((width,), F32)
    return pl.pallas_call(
        mlp_back_kernel,
        grid=(steps,),
        in_specs=[
            pl.BlockSpec((tokens, size), lambda k: (0, k)),
            pl.BlockSpec((width, size), lambda k: (0, k)),
            whole_spec(resid.shape),
            whole_spec(resid.shape),
            whole_spec((width,)),
            whole_spec(proj_full.shape),
        ],
        out_specs=[whole_spec(resid.shape)] * 3
        + [whole_spec((width,))] * 3
        + [pl.BlockSpec((size,), lambda k: (k,))],
        out_shape=[
            jax.ShapeDtypeStruct(resid.shape, F32),
            jax.ShapeDtypeStruct(resid.shape, BF),
            jax.ShapeDtypeStruct(resid.shape, BF),
            flat,
            flat,
            flat,
            jax.ShapeDtypeStruct((hidden,), F32),
        ],
        scratch_shapes=[pltpu.VMEM(resid.shape, F32)],
        cost_estimate=pl.CostEstimate(flops=0, bytes_accessed=0, transcendentals=0),
        name="mlp_back",
    )(pre_grad, up_full, resid, result_grad, gain, proj_full)


def input_back_kernel(
    at, dqkv, weight, low, resid_grad, gain, pad_sum, turn, up, mid, gain_grad, shift_grad,
    query_sum, value_sum, total,
):
    step = pl.program_id(0)
    part = mm_nt(dqkv[...], weight[...])
    sums = jnp.sum(dqkv[...].astype(F32), axis=0)

    @pl.when(step == 0)
    def first():
        total[...] = part
        query_sum[...] = sums

    @pl.when(step > 0)
    def more():
        total[...] += part

    @pl.when(step == pl.num_programs(0) - 1)
    def last():
        value_sum[...] = sums + pad_sum[0]
        row = lax.broadcasted_iota(jnp.int32, (total.shape[0], 1), 0)
        full = WIN * SLOT
        limit = jnp.where(row < full, row - (row & (SLOT - 1)) + WIN, full + at[3])
        real = row < limit
        grad = jnp.where(real, total[...], 0.0)
        unit, scale = norm_parts(low[...].astype(F32))
        gain_grad[...] = jnp.sum(grad * unit, axis=0)
        shift_grad[...] = jnp.sum(grad, axis=0)
        total[...] = resid_grad[...] + norm_back(grad, unit, scale, gain[...])
        unwindow(at, (total,), turn, up, mid)


def input_back(marks, dqkv, qkv_full, low, resid_grad, gain, pad_sum):
    tokens, width = low.shape
    full = SLOT + EDGE
    flat = jax.ShapeDtypeStruct((width,), F32)
    shapes = [(1, 8, full, width), (1, 16, full, width)]
    return pl.pallas_call(
        input_back_kernel,
        grid_spec=pltpu.PrefetchScalarGridSpec(
            num_scalar_prefetch=1,
            grid=(3,),
            in_specs=[
                pl.BlockSpec((tokens, width), lambda k, at: (0, k)),
                pl.BlockSpec((width, width), lambda k, at: (0, k)),
                whole_spec(low.shape),
                whole_spec(low.shape),
                whole_spec((width,)),
                whole_spec((1, width)),
                whole_spec((WIN * EDGE, EDGE * full)),
            ],
            out_specs=[whole_spec(shape) for shape in shapes] + [whole_spec((width,))] * 4,
            scratch_shapes=[pltpu.VMEM(low.shape, F32)],
        ),
        out_shape=[jax.ShapeDtypeStruct(shape, BF) for shape in shapes] + [flat] * 4,
        cost_estimate=pl.CostEstimate(flops=0, bytes_accessed=0, transcendentals=0),
        name="input_back",
    )(marks, dqkv, qkv_full, low, resid_grad, gain, pad_sum, jnp.asarray(turn_picks(), BF))


def result_rows_kernel(at, result, turn, up, mid, block):
    row = lax.broadcasted_iota(jnp.int32, (result.shape[0], 1), 0)
    full = WIN * SLOT
    limit = jnp.where(row < full, row - (row & (SLOT - 1)) + WIN, full + at[3])
    block[...] = jnp.where(row < limit, result[...], 0.0)
    unwindow(at, (block,), turn, up, mid)


def result_rows(marks, result):
    width, full = result.shape[1], SLOT + EDGE
    shapes = [(1, 8, full, width), (1, 16, full, width)]
    return pl.pallas_call(
        result_rows_kernel,
        grid_spec=pltpu.PrefetchScalarGridSpec(
            num_scalar_prefetch=1,
            grid=(1,),
            in_specs=[whole_spec(result.shape), whole_spec((WIN * EDGE, EDGE * full))],
            out_specs=[whole_spec(shape) for shape in shapes],
            scratch_shapes=[pltpu.VMEM(result.shape, F32)],
        ),
        out_shape=[jax.ShapeDtypeStruct(shape, BF) for shape in shapes],
        cost_estimate=pl.CostEstimate(flops=0, bytes_accessed=0, transcendentals=0),
        name="result_rows",
    )(marks, result, jnp.asarray(turn_picks(), BF))


def mm(a, b):
    return jnp.dot(a, b, preferred_element_type=F32)


def mm_nt(a, b):
    return lax.dot_general(a, b, (((1,), (1,)), ((), ())), preferred_element_type=F32)


def mm_tn(a, b):
    return lax.dot_general(a, b, (((0,), (0,)), ((), ())), preferred_element_type=F32)


def local(
    images, teacher, valid_mask, out_grad, attn_gain, attn_shift, qkv_weight, query_bias,
    value_bias, rel_rows, rel_cols, proj_weight, proj_bias, mlp_gain, mlp_shift, up_weight,
    up_bias, down_weight, down_bias,
):
    band = lax.axis_index("tok")
    bands = lax.axis_size("tok")
    place = lax.axis_index("yy") * lax.axis_size("core") + lax.axis_index("core")
    width = images.shape[-1]
    image_rows = images.shape[1] * bands * lax.axis_size("yy") * lax.axis_size("core")
    tokens_all = images.shape[0] * lax.axis_size("img") * image_rows * images.shape[2]

    marks = layout_marks(band, place)
    real_edge = marks[3]
    marks = jnp.stack(marks).astype(jnp.int32)
    x_got = exchanged(packed(images))
    qkv_1 = over_images(quarter(qkv_weight))
    proj_1 = [over_images(c) for c in half_of(proj_weight)]
    up_1 = [over_images(c) for c in half_of(up_weight)]
    down_1 = [over_images(c) for c in half_of(down_weight, 2)]
    count = jnp.broadcast_to(jnp.sum(valid_mask.astype(F32)), (8, LANES))
    count = paired(count, "img")
    x_got, qkv_1, marks, count = tie(x_got, qkv_1, marks, count)
    qkv_2 = gather_over_rows(qkv_1)
    x_ring = ring_rows(x_got, 1)
    qkv_3 = over_cores(qkv_1)
    count = paired(count, "core")
    marked = jnp.where(valid_mask[..., None] > 0, teacher, jnp.full_like(teacher, FAR))
    late_pack = packed(tie(jnp.concatenate([marked, out_grad], axis=0), qkv_1)[0])
    x_ring, x_got, late_pack, count = tie(x_ring, x_got, late_pack, count)
    x_low, tokens_low = windowed(x_got, x_ring, marks, (attn_gain, attn_shift))
    x_low = x_low[0]
    count = paired(count, "yy")
    qkv_2, x_low, tokens_low, qkv_3 = tie(qkv_2, x_low, tokens_low, qkv_3)
    qkv_4 = over_cores(qkv_2)
    late_got = exchanged(tie(late_pack, x_low)[0])
    qkv_4, proj_1[0], count, up_1[0] = tie(qkv_4, proj_1[0], count, up_1[0])
    up_2 = [half_over_cores(up_1[0])]
    proj_2 = half_over_cores(proj_1[0])
    count = paired(count, 1)

    row_a = lax.broadcasted_iota(jnp.int32, (WIN * SLOT, 1), 0)
    row_b = lax.broadcasted_iota(jnp.int32, (WIN * EDGE, 1), 0)
    real = jnp.concatenate(
        [(row_a & (SLOT - 1)) < WIN, row_b < real_edge], axis=0
    )
    inputs = x_low.astype(F32)
    qkv_bias = jnp.concatenate([query_bias, jnp.zeros_like(query_bias), value_bias])
    qkv_full = assembled(qkv_weight, qkv_1, qkv_2, qkv_3, qkv_4)
    qkv = (mm(tokens_low, qkv_full) + qkv_bias).astype(BF)
    proj_full = assembled_halves(proj_weight, proj_2)
    up_full = assembled_halves(up_weight, *up_2)
    qkv, late_got, proj_full, count, up_full, down_1[0] = tie(
        qkv, late_got, proj_full, count, up_full, down_1[0]
    )
    late_ring = ring_rows(late_got, 1)
    count = paired(count, 2)
    attended, attention_back = attention(qkv, value_bias, rel_rows, rel_cols, marks)
    down_2 = [half_over_cores(down_1[0])]
    attended, count, late_ring, down_1, down_2 = tie(attended, count, late_ring, down_1, down_2)
    resid = inputs + mm(attended, proj_full) + proj_bias
    unit2, scale2 = norm_parts(resid)
    normed2 = (unit2 * mlp_gain + mlp_shift).astype(BF)
    down_2 = down_2 + [half_over_cores(c) for c in down_1[1:]]
    hidden_pre = mm(normed2, up_full) + up_bias
    cdf = 0.5 * (1.0 + lax.erf(hidden_pre * (0.5**0.5)))
    hidden = (hidden_pre * cdf).astype(BF)
    slope = cdf + hidden_pre * jnp.exp(-0.5 * hidden_pre * hidden_pre) * ((2 * np.pi) ** -0.5)
    hidden, slope, down_2 = tie(hidden, slope, down_2)
    count_total = count[0, 0]
    (late,) = windowed(late_got, late_ring, marks)
    late, down_2 = tie(late, down_2)
    down_full = assembled_halves(down_weight, *down_2)
    result = resid + mm(hidden, down_full) + down_bias

    teach = late[0].astype(F32)
    valid = (real & (teach[:, :1] < 0.5 * FAR)).astype(F32)
    differ = valid * (result - teach)
    squares = jnp.sum(differ * differ)
    grads = jnp.where(real, late[1], jnp.zeros_like(late[1])).astype(F32)
    result_grad = grads + differ * (tokens_all / (4.0 * count_total))
    down_in = result_grad.astype(BF)

    d_send, d_keep = split_grad(hidden, down_in)
    d_send, down_in = tie(d_send, down_in)
    d_got = sent(d_send, "core")
    pre_grad = (slope * mm_nt(down_in, down_full)).astype(BF)
    d_got, d_keep, pre_grad = tie(d_got, d_keep, pre_grad)
    d_terms = [d_keep, d_got]
    d_out, pre_grad = tie(to_send(d_terms, 0, "img"), pre_grad)
    d_got = sent(d_out, "img")
    u_send, u_keep = split_grad(normed2, pre_grad)
    u_send, pre_grad = tie(u_send, pre_grad)
    u_got = sent(u_send, "core")
    u_got, u_keep, pre_grad = tie(u_got, u_keep, pre_grad)
    u_terms = [u_keep, u_got]
    u_out, pre_grad = tie(to_send(u_terms, 1, "yy"), pre_grad)
    u_got = sent(u_out, "yy")
    (
        resid_grad, proj_in, attended_grad, mlp_gain_grad, mlp_shift_grad, proj_bias_grad, up_bias_grad
    ) = mlp_back(pre_grad, up_full, resid, result_grad, mlp_gain, proj_full)
    p_send, p_keep = split_grad(attended, proj_in)
    p_send, proj_in = tie(p_send, proj_in)
    p_got = sent(p_send, "core")
    attended_grad, p_got, p_keep = tie(attended_grad, p_got, p_keep)
    p_terms = [p_keep, p_got]
    p_out, attended_grad = tie(to_send(p_terms, 0, "img"), attended_grad)
    p_got = sent(p_out, "img")

    dqkv, pad_sum, rel_grad = attention_back(attended_grad)
    dqkv, pad_sum, d_got, u_got = tie(dqkv, pad_sum, d_got, u_got)
    d_terms = kept(d_terms, 0, "img", d_got)
    u_terms = kept(u_terms, 1, "yy", u_got)
    d_out, u_out, dqkv = tie(to_send(d_terms, 0, "yy"), to_send(u_terms, 0, "img"), dqkv)
    d_got = sent(d_out, "yy")
    u_got = sent(u_out, "img")
    q_send, q_keep = split_grad(tokens_low, dqkv)
    q_send, dqkv = tie(q_send, dqkv)
    q_got = sent(q_send, "core")
    block_up, block_mid = result_rows(marks, tie(result, q_send)[0])
    block_ring = sent_back(block_up)
    q_got, q_keep, dqkv, p_got, block_mid = tie(q_got, q_keep, dqkv, p_got, block_mid)
    p_terms = kept(p_terms, 0, "img", p_got)
    half = bands // 2
    qa_terms = [q_keep[:, :, :half], q_got[:, :, :half]]
    qb_terms = [q_keep[:, :, half:], q_got[:, :, half:]]
    qa_out, qb_out, p_out = tie(
        to_send(qa_terms, 0, "img"), to_send(qb_terms, 1, "yy"), to_send(p_terms, 0, "yy")
    )
    p_got = sent(p_out, "yy")
    qa_got = sent(qa_out, "img")
    qb_got = sent(qb_out, "yy")
    d_got, qa_out = tie(d_got, qa_out)
    d_terms = [by_bits(added(kept(d_terms, 0, "yy", d_got)))]
    d_out, u_got, p_got = tie(low_send(d_terms), u_got, p_got)
    d_got = crossed(d_out, 1)
    u_sum = added(kept(u_terms, 0, "img", u_got))
    p_sum = added(kept(p_terms, 0, "yy", p_got))
    part, cols = p_sum.shape[1], p_sum.shape[2]
    blocks = u_sum.shape[-1] // cols
    u_terms = [by_bits(jnp.concatenate([u_sum, p_sum], axis=-1))]
    qkv_parts = tie(qkv_1, qkv_2, qkv_3, qkv_4, d_out)[:4]
    qkv_back = assembled(qkv_weight, *qkv_parts)
    u_out, qa_got, qb_got, block_ring, qkv_back = tie(
        low_send(u_terms), qa_got, qb_got, block_ring, qkv_back
    )
    u_got = crossed(u_out, 1)
    qa_terms = kept(qa_terms, 0, "img", qa_got)
    qb_terms = kept(qb_terms, 1, "yy", qb_got)
    qa_out, qb_out, dqkv, d_got = tie(
        to_send(qa_terms, 0, "yy"), to_send(qb_terms, 0, "img"), dqkv, d_got
    )
    qa_got = sent(qa_out, "yy")
    qb_got = sent(qb_out, "img")
    d_terms = after_low(d_terms, d_got)
    d_out, dqkv = tie(high_send(d_terms), dqkv)
    d_got = crossed(d_out, 2)
    down_bias_grad = jnp.sum(down_in.astype(F32), axis=0)
    *backs, attn_gain_grad, attn_shift_grad, query_bias_grad, value_bias_grad = input_back(
        marks, dqkv, qkv_back, x_low, resid_grad, attn_gain, pad_sum
    )
    small = small_packed(
        (
            attn_gain_grad, attn_shift_grad, query_bias_grad, value_bias_grad, proj_bias_grad,
            mlp_gain_grad, mlp_shift_grad, down_bias_grad,
        ),
        up_bias_grad,
        rel_grad,
        squares.reshape(1, 1),
    )
    small = paired(small, "core")
    backs, d_got, qa_got, qb_got, u_got = tie(backs, d_got, qa_got, qb_got, u_got)
    d_sum = after_high(d_terms, d_got)
    d_got = crossed(d_sum, 2)
    u_terms = after_low(u_terms, u_got)
    u_out, d_sum, small = tie(high_send(u_terms), d_sum, small)
    q_whole = [
        by_bits(
            jnp.concatenate(
                [added(kept(qa_terms, 0, "yy", qa_got)), added(kept(qb_terms, 0, "img", qb_got))],
                axis=0,
            )
        )
    ]
    q_out, u_out = tie(low_send(q_whole), u_out)
    small = paired(small, "img")
    d_got, q_out, u_out, small = tie(d_got, q_out, u_out, small)
    u_got = crossed(u_out, 2)
    q_got = crossed(q_out, 1)
    back_ring = sent_back(tie(backs[0], u_out)[0])
    small = paired(small, "yy")
    d_pair = jnp.stack([d_sum, d_got])
    d_got = crossed(d_pair, 1)
    u_got, d_pair, back_ring, small = tie(u_got, d_pair, back_ring, small)
    small = paired(small, 1)
    u_sum = after_high(u_terms, u_got)
    u_got = crossed(u_sum, 2)
    own_rows = band_rows_of(
        jnp.concatenate([block_mid, backs[1]]), jnp.concatenate([block_ring, back_ring])
    )
    q_got, u_sum, own_rows = tie(q_got, u_sum, own_rows)
    back_got = exchanged(own_rows)
    q_terms = after_low(q_whole, q_got)
    q_out, d_got, u_got, small = tie(high_send(q_terms), d_got, u_got, small)
    q_got = crossed(q_out, 2)
    small = paired(small, 2)
    d_own = jnp.concatenate([d_pair, d_got], axis=0)
    d_beside, d_other = swapped(d_own, "yy"), swapped(d_own, "core")
    u_pair = jnp.stack([u_sum, u_got])
    u_got = crossed(u_pair, 1)
    block_out, images_grad = unpacked(tie(back_got, u_pair)[0], images.shape[2], (BF, F32))
    q_got, u_pair, d_other, block_out, small = tie(q_got, u_pair, d_other, block_out, small)
    q_sum = after_high(q_terms, q_got)
    q_got = crossed(q_sum, 2)
    d_beside, u_got, q_sum = tie(d_beside, u_got, q_sum)
    d_last = swapped(d_beside, "core")
    u_own = jnp.concatenate([u_pair, u_got], axis=0)
    u_beside, u_other = swapped(u_own, "yy"), swapped(u_own, "core")
    q_got, u_own = tie(q_got, u_own)
    q_pair = jnp.stack([q_sum, q_got])
    q_got = crossed(q_pair, 1)
    q_pair, d_last = tie(q_pair, d_last)
    (down_grad,) = final(marks, d_own, d_other, d_beside, d_last, ((d_own.shape[1], 0, 1),))
    q_got, down_grad, u_other, small = tie(q_got, down_grad, u_other, small)
    q_own = jnp.concatenate([q_pair, q_got], axis=0)
    q_beside, q_other = swapped(q_own, "yy"), swapped(q_own, "core")
    u_beside, q_own = tie(u_beside, q_own)
    u_last = swapped(u_beside, "core")
    *sums, squares = small_unpacked(small, 8, up_bias.shape[0])
    u_last, squares = tie(u_last, squares)
    up_grad, proj_grad = final(
        marks, u_own, u_other, u_beside, u_last, ((part, 0, blocks), (part, blocks, 1))
    )
    q_beside, up_grad = tie(q_beside, up_grad)
    q_last = swapped(q_beside, "core")
    (qkv_grad,) = final(marks, q_own, q_other, q_beside, q_last, ((q_own.shape[1], 0, 1),))
    distill_loss = squares[0] / (count_total * width)
    return (
        block_out[None], distill_loss, images_grad[None], sums[0], sums[1], qkv_grad, sums[2], sums[3],
        sums[9], sums[10], proj_grad, sums[4], sums[5], sums[6], up_grad, sums[8], down_grad, sums[7],
    )


def solution(mesh):
    shape = dict(mesh.shape)
    fine = Mesh(
        mesh.devices.reshape(shape["img"], shape["tok"], shape["seq"] // 2, 2), EVERY
    )
    tokens = P("img", ("tok",) + SEQ, None, None)
    mask = P("img", ("tok",) + SEQ, None)
    split, whole = P("img", None), P()
    return jax.shard_map(
        local,
        mesh=fine,
        in_specs=(
            tokens, tokens, mask, tokens, whole, whole, split, whole, whole, whole, whole, split,
            whole, whole, whole, split, whole, split, whole,
        ),
        out_specs=(
            tokens, whole, tokens, whole, whole, split, whole, whole, whole, whole, split, whole,
            whole, whole, split, whole, split, whole,
        ),
        check_vma=False,
    )
```
